32 devices in a mesh: dp: 4 (over z), ctx: 4 (over y, x), tp: 2 (over core).
Axes of the slice: x: 2, y: 2, z: 4, core: 2. Of those that a mesh axis runs over, the one named last changes fastest.
Arguments:
- tokens: bfloat16 [8, 2048, 2048], P('dp', 'ctx'), may hold values from -6 to 6
- cotangent: bfloat16 [8, 2048, 2048], P('dp', 'ctx'), may hold values from -6 to 6
- attention_gain: bfloat16 [2048], P(('dp', 'ctx')), may hold values from 0.5 to 1.5
- attention_bias: bfloat16 [2048], P(('dp', 'ctx')), may hold values from -3 to 3
- feedforward_gain: bfloat16 [2048], P(('dp', 'ctx')), may hold values from 0.5 to 1.5
- feedforward_bias: bfloat16 [2048], P(('dp', 'ctx')), may hold values from -3 to 3
- query_weight: bfloat16 [2048, 2048], P(('dp', 'ctx'), 'tp'), may hold values from -0.1875 to 0.1875
- query_bias: bfloat16 [2048], P('tp'), may hold values from -3 to 3
- key_weight: bfloat16 [2048, 2048], P(('dp', 'ctx'), 'tp'), may hold values from -0.1875 to 0.1875
- value_weight: bfloat16 [2048, 2048], P(('dp', 'ctx'), 'tp'), may hold values from -0.125 to 0.125
- value_bias: bfloat16 [2048], P('tp'), may hold values from -3 to 3
- output_weight: bfloat16 [2048, 2048], P('tp', ('dp', 'ctx')), may hold values from -0.5 to 0.5
- output_bias: bfloat16 [2048], P(('dp', 'ctx')), may hold values from -3 to 3
- up_weight: bfloat16 [2048, 8192], P(('dp', 'ctx'), 'tp'), may hold values from -0.125 to 0.125
- up_bias: bfloat16 [8192], P('tp'), may hold values from -3 to 3
- down_weight: bfloat16 [8192, 2048], P('tp', ('dp', 'ctx')), may hold values from -0.0625 to 0.0625
- down_bias: bfloat16 [2048], P(('dp', 'ctx')), may hold values from -3 to 3
Outputs:
- layer_output: bfloat16 [8, 2048, 2048], P('dp', 'ctx')
- input_gradient: bfloat16 [8, 2048, 2048], P('dp', 'ctx')
- attention_gain_grad: float32 [2048], P(('dp', 'ctx'))
- attention_bias_grad: float32 [2048], P(('dp', 'ctx'))
- feedforward_gain_grad: float32 [2048], P(('dp', 'ctx'))
- feedforward_bias_grad: float32 [2048], P(('dp', 'ctx'))
- query_weight_grad: float32 [2048, 2048], P(('dp', 'ctx'), 'tp')
- query_bias_grad: float32 [2048], P('tp')
- key_weight_grad: float32 [2048, 2048], P(('dp', 'ctx'), 'tp')
- value_weight_grad: float32 [2048, 2048], P(('dp', 'ctx'), 'tp')
- value_bias_grad: float32 [2048], P('tp')
- output_weight_grad: float32 [2048, 2048], P('tp', ('dp', 'ctx'))
- output_bias_grad: float32 [2048], P(('dp', 'ctx'))
- up_weight_grad: float32 [2048, 8192], P(('dp', 'ctx'), 'tp')
- up_bias_grad: float32 [8192], P('tp')
- down_weight_grad: float32 [8192, 2048], P('tp', ('dp', 'ctx'))
- down_bias_grad: float32 [2048], P(('dp', 'ctx'))
The draws below stay inside these ranges and needn't reach their ends.
All inputs are finite; a program needn't handle non-finite values.
Results may differ from the reference program's by a relative error of at most 0.015.
The reference program's roundings to bfloat16 on the way count: a program that leaves them out, or rounds other values in their place, can miss the bound.
Values may be sent and summed in bfloat16 or wider, within the bound.
A program may use at most 384 MiB of HBM per device.

```python
import math
import jax
import jax.numpy as jnp
from jax import lax

D = 2048
HEADS = 16
HEAD_DIM = 128
FF = 8192
SEQ_LEN = 2048
SEQS = 8


def raised(entries, stream_key, source, target, parts, factor):
    owner, partner = [(jnp.arange(entries.shape[axis_at]) // (entries.shape[axis_at] // parts)).reshape([-1 if axis == axis_at else 1 for axis in range(entries.ndim)]) for axis_at in (source, target)]
    chosen = jax.random.permutation(stream_key, parts)[partner]
    strong = (owner == chosen) | (owner == (partner + parts // 2) % parts)
    return jnp.where(strong, factor * entries, entries)


def block_levels(own_key, shape, cuts, low, high):
    gain, own = 1.0, jax.random.fold_in(own_key, 6)
    for dim, parts in cuts:
        heights = jnp.exp(jax.random.uniform(jax.random.fold_in(own, dim), (parts,), jnp.float32, low / len(cuts), high / len(cuts)))
        gain = gain * jnp.repeat(heights, shape[dim] // parts).reshape([-1 if axis == dim else 1 for axis in range(len(shape))])
    return gain


def gaussian(key, extent, scale, bound, shards=(), held_as=jnp.bfloat16):
    values = scale * jax.random.normal(key, extent, jnp.float32)
    if shards:
        values = values * block_levels(key, extent, shards, -0.22, 0.18)
    return jnp.clip(values, -bound, bound).astype(held_as)


def bell_draw_with(own_key, extent, deviation, limit, pieces, heavy, kind=jnp.bfloat16):
    entries = deviation * jax.random.normal(own_key, extent, jnp.float32)
    if pieces:
        entries = entries * block_levels(own_key, extent, pieces, -0.22, 0.18)
    return jnp.clip(raised(entries, jax.random.fold_in(own_key, 3), *heavy), -limit, limit).astype(kind)


def setup_inputs(seed: int = 0) -> dict:
    key_of = jax.random.split(jax.random.key(seed), 18)
    return {
        "tokens": gaussian(key_of[0], (SEQS, SEQ_LEN, D), 1.0, 6.0, ((0, 4), (1, 4))),
        "cotangent": bell_draw_with(key_of[1], (SEQS, SEQ_LEN, D), 1.0, 6.0, ((0, 4), (1, 4)), (1, 2, 4, 2.0)),
        "attention_gain": jnp.clip(1.0 + 0.1 * jax.random.normal(key_of[2], (D,), jnp.float32), 0.5, 1.5).astype(jnp.bfloat16),
        "attention_bias": gaussian(key_of[3], (D,), 0.5, 3.0, ((0, 16),)),
        "feedforward_gain": jnp.clip(1.0 + 0.1 * jax.random.normal(key_of[4], (D,), jnp.float32), 0.5, 1.5).astype(jnp.bfloat16),
        "feedforward_bias": gaussian(key_of[5], (D,), 0.5, 3.0, ((0, 16),)),
        "query_weight": gaussian(key_of[6], (D, D), (D // 2) ** -0.5, 0.1875, ((0, 16), (1, 2))),
        "query_bias": gaussian(key_of[7], (D,), 0.5, 3.0, ((0, 2),)),
        "key_weight": gaussian(key_of[8], (D, D), (D // 2) ** -0.5, 0.1875, ((0, 16), (1, 2))),
        "value_weight": gaussian(key_of[9], (D, D), D ** -0.5, 0.125, ((0, 16), (1, 2))),
        "value_bias": gaussian(key_of[10], (D,), 0.5, 3.0, ((0, 2),)),
        "output_weight": gaussian(key_of[11], (D, D), (D // 16) ** -0.5, 0.5, ((0, 2), (1, 16))),
        "output_bias": gaussian(key_of[12], (D,), 0.5, 3.0, ((0, 16),)),
        "up_weight": gaussian(key_of[13], (D, FF), D ** -0.5, 0.125, ((0, 16), (1, 2))),
        "up_bias": gaussian(key_of[14], (FF,), 0.5, 3.0, ((0, 2),)),
        "down_weight": gaussian(key_of[15], (FF, D), FF ** -0.5, 0.0625, ((0, 2), (1, 16))),
        "down_bias": gaussian(key_of[16], (D,), 0.5, 3.0, ((0, 16),)),
    }


@jax.custom_vjp
def low(v):
    return lax.optimization_barrier(v.astype(jnp.bfloat16)).astype(jnp.float32)

@jax.custom_vjp
def low_back(v):
    return v

def low_keep(v):
    return (low(v), None)

def low_pass(kept, grad):
    return (grad,)

def back_keep(v):
    return (v, None)

def back_low(kept, grad):
    return (low(grad),)
low.defvjp(low_keep, low_pass)
low_back.defvjp(back_keep, back_low)
EPSILON = 1e-05
NEGATIVE = -1e+30
HIGHEST = lax.Precision.HIGHEST

def product(former, latter):
    return jnp.dot(former, latter, precision=HIGHEST)

def normalize(values):
    average = lax.optimization_barrier(jnp.mean(values, axis=-1, keepdims=True))
    centred = values - average
    spread = lax.rsqrt(lax.optimization_barrier(jnp.mean(centred * centred, axis=-1, keepdims=True)) + EPSILON)
    return centred * spread

def attend(queries, key_rows, value_rows):
    length = queries.shape[0]
    block_rows = math.gcd(length, 512)
    block_count = length // block_rows
    query_blocks = queries.reshape(block_count, block_rows, HEADS, HEAD_DIM)
    key_heads = key_rows.reshape(length, HEADS, HEAD_DIM)
    value_heads = value_rows.reshape(length, HEADS, HEAD_DIM)
    starts = jnp.arange(block_count, dtype=jnp.int32) * block_rows

    def one_block(query_block, first_row, key_all, value_all):
        scores = jnp.einsum('qhd,khd->hqk', query_block, key_all, precision=HIGHEST) * HEAD_DIM ** (-0.5)
        scores = low_back(scores)
        query_pos = first_row + jnp.arange(block_rows, dtype=jnp.int32)
        key_pos = jnp.arange(length, dtype=jnp.int32)
        scores = jnp.where(key_pos[None, None, :] <= query_pos[None, :, None], scores, NEGATIVE)
        attention = low(jax.nn.softmax(scores, axis=-1))
        return jnp.einsum('hqk,khd->qhd', attention, value_all, precision=HIGHEST)
    checked = jax.checkpoint(one_block)
    mixed_heads = lax.map(lambda member: checked(member[0], member[1], key_heads, value_heads), (query_blocks, starts))
    return mixed_heads.reshape(length, HEADS * HEAD_DIM)

def layer(inputs, attention_gain, attention_bias, feedforward_gain, feedforward_bias, query_weight, query_bias, key_weight, value_weight, value_bias, output_weight, output_bias, up_weight, up_bias, down_weight, down_bias):
    first_in = low(normalize(inputs) * attention_gain + attention_bias)
    queries = low_back(low(product(first_in, query_weight) + query_bias))
    key_rows = low_back(low(product(first_in, key_weight)))
    value_rows = low_back(low(product(first_in, value_weight) + value_bias))
    mixed = low_back(low(attend(queries, key_rows, value_rows)))
    residual = inputs + low_back(product(mixed, output_weight) + output_bias)
    second_in = low(normalize(residual) * feedforward_gain + feedforward_bias)
    hidden_pre = low_back(product(second_in, up_weight) + up_bias)
    hidden = low(jax.nn.gelu(hidden_pre, approximate=False))
    return residual + low_back(product(hidden, down_weight) + down_bias)

def reference(tokens, cotangent, attention_gain, attention_bias, feedforward_gain, feedforward_bias, query_weight, query_bias, key_weight, value_weight, value_bias, output_weight, output_bias, up_weight, up_bias, down_weight, down_bias):
    floats = tuple((weight.astype(jnp.float32) for weight in (attention_gain, attention_bias, feedforward_gain, feedforward_bias, query_weight, query_bias, key_weight, value_weight, value_bias, output_weight, output_bias, up_weight, up_bias, down_weight, down_bias)))

    def one_sequence(totals, member):
        sequence, incoming = member
        result, pullback = jax.vjp(layer, sequence.astype(jnp.float32), *floats)
        gradients = pullback(incoming.astype(jnp.float32))
        totals = tuple((total + gradient for total, gradient in zip(totals, gradients[1:])))
        return (totals, (result.astype(jnp.bfloat16), gradients[0].astype(jnp.bfloat16)))
    start_totals = tuple((jnp.zeros(weight.shape, jnp.float32) for weight in floats))
    totals, (outputs, input_grads) = lax.scan(one_sequence, start_totals, (tokens, cotangent))
    return (outputs, input_grads, totals[0], totals[1], totals[2], totals[3], totals[4], totals[5], totals[6], totals[7], totals[8], totals[9], totals[10], totals[11], totals[12], totals[13], totals[14])
```

```python
import functools

import jax
import jax.numpy as jnp
from jax import lax
from jax.experimental import pallas as pl
from jax.experimental.pallas import tpu as pltpu
from jax.sharding import PartitionSpec as P

HEAD_DIM = 128
EPSILON = 1e-05
NEGATIVE = -1e30
F32 = jnp.float32
BF16 = jnp.bfloat16


def product(former, latter):
    return jnp.dot(former, latter, preferred_element_type=F32)


def inner(former, latter):
    return lax.dot_general(former, latter, (((0,), (0,)), ((), ())), preferred_element_type=F32)


def across(former, latter):
    return lax.dot_general(former, latter, (((1,), (1,)), ((), ())), preferred_element_type=F32)


def normalize(values):
    average = jnp.mean(values, axis=-1, keepdims=True)
    centred = values - average
    spread = lax.rsqrt(jnp.mean(centred * centred, axis=-1, keepdims=True) + EPSILON)
    return (centred * spread, spread)


def norm_back(gradient, normed, spread):
    first_mean = jnp.mean(gradient, axis=-1, keepdims=True)
    second_mean = jnp.mean(gradient * normed, axis=-1, keepdims=True)
    return spread * (gradient - first_mean - normed * second_mean)


def after(values, *earlier):
    return lax.optimization_barrier((values, earlier))[0]


def swap(value, axis, mask):
    size = lax.axis_size(axis)
    return lax.ppermute(value, axis, [(i, i ^ mask) for i in range(size)])


def bit_order(part):
    bits = list(range((lax.axis_size("ctx") - 1).bit_length()))
    return bits if part == 0 else bits[::-1]


def share(parts):
    found = {}
    for part in (0, 1):
        have = {0: parts[part]}
        for bit in bit_order(part):
            mask = 1 << bit
            have.update({r ^ mask: swap(have[r], "ctx", mask) for r in list(have)})
        found.update({(r, part): have[r] for r in have})
    return found


def total(partial):
    sums = []
    for part in (0, 1):
        have = {r: partial[(r, part)] for r in range(lax.axis_size("ctx"))}
        for bit in bit_order(part)[::-1]:
            mask = 1 << bit
            came = {r ^ mask: swap(have[r].astype(BF16), "ctx", mask) for r in have if r & mask}
            have = {r: have[r].astype(F32) + came[r].astype(F32) for r in came}
        sums.append(have[0])
    return jnp.concatenate(sums, axis=0)


def joined(blocks):
    return jnp.concatenate([blocks[key] for key in sorted(blocks)], axis=0)


def halves(rows):
    middle = rows.shape[0] // 2
    return (rows[:middle], rows[middle:])


def exchange(pieces):
    count = pieces.shape[0]
    here = lax.axis_index("ctx")
    result = pieces
    for mask in range(1, count):
        other = here ^ mask
        came = swap(lax.dynamic_index_in_dim(pieces, other, 0, keepdims=False), "ctx", mask)
        result = lax.dynamic_update_index_in_dim(result, came, other, 0)
    return result


def gather_weight(pieces):
    count, rows, columns = pieces.shape
    block = exchange(pieces).reshape(count * rows, columns)
    half = lax.all_gather(block, "dp", axis=0, tiled=True)
    return jnp.concatenate([half, swap(half, "tp", 1)], axis=1)


def scatter_grad(former, latter):
    width = latter.shape[1] // 2
    theirs = inner(former, latter[:, width:]).astype(BF16)
    came = swap(theirs, "tp", 1)
    ours = inner(former, latter[:, :width])
    summed = (ours + came.astype(F32)).astype(BF16)
    rows = lax.psum_scatter(summed, "dp", scatter_dimension=0, tiled=True)
    count = lax.axis_size("ctx")
    return exchange(rows.reshape(count, rows.shape[0] // count, width))


def rows_of(here, block, size):
    return pl.multiple_of(lax.bitwise_xor(here, block) * size, size)


def attend_forward_kernel(size, blocks, here_ref, qkv_ref, out_ref, log_ref, scores_ref):
    here = here_ref[0]
    scaling = HEAD_DIM ** (-0.5)
    behind = lax.broadcasted_iota(jnp.int32, (size, size), 1) <= lax.broadcasted_iota(
        jnp.int32, (size, size), 0
    )
    for i in range(blocks):
        at = rows_of(here, i, size)
        queries = qkv_ref[pl.ds(at, size), 0:HEAD_DIM]
        highest = jnp.full((size, 1), NEGATIVE, F32)
        for j in range(i + 1):
            keys = qkv_ref[pl.ds(rows_of(here, j, size), size), HEAD_DIM : 2 * HEAD_DIM]
            scores = across(queries, keys) * scaling
            if j == i:
                scores = jnp.where(behind, scores, NEGATIVE)
            scores_ref[:, j * size : (j + 1) * size] = scores
            highest = jnp.maximum(highest, jnp.max(scores, axis=1, keepdims=True))
        row_total = jnp.zeros((size, 1), F32)
        mixed = jnp.zeros((size, HEAD_DIM), F32)
        for j in range(i + 1):
            exponent = jnp.exp(scores_ref[:, j * size : (j + 1) * size] - highest)
            row_total = row_total + jnp.sum(exponent, axis=1, keepdims=True)
            values = qkv_ref[pl.ds(rows_of(here, j, size), size), 2 * HEAD_DIM : 3 * HEAD_DIM]
            mixed = mixed + product(exponent.astype(BF16), values)
        out_ref[pl.ds(at, size), :] = (mixed / row_total).astype(BF16)
        log_total = jnp.broadcast_to(highest + jnp.log(row_total), (size, HEAD_DIM))
        log_ref[0, :, pl.ds(at, size)] = log_total.T[0:8, :]


def attend_backward_kernel(
    size, blocks, here_ref, qkv_ref, grad_ref, out_ref, log_ref, result_ref, key_ref, value_ref
):
    here = here_ref[0]
    scaling = HEAD_DIM ** (-0.5)
    behind = lax.broadcasted_iota(jnp.int32, (size, size), 0) <= lax.broadcasted_iota(
        jnp.int32, (size, size), 1
    )
    for i in range(blocks):
        at = rows_of(here, i, size)
        queries = qkv_ref[pl.ds(at, size), 0:HEAD_DIM]
        grads = grad_ref[pl.ds(at, size), :]
        both = grads.astype(F32) * out_ref[pl.ds(at, size), :].astype(F32)
        centre = jnp.sum(both.T, axis=0, keepdims=True)
        log_total = log_ref[0, 0:1, pl.ds(at, size)]
        query_grad = jnp.zeros((size, HEAD_DIM), F32)
        for j in range(i + 1):
            there = rows_of(here, j, size)
            keys = qkv_ref[pl.ds(there, size), HEAD_DIM : 2 * HEAD_DIM]
            values = qkv_ref[pl.ds(there, size), 2 * HEAD_DIM : 3 * HEAD_DIM]
            weights = jnp.exp(across(keys, queries) * scaling - log_total)
            if j == i:
                weights = jnp.where(behind, weights, 0.0)
            slopes = (weights * (across(values, grads) - centre)).astype(BF16)
            value_term = product(weights.astype(BF16), grads)
            key_term = product(slopes, queries)
            query_grad = query_grad + inner(slopes, keys)
            place = slice(j * size, (j + 1) * size)
            if i == j:
                value_ref[place, :] = value_term
                key_ref[place, :] = key_term
            else:
                value_ref[place, :] += value_term
                key_ref[place, :] += key_term
        result_ref[pl.ds(at, size), 0:HEAD_DIM] = (query_grad * scaling).astype(BF16)
    for j in range(blocks):
        there = rows_of(here, j, size)
        place = slice(j * size, (j + 1) * size)
        result_ref[pl.ds(there, size), HEAD_DIM : 2 * HEAD_DIM] = (
            key_ref[place, :] * scaling
        ).astype(BF16)
        result_ref[pl.ds(there, size), 2 * HEAD_DIM : 3 * HEAD_DIM] = value_ref[place, :].astype(
            BF16
        )


def attend_forward(here, qkv, blocks):
    length, width = qkv.shape
    heads = width // (3 * HEAD_DIM)
    size = length // blocks
    pairs = heads * length * (length + size) // 2
    return pl.pallas_call(
        functools.partial(attend_forward_kernel, size, blocks),
        out_shape=(
            jax.ShapeDtypeStruct((length, heads * HEAD_DIM), BF16),
            jax.ShapeDtypeStruct((heads, 8, length), F32),
        ),
        grid_spec=pltpu.PrefetchScalarGridSpec(
            num_scalar_prefetch=1,
            grid=(heads,),
            in_specs=[pl.BlockSpec((length, 3 * HEAD_DIM), lambda h, _: (0, h))],
            out_specs=(
                pl.BlockSpec((length, HEAD_DIM), lambda h, _: (0, h)),
                pl.BlockSpec((1, 8, length), lambda h, _: (h, 0, 0)),
            ),
            scratch_shapes=[pltpu.VMEM((size, length), F32)],
        ),
        compiler_params=pltpu.CompilerParams(vmem_limit_bytes=40 * 1024 * 1024),
        cost_estimate=pl.CostEstimate(
            flops=pairs * HEAD_DIM * 8,
            bytes_accessed=length * width * 2 * 2,
            transcendentals=pairs,
        ),
        name="attend_forward",
    )(here, qkv)


def attend_backward(here, qkv, grads, mixed, log_total, blocks):
    length, width = qkv.shape
    heads = width // (3 * HEAD_DIM)
    size = length // blocks
    pairs = heads * length * (length + size) // 2
    narrow = pl.BlockSpec((length, HEAD_DIM), lambda h, _: (0, h))
    wide = pl.BlockSpec((length, 3 * HEAD_DIM), lambda h, _: (0, h))
    return pl.pallas_call(
        functools.partial(attend_backward_kernel, size, blocks),
        out_shape=jax.ShapeDtypeStruct((length, width), BF16),
        grid_spec=pltpu.PrefetchScalarGridSpec(
            num_scalar_prefetch=1,
            grid=(heads,),
            in_specs=[
                wide,
                narrow,
                narrow,
                pl.BlockSpec((1, 8, length), lambda h, _: (h, 0, 0)),
            ],
            out_specs=wide,
            scratch_shapes=[pltpu.VMEM((length, HEAD_DIM), F32)] * 2,
        ),
        compiler_params=pltpu.CompilerParams(vmem_limit_bytes=40 * 1024 * 1024),
        cost_estimate=pl.CostEstimate(
            flops=pairs * HEAD_DIM * 20,
            bytes_accessed=length * width * 2 * 4,
            transcendentals=pairs,
        ),
        name="attend_backward",
    )(here, qkv, grads, mixed, log_total)


def body(
    tokens,
    cotangent,
    attention_gain,
    attention_bias,
    feedforward_gain,
    feedforward_bias,
    query_weight,
    query_bias,
    key_weight,
    value_weight,
    value_bias,
    output_weight,
    output_bias,
    up_weight,
    up_bias,
    down_weight,
    down_bias,
):
    _, local_rows, model_width = tokens.shape
    ctx, dp = lax.axis_size("ctx"), lax.axis_size("dp")
    here, core = lax.axis_index("ctx"), lax.axis_index("tp")
    shard = lax.axis_index("dp") * ctx + here
    here_ref = jnp.full((1,), here, jnp.int32)
    thin = query_weight.shape[0]
    heads = query_weight.shape[1] // (HEAD_DIM * ctx)
    hidden = up_weight.shape[1] // ctx
    half_rows = local_rows // 2
    units = [(r, part) for r in range(ctx) for part in (0, 1)]
    place = {key: slice(n * half_rows, (n + 1) * half_rows) for n, key in enumerate(units)}

    small = jnp.stack(
        [attention_gain, attention_bias, feedforward_gain, feedforward_bias, output_bias, down_bias]
    ).astype(F32)
    table = jnp.zeros((6, model_width), F32)
    table = lax.dynamic_update_slice(table, small, (0, shard * thin))
    flat = ("dp", "ctx")
    mask = 1
    while mask < dp * ctx:
        table = table + lax.ppermute(table, flat, [(i, i ^ mask) for i in range(dp * ctx)])
        mask *= 2
    gain_one, shift_one, gain_two, shift_two, output_shift, down_shift = [
        table[n : n + 1] for n in range(6)
    ]

    packed = jnp.stack(
        [w.reshape(thin, ctx, heads, HEAD_DIM) for w in (query_weight, key_weight, value_weight)],
        axis=3,
    ).reshape(thin, ctx, heads * 3 * HEAD_DIM)
    qkv_weight = gather_weight(packed.transpose(1, 0, 2))
    out_weight = gather_weight(
        output_weight.reshape(ctx, heads * HEAD_DIM, thin).transpose(0, 2, 1)
    )
    rise_weight = gather_weight(up_weight.reshape(thin, ctx, hidden).transpose(1, 0, 2))
    fall_weight = gather_weight(down_weight.reshape(ctx, hidden, thin).transpose(0, 2, 1))

    def own_columns(vector):
        return lax.dynamic_index_in_dim(vector.reshape(ctx, -1), here, 0, keepdims=False)

    query_shift = own_columns(query_bias).reshape(heads, HEAD_DIM)
    value_shift = own_columns(value_bias).reshape(heads, HEAD_DIM)
    qkv_shift = jnp.stack([query_shift, jnp.zeros_like(query_shift), value_shift], axis=1)
    shifts = jnp.concatenate([qkv_shift.reshape(-1), own_columns(up_bias)])
    other_shifts = swap(shifts, "tp", 1)
    wide = heads * 3 * HEAD_DIM
    qkv_shift = jnp.concatenate([shifts[:wide], other_shifts[:wide]]).astype(F32)
    rise_shift = jnp.concatenate([shifts[wide:], other_shifts[wide:]]).astype(F32)

    inputs = lax.dynamic_index_in_dim(tokens, core, 0, keepdims=False).astype(F32)
    incoming = lax.dynamic_index_in_dim(cotangent, core, 0, keepdims=False)
    normed_one, spread_one = normalize(inputs)
    input_one = (normed_one * gain_one + shift_one).astype(BF16)
    ones = joined(share(halves(input_one)))
    qkv = (product(ones, qkv_weight) + qkv_shift).astype(BF16)
    later = after(incoming, ones)
    grads_in = joined(share(halves(later)))
    mixed, log_total = attend_forward(here_ref, qkv, ctx)
    branch = total({key: across(mixed[place[key]], out_weight) for key in units})
    residual = inputs + (branch + output_shift)

    normed_two, spread_two = normalize(residual)
    input_two = (normed_two * gain_two + shift_two).astype(BF16)
    hidden_back = product(grads_in, fall_weight)
    twos = share(halves(input_two))
    hid, hid_grad, second = {}, {}, {}
    for key in units:
        pre = product(twos[key], rise_weight) + rise_shift
        cumulative = 0.5 * (1.0 + lax.erf(pre * 0.7071067811865476))
        density = jnp.exp(-0.5 * pre * pre) * 0.3989422804014327
        hid[key] = (pre * cumulative).astype(BF16)
        hid_grad[key] = (hidden_back[place[key]] * (cumulative + pre * density)).astype(BF16)
        second[key] = across(hid_grad[key], rise_weight)
    second_grad = total(second)
    gain_two_sum = jnp.sum(second_grad * normed_two, axis=0)
    bias_two_sum = jnp.sum(second_grad, axis=0)
    wide_incoming = incoming.astype(F32)
    residual_grad = wide_incoming + norm_back(second_grad * gain_two, normed_two, spread_two)
    branch_grad = residual_grad.astype(BF16)
    branch_grads = joined(share(halves(branch_grad)))

    all_hid, all_hid_grad, all_twos = joined(hid), joined(hid_grad), joined(twos)
    fall_grad = scatter_grad(grads_in, all_hid)
    rise_grad = scatter_grad(all_twos, all_hid_grad)
    rise_bias = jnp.sum(all_hid_grad.astype(F32), axis=0)

    mixed_grad = product(branch_grads, out_weight).astype(BF16)
    out_grad = scatter_grad(branch_grads, mixed)
    late_hid = after(all_hid, branch_grads)
    block_out = residual + (
        total({key: across(late_hid[place[key]], fall_weight) for key in units}) + down_shift
    )
    own_out = block_out.astype(BF16)
    qkv_grads = attend_backward(here_ref, qkv, mixed_grad, mixed, log_total, ctx)
    first_grad = total({key: across(qkv_grads[place[key]], qkv_weight) for key in units})
    qkv_grad = scatter_grad(ones, qkv_grads)
    qkv_bias = jnp.sum(qkv_grads.astype(F32), axis=0)
    gain_one_sum = jnp.sum(first_grad * normed_one, axis=0)
    bias_one_sum = jnp.sum(first_grad, axis=0)
    token_grad = residual_grad + norm_back(first_grad * gain_one, normed_one, spread_one)
    own_grad = token_grad.astype(BF16)

    def both_sequences(own):
        other = swap(own, "tp", 1)
        first = core == 0
        return jnp.stack([jnp.where(first, own, other), jnp.where(first, other, own)])

    def spread_columns(vector):
        own, other = jnp.split(vector, 2)
        whole = jnp.zeros((2, ctx, own.shape[0]), F32)
        whole = lax.dynamic_update_slice(whole, own[None, None], (core, here, 0))
        return lax.dynamic_update_slice(whole, other[None, None], (1 - core, here, 0))

    features = jnp.stack(
        [
            gain_one_sum,
            bias_one_sum,
            gain_two_sum,
            bias_two_sum,
            jnp.sum(branch_grad.astype(F32), axis=0),
            jnp.sum(wide_incoming, axis=0),
        ]
    )
    features, qkv_bias, rise_bias = lax.psum(
        (features, spread_columns(qkv_bias), spread_columns(rise_bias)), ("dp", "ctx", "tp")
    )
    features = lax.dynamic_slice(features, (0, shard * thin), (6, thin))
    qkv_bias = lax.dynamic_index_in_dim(qkv_bias, core, 0, keepdims=False)
    qkv_bias = qkv_bias.reshape(ctx * heads, 3, HEAD_DIM)
    rise_bias = lax.dynamic_index_in_dim(rise_bias, core, 0, keepdims=False).reshape(-1)

    qkv_grad = qkv_grad.reshape(ctx, thin, heads, 3, HEAD_DIM).transpose(3, 1, 0, 2, 4)
    qkv_grad = qkv_grad.reshape(3, thin, ctx * heads * HEAD_DIM).astype(F32)
    return (
        both_sequences(own_out),
        both_sequences(own_grad),
        features[0],
        features[1],
        features[2],
        features[3],
        qkv_grad[0],
        qkv_bias[:, 0].reshape(-1),
        qkv_grad[1],
        qkv_grad[2],
        qkv_bias[:, 2].reshape(-1),
        out_grad.transpose(0, 2, 1).reshape(-1, thin).astype(F32),
        features[4],
        rise_grad.transpose(1, 0, 2).reshape(thin, -1).astype(F32),
        rise_bias,
        fall_grad.transpose(0, 2, 1).reshape(-1, thin).astype(F32),
        features[5],
    )


def solution(mesh):
    placed = (
        P("dp", "ctx", None),
        P("dp", "ctx", None),
        P(("dp", "ctx")),
        P(("dp", "ctx")),
        P(("dp", "ctx")),
        P(("dp", "ctx")),
        P(("dp", "ctx"), "tp"),
        P("tp"),
        P(("dp", "ctx"), "tp"),
        P(("dp", "ctx"), "tp"),
        P("tp"),
        P("tp", ("dp", "ctx")),
        P(("dp", "ctx")),
        P(("dp", "ctx"), "tp"),
        P("tp"),
        P("tp", ("dp", "ctx")),
        P(("dp", "ctx")),
    )
    return jax.shard_map(
        body,
        mesh=mesh,
        in_specs=placed,
        out_specs=(
            P("dp", "ctx", None),
            P("dp", "ctx", None),
            P(("dp", "ctx")),
            P(("dp", "ctx")),
            P(("dp", "ctx")),
            P(("dp", "ctx")),
            P(("dp", "ctx"), "tp"),
            P("tp"),
            P(("dp", "ctx"), "tp"),
            P(("dp", "ctx"), "tp"),
            P("tp"),
            P("tp", ("dp", "ctx")),
            P(("dp", "ctx")),
            P(("dp", "ctx"), "tp"),
            P("tp"),
            P("tp", ("dp", "ctx")),
            P(("dp", "ctx")),
        ),
        check_vma=False,
    )
```

```python
import functools

import jax
import jax.numpy as jnp
from jax import lax
from jax.experimental import pallas as pl
from jax.experimental.pallas import tpu as pltpu
from jax.sharding import PartitionSpec as P

HEAD_DIM = 128
EPSILON = 1e-05
NEGATIVE = -1e30
F32 = jnp.float32
BF16 = jnp.bfloat16
MESH = pl.DeviceIdType.MESH


def product(former, latter):
    return jnp.dot(former, latter, preferred_element_type=F32)


def inner(former, latter):
    return lax.dot_general(former, latter, (((0,), (0,)), ((), ())), preferred_element_type=F32)


def across(former, latter):
    return lax.dot_general(former, latter, (((1,), (1,)), ((), ())), preferred_element_type=F32)


def normalize(values):
    average = jnp.mean(values, axis=-1, keepdims=True)
    centred = values - average
    spread = lax.rsqrt(jnp.mean(centred * centred, axis=-1, keepdims=True) + EPSILON)
    return (centred * spread, spread)


def norm_back(gradient, normed, spread):
    first_mean = jnp.mean(gradient, axis=-1, keepdims=True)
    second_mean = jnp.mean(gradient * normed, axis=-1, keepdims=True)
    return spread * (gradient - first_mean - normed * second_mean)


def after(values, *earlier):
    return lax.optimization_barrier((values, earlier))[0]


def swap(value, axis, mask):
    size = lax.axis_size(axis)
    return lax.ppermute(value, axis, [(i, i ^ mask) for i in range(size)])


def bit_order(part):
    bits = list(range((lax.axis_size("ctx") - 1).bit_length()))
    return bits if part == 0 else bits[::-1]


def share(parts):
    found = {}
    for part in (0, 1):
        have = {0: parts[part]}
        for bit in bit_order(part):
            mask = 1 << bit
            have.update({r ^ mask: swap(have[r], "ctx", mask) for r in list(have)})
        found.update({(r, part): have[r] for r in have})
    return found


def total(partial):
    sums = []
    for part in (0, 1):
        have = {r: partial[(r, part)] for r in range(lax.axis_size("ctx"))}
        for bit in bit_order(part)[::-1]:
            mask = 1 << bit
            came = {r ^ mask: swap(have[r].astype(BF16), "ctx", mask) for r in have if r & mask}
            have = {r: have[r].astype(F32) + came[r].astype(F32) for r in came}
        sums.append(have[0])
    return jnp.concatenate(sums, axis=0)


def summed(values, axes):
    for axis in axes:
        mask = 1
        while mask < lax.axis_size(axis):
            values = values + swap(values, axis, mask)
            mask *= 2
    return values


def joined(blocks):
    return jnp.concatenate([blocks[key] for key in sorted(blocks)], axis=0)


def halves(rows):
    middle = rows.shape[0] // 2
    return (rows[:middle], rows[middle:])


def exchange(pieces):
    count = pieces.shape[0]
    here = lax.axis_index("ctx")
    result = pieces
    for mask in range(1, count):
        other = here ^ mask
        came = swap(lax.dynamic_index_in_dim(pieces, other, 0, keepdims=False), "ctx", mask)
        result = lax.dynamic_update_index_in_dim(result, came, other, 0)
    return result


def gather_weight(pieces):
    count, rows, columns = pieces.shape
    block = exchange(pieces).reshape(count * rows, columns)
    half = lax.all_gather(block, "dp", axis=0, tiled=True)
    return jnp.concatenate([half, swap(half, "tp", 1)], axis=1)


def weight_grad(former, latter):
    width = latter.shape[1] // 2
    theirs = inner(former, latter[:, width:]).astype(BF16)
    return (theirs, inner(former, latter[:, :width]))


def over_cores(theirs, ours):
    return (ours + swap(theirs, "tp", 1).astype(F32)).astype(BF16)


def over_dp(both):
    return lax.psum_scatter(both, "dp", scatter_dimension=0, tiled=True)


def to_shards(rows):
    count = lax.axis_size("ctx")
    return exchange(rows.reshape(count, rows.shape[0] // count, rows.shape[1]))


def rows_of(here, block, size):
    return pl.multiple_of(lax.bitwise_xor(here, block) * size, size)


def attend_forward_kernel(size, blocks, here_ref, qkv_ref, out_ref, log_ref, scores_ref):
    here = here_ref[0]
    scaling = HEAD_DIM ** (-0.5)
    behind = lax.broadcasted_iota(jnp.int32, (size, size), 1) <= lax.broadcasted_iota(
        jnp.int32, (size, size), 0
    )
    for i in range(blocks):
        at = rows_of(here, i, size)
        queries = qkv_ref[pl.ds(at, size), 0:HEAD_DIM]
        highest = jnp.full((size, 1), NEGATIVE, F32)
        for j in range(i + 1):
            keys = qkv_ref[pl.ds(rows_of(here, j, size), size), HEAD_DIM : 2 * HEAD_DIM]
            scores = across(queries, keys) * scaling
            if j == i:
                scores = jnp.where(behind, scores, NEGATIVE)
            scores_ref[:, j * size : (j + 1) * size] = scores
            highest = jnp.maximum(highest, jnp.max(scores, axis=1, keepdims=True))
        row_total = jnp.zeros((size, 1), F32)
        mixed = jnp.zeros((size, HEAD_DIM), F32)
        for j in range(i + 1):
            exponent = jnp.exp(scores_ref[:, j * size : (j + 1) * size] - highest)
            row_total = row_total + jnp.sum(exponent, axis=1, keepdims=True)
            values = qkv_ref[pl.ds(rows_of(here, j, size), size), 2 * HEAD_DIM : 3 * HEAD_DIM]
            mixed = mixed + product(exponent.astype(BF16), values)
        out_ref[pl.ds(at, size), :] = (mixed / row_total).astype(BF16)
        log_total = jnp.broadcast_to(highest + jnp.log(row_total), (size, HEAD_DIM))
        log_ref[0, :, pl.ds(at, size)] = log_total.T[0:8, :]


def attend_backward_kernel(
    size, blocks, here_ref, qkv_ref, grad_ref, out_ref, log_ref, result_ref, key_ref, value_ref
):
    here = here_ref[0]
    scaling = HEAD_DIM ** (-0.5)
    behind = lax.broadcasted_iota(jnp.int32, (size, size), 0) <= lax.broadcasted_iota(
        jnp.int32, (size, size), 1
    )
    for i in range(blocks):
        at = rows_of(here, i, size)
        queries = qkv_ref[pl.ds(at, size), 0:HEAD_DIM]
        grads = grad_ref[pl.ds(at, size), :]
        both = grads.astype(F32) * out_ref[pl.ds(at, size), :].astype(F32)
        centre = jnp.sum(both.T, axis=0, keepdims=True)
        log_total = log_ref[0, 0:1, pl.ds(at, size)]
        query_grad = jnp.zeros((size, HEAD_DIM), F32)
        for j in range(i + 1):
            there = rows_of(here, j, size)
            keys = qkv_ref[pl.ds(there, size), HEAD_DIM : 2 * HEAD_DIM]
            values = qkv_ref[pl.ds(there, size), 2 * HEAD_DIM : 3 * HEAD_DIM]
            weights = jnp.exp(across(keys, queries) * scaling - log_total)
            if j == i:
                weights = jnp.where(behind, weights, 0.0)
            slopes = (weights * (across(values, grads) - centre)).astype(BF16)
            value_term = product(weights.astype(BF16), grads)
            key_term = product(slopes, queries)
            query_grad = query_grad + inner(slopes, keys)
            place = slice(j * size, (j + 1) * size)
            if i == j:
                value_ref[place, :] = value_term
                key_ref[place, :] = key_term
            else:
                value_ref[place, :] += value_term
                key_ref[place, :] += key_term
        result_ref[pl.ds(at, size), 0:HEAD_DIM] = (query_grad * scaling).astype(BF16)
    for j in range(blocks):
        there = rows_of(here, j, size)
        place = slice(j * size, (j + 1) * size)
        result_ref[pl.ds(there, size), HEAD_DIM : 2 * HEAD_DIM] = (
            key_ref[place, :] * scaling
        ).astype(BF16)
        result_ref[pl.ds(there, size), 2 * HEAD_DIM : 3 * HEAD_DIM] = value_ref[place, :].astype(
            BF16
        )


class Links:
    def __init__(self, count, half):
        self.count, self.half = count, half
        self.bits = (count - 1).bit_length()
        self.pairs = [(i, part) for i in range(1, count) for part in (0, 1)]
        self.slot = {pair: n for n, pair in enumerate(self.pairs)}

    def block(self, i, part):
        if part == 0:
            return i
        return sum(((i >> b) & 1) << (self.bits - 1 - b) for b in range(self.bits))

    def top(self, i):
        return 1 << (i.bit_length() - 1)

    def near(self, i):
        return i ^ self.top(i)

    def given(self, i):
        return [j for j in range(self.count - 1, 0, -1) if self.near(j) == i]

    def far(self, i, part):
        mask = self.block(self.top(i), part)
        return {"ctx": lax.bitwise_xor(lax.axis_index("ctx"), mask)}

    def start_row(self, i, part):
        return (2 * self.block(i, part) + part) * self.half

    def rows(self, ref, i, part):
        return ref.at[pl.ds(self.start_row(i, part), self.half)]

    def greet(self, others=()):
        barrier = pltpu.get_barrier_semaphore()
        partners = [
            {"ctx": lax.bitwise_xor(lax.axis_index("ctx"), 1 << bit)} for bit in range(self.bits)
        ]
        partners += list(others)
        for partner in partners:
            pl.semaphore_signal(barrier, 1, device_id=partner, device_id_type=MESH)
        pl.semaphore_wait(barrier, len(partners))

    def sharing(self, own_ref, full_ref, send_sem, recv_sem):
        copies = {}
        for i, part in self.pairs:
            near = self.near(i)
            source = (
                own_ref.at[pl.ds(part * self.half, self.half)]
                if near == 0
                else self.rows(full_ref, near, part)
            )
            n = self.slot[(i, part)]
            copies[(i, part)] = pltpu.make_async_remote_copy(
                src_ref=source,
                dst_ref=self.rows(full_ref, i, part),
                send_sem=send_sem.at[n],
                recv_sem=recv_sem.at[n],
                device_id=self.far(i, part),
                device_id_type=MESH,
            )
        return copies

    def summing(self, send_ref, recv_ref, send_sem, recv_sem):
        copies = {}
        for i, part in self.pairs:
            n = self.slot[(i, part)]
            copies[(i, part)] = pltpu.make_async_remote_copy(
                src_ref=send_ref.at[n],
                dst_ref=recv_ref.at[n],
                send_sem=send_sem.at[n],
                recv_sem=recv_sem.at[n],
                device_id=self.far(i, part),
                device_id_type=MESH,
            )
        return copies

    def pass_on(self, copies, arrived, own=False):
        for i, part in self.pairs:
            if self.near(i) == arrived:
                copies[(i, part)].start()

    def finish(self, copies, kept_ref, send_ref, recv_ref, result_ref):
        middle = self.count // 2
        for i in range(middle - 1, -1, -1):
            for part in (0, 1):
                for j in self.given(i):
                    copies[(j, part)].wait_recv()
                chunk = min(32, self.half)

                def add(step, _, i=i, part=part):
                    at = pl.ds(pl.multiple_of(step * chunk, chunk), chunk)
                    value = kept_ref[2 * i + part, at, :]
                    for j in self.given(i):
                        value = value + recv_ref[self.slot[(j, part)], at, :].astype(F32)
                    if i == 0:
                        place = pl.ds(pl.multiple_of(part * self.half + step * chunk, chunk), chunk)
                        result_ref[place, :] = value
                    else:
                        send_ref[self.slot[(i, part)], at, :] = value.astype(BF16)
                    return 0

                lax.fori_loop(0, self.half // chunk, add, 0)
                if i:
                    copies[(i, part)].start()
        for pair in self.pairs:
            copies[pair].wait_send()


def feed_forward_kernel(
    links,
    own_ref,
    grads_ref,
    rise_ref,
    shift_ref,
    fall_ref,
    full_ref,
    hid_ref,
    slope_ref,
    result_ref,
    bias_ref,
    rise_v,
    fall_v,
    rows_v,
    grads_v,
    hid_v,
    slope_v,
    kept_v,
    send_v,
    recv_v,
    load_sem,
    store_sem,
    share_send,
    share_recv,
    sum_send,
    sum_recv,
):
    half, count = links.half, links.count
    width, hidden = rise_v.shape
    links.greet()
    shares = links.sharing(own_ref, full_ref, share_send, share_recv)
    sums = links.summing(send_v, recv_v, sum_send, sum_recv)
    links.pass_on(shares, 0)
    keep = pltpu.make_async_copy(own_ref, full_ref.at[pl.ds(0, 2 * half)], load_sem.at[0])
    keep.start()
    first = pltpu.make_async_copy(own_ref, rows_v, load_sem.at[1])
    first.start()
    rise = pltpu.make_async_copy(rise_ref, rise_v, load_sem.at[2])
    rise.start()
    fall = pltpu.make_async_copy(fall_ref, fall_v, load_sem.at[3])
    fall.start()
    bias_ref[...] = jnp.zeros_like(bias_ref)

    def loads(ref, buffer, i, base):
        return [
            pltpu.make_async_copy(
                links.rows(ref, i, part), buffer.at[pl.ds(part * half, half)], load_sem.at[base + part]
            )
            for part in (0, 1)
        ]

    grad_loads = loads(grads_ref, grads_v.at[0], 0, 4)
    for copy in grad_loads:
        copy.start()
    stores = []
    tile = min(256, hidden)
    for i in range(count):
        if i == 0:
            first.wait()
            rise.wait()
            fall.wait()
        else:
            for part in (0, 1):
                shares[(i, part)].wait_recv()
            links.pass_on(shares, i)
            row_loads = loads(full_ref, rows_v, i, 8)
            for copy in row_loads:
                copy.start()
            for copy in row_loads:
                copy.wait()
        for copy in grad_loads:
            copy.wait()
        if i + 1 < count:
            grad_loads = loads(grads_ref, grads_v.at[(i + 1) % 2], i + 1, 4 + 2 * ((i + 1) % 2))
            for copy in grad_loads:
                copy.start()
        for copy in stores:
            copy.wait()

        def rise_step(step, _, i=i):
            at = pl.ds(pl.multiple_of(step * tile, tile), tile)
            pre = product(rows_v[...], rise_v[:, at]) + shift_ref[0:1, at]
            back = product(grads_v[i % 2], fall_v[:, at])
            cumulative = 0.5 * (1.0 + lax.erf(pre * 0.7071067811865476))
            density = jnp.exp(-0.5 * pre * pre) * 0.3989422804014327
            hid_v[:, at] = (pre * cumulative).astype(BF16)
            slope = (back * (cumulative + pre * density)).astype(BF16)
            slope_v[:, at] = slope
            bias_ref[0:1, at] += jnp.sum(slope.astype(F32), axis=0, keepdims=True)
            return 0

        lax.fori_loop(0, hidden // tile, rise_step, 0)
        stores = []
        for n, (buffer, ref) in enumerate(((hid_v, hid_ref), (slope_v, slope_ref))):
            for part in (0, 1):
                copy = pltpu.make_async_copy(
                    buffer.at[pl.ds(part * half, half)],
                    links.rows(ref, i, part),
                    store_sem.at[2 * n + part],
                )
                copy.start()
                stores.append(copy)

        def back_step(step, _, i=i):
            at = pl.ds(pl.multiple_of(step * 256, 256), 256)
            term = across(slope_v[...], rise_v[at, :])
            for part in (0, 1):
                piece = term[part * half : (part + 1) * half]
                if i < count // 2:
                    kept_v[2 * i + part, :, at] = piece
                else:
                    send_v[links.slot[(i, part)], :, at] = piece.astype(BF16)
            return 0

        lax.fori_loop(0, width // 256, back_step, 0)
        if i >= count // 2:
            for part in (0, 1):
                sums[(i, part)].start()
    links.finish(sums, kept_v, send_v, recv_v, result_ref)
    for copy in stores:
        copy.wait()
    keep.wait()
    for pair in links.pairs:
        shares[pair].wait_send()


def feed_forward(own, grads, rise_weight, shift, fall_weight, count):
    rows, width = own.shape
    hidden = rise_weight.shape[1]
    length = rows * count
    links = Links(count, rows // 2)
    half, copies = links.half, len(links.pairs)
    anywhere = pl.BlockSpec(memory_space=pl.ANY)
    inside = pl.BlockSpec(memory_space=pltpu.VMEM)
    dma = pltpu.SemaphoreType.DMA
    return pl.pallas_call(
        functools.partial(feed_forward_kernel, links),
        out_shape=(
            jax.ShapeDtypeStruct((length, width), BF16),
            jax.ShapeDtypeStruct((length, hidden), BF16),
            jax.ShapeDtypeStruct((length, hidden), BF16),
            jax.ShapeDtypeStruct((rows, width), F32),
            jax.ShapeDtypeStruct((1, hidden), F32),
        ),
        in_specs=[anywhere, anywhere, anywhere, inside, anywhere],
        out_specs=(anywhere, anywhere, anywhere, inside, inside),
        scratch_shapes=[
            pltpu.VMEM((width, hidden), BF16),
            pltpu.VMEM((width, hidden), BF16),
            pltpu.VMEM((rows, width), BF16),
            pltpu.VMEM((2, rows, width), BF16),
            pltpu.VMEM((rows, hidden), BF16),
            pltpu.VMEM((rows, hidden), BF16),
            pltpu.VMEM((count, half, width), F32),
            pltpu.VMEM((copies, half, width), BF16),
            pltpu.VMEM((copies, half, width), BF16),
            dma((10,)),
            dma((4,)),
            dma((copies,)),
            dma((copies,)),
            dma((copies,)),
            dma((copies,)),
        ],
        compiler_params=pltpu.CompilerParams(
            collective_id=3, has_side_effects=True, vmem_limit_bytes=58 * 1024 * 1024
        ),
        cost_estimate=pl.CostEstimate(
            flops=6 * length * width * hidden,
            bytes_accessed=length * width * 8 + width * hidden * 4 + length * hidden * 4,
            transcendentals=length * hidden * 2,
        ),
        name="feed_forward",
    )(own, grads, rise_weight, shift, fall_weight)


def attend_forward(here, qkv, blocks):
    length, width = qkv.shape
    heads = width // (3 * HEAD_DIM)
    size = length // blocks
    pairs = heads * length * (length + size) // 2
    return pl.pallas_call(
        functools.partial(attend_forward_kernel, size, blocks),
        out_shape=(
            jax.ShapeDtypeStruct((length, heads * HEAD_DIM), BF16),
            jax.ShapeDtypeStruct((heads, 8, length), F32),
        ),
        grid_spec=pltpu.PrefetchScalarGridSpec(
            num_scalar_prefetch=1,
            grid=(heads,),
            in_specs=[pl.BlockSpec((length, 3 * HEAD_DIM), lambda h, _: (0, h))],
            out_specs=(
                pl.BlockSpec((length, HEAD_DIM), lambda h, _: (0, h)),
                pl.BlockSpec((1, 8, length), lambda h, _: (h, 0, 0)),
            ),
            scratch_shapes=[pltpu.VMEM((size, length), F32)],
        ),
        compiler_params=pltpu.CompilerParams(vmem_limit_bytes=40 * 1024 * 1024),
        cost_estimate=pl.CostEstimate(
            flops=pairs * HEAD_DIM * 8,
            bytes_accessed=length * width * 2 * 2,
            transcendentals=pairs,
        ),
        name="attend_forward",
    )(here, qkv)


def attend_backward(here, qkv, grads, mixed, log_total, blocks):
    length, width = qkv.shape
    heads = width // (3 * HEAD_DIM)
    size = length // blocks
    pairs = heads * length * (length + size) // 2
    narrow = pl.BlockSpec((length, HEAD_DIM), lambda h, _: (0, h))
    wide = pl.BlockSpec((length, 3 * HEAD_DIM), lambda h, _: (0, h))
    return pl.pallas_call(
        functools.partial(attend_backward_kernel, size, blocks),
        out_shape=jax.ShapeDtypeStruct((length, width), BF16),
        grid_spec=pltpu.PrefetchScalarGridSpec(
            num_scalar_prefetch=1,
            grid=(heads,),
            in_specs=[
                wide,
                narrow,
                narrow,
                pl.BlockSpec((1, 8, length), lambda h, _: (h, 0, 0)),
            ],
            out_specs=wide,
            scratch_shapes=[pltpu.VMEM((length, HEAD_DIM), F32)] * 2,
        ),
        compiler_params=pltpu.CompilerParams(vmem_limit_bytes=40 * 1024 * 1024),
        cost_estimate=pl.CostEstimate(
            flops=pairs * HEAD_DIM * 20,
            bytes_accessed=length * width * 2 * 4,
            transcendentals=pairs,
        ),
        name="attend_backward",
    )(here, qkv, grads, mixed, log_total)


def body(
    tokens,
    cotangent,
    attention_gain,
    attention_bias,
    feedforward_gain,
    feedforward_bias,
    query_weight,
    query_bias,
    key_weight,
    value_weight,
    value_bias,
    output_weight,
    output_bias,
    up_weight,
    up_bias,
    down_weight,
    down_bias,
):
    _, local_rows, model_width = tokens.shape
    ctx, dp = lax.axis_size("ctx"), lax.axis_size("dp")
    here, core = lax.axis_index("ctx"), lax.axis_index("tp")
    shard = lax.axis_index("dp") * ctx + here
    here_ref = jnp.full((1,), here, jnp.int32)
    thin = query_weight.shape[0]
    heads = query_weight.shape[1] // (HEAD_DIM * ctx)
    hidden = up_weight.shape[1] // ctx
    half_rows = local_rows // 2
    units = [(r, part) for r in range(ctx) for part in (0, 1)]
    place = {key: slice(n * half_rows, (n + 1) * half_rows) for n, key in enumerate(units)}

    inputs = lax.dynamic_index_in_dim(tokens, core, 0, keepdims=False)
    incoming = lax.dynamic_index_in_dim(cotangent, core, 0, keepdims=False)

    packed = jnp.stack(
        [w.reshape(thin, ctx, heads, HEAD_DIM) for w in (query_weight, key_weight, value_weight)],
        axis=3,
    ).reshape(thin, ctx, heads * 3 * HEAD_DIM)
    qkv_pieces = packed.transpose(1, 0, 2)
    qkv_weight = gather_weight(qkv_pieces)
    token_blocks = share(halves(inputs))
    first_arrivals = [token_blocks[(1, 0)], token_blocks[(ctx // 2, 1)]]
    out_pieces, rise_pieces, fall_pieces = after(
        (
            output_weight.reshape(ctx, heads * HEAD_DIM, thin).transpose(0, 2, 1),
            up_weight.reshape(thin, ctx, hidden).transpose(1, 0, 2),
            down_weight.reshape(ctx, hidden, thin).transpose(0, 2, 1),
        ),
        *first_arrivals,
    )
    out_weight = gather_weight(out_pieces)
    rise_weight = gather_weight(rise_pieces)
    fall_weight = gather_weight(fall_pieces)

    small = jnp.stack(
        [attention_gain, attention_bias, feedforward_gain, feedforward_bias, output_bias, down_bias]
    ).astype(F32)
    table = jnp.zeros((6, model_width), F32)
    table = lax.dynamic_update_slice(table, small, (0, shard * thin))
    table = summed(table, ("dp", "ctx"))
    gain_one, shift_one, gain_two, shift_two, output_shift, down_shift = [
        table[n : n + 1] for n in range(6)
    ]

    def own_columns(vector):
        return lax.dynamic_index_in_dim(vector.reshape(ctx, -1), here, 0, keepdims=False)

    query_shift = own_columns(query_bias).reshape(heads, HEAD_DIM)
    value_shift = own_columns(value_bias).reshape(heads, HEAD_DIM)
    qkv_shift = jnp.stack([query_shift, jnp.zeros_like(query_shift), value_shift], axis=1)
    shifts = jnp.concatenate([qkv_shift.reshape(-1), own_columns(up_bias)])
    other_shifts = swap(shifts, "tp", 1)
    wide = heads * 3 * HEAD_DIM
    qkv_shift = jnp.concatenate([shifts[:wide], other_shifts[:wide]]).astype(F32)
    rise_shift = jnp.concatenate([shifts[wide:], other_shifts[wide:]]).astype(F32)

    def first_norm(rows):
        normed, spread = normalize(rows.astype(F32))
        return (normed * gain_one + shift_one).astype(BF16), normed, spread

    ones = joined({key: first_norm(token_blocks[key])[0] for key in units})
    wide_inputs = inputs.astype(F32)
    _, normed_one, spread_one = first_norm(inputs)
    qkv = (product(ones, qkv_weight) + qkv_shift).astype(BF16)
    later = after(incoming, *[token_blocks[key] for key in units])
    grads_in = joined(share(halves(later)))
    mixed, log_total = attend_forward(here_ref, qkv, ctx)
    branch = total({key: across(mixed[place[key]], out_weight) for key in units})
    residual = wide_inputs + (branch + output_shift)

    normed_two, spread_two = normalize(residual)
    input_two = (normed_two * gain_two + shift_two).astype(BF16)
    all_twos, all_hid, all_hid_grad, second_grad, rise_bias = feed_forward(
        input_two, grads_in, rise_weight, rise_shift[None], fall_weight, ctx
    )
    fall_parts = weight_grad(grads_in, all_hid)
    rise_parts = weight_grad(all_twos, all_hid_grad)
    second_grad = after(second_grad, fall_parts, rise_parts)
    fall_both = over_cores(*fall_parts)
    rise_both = over_cores(*rise_parts)
    fall_rows = over_dp(fall_both)
    rise_rows = over_dp(rise_both)
    gain_two_sum = jnp.sum(second_grad * normed_two, axis=0)
    bias_two_sum = jnp.sum(second_grad, axis=0)
    wide_incoming = incoming.astype(F32)
    residual_grad = wide_incoming + norm_back(second_grad * gain_two, normed_two, spread_two)
    branch_grad = residual_grad.astype(BF16)
    branch_blocks = share(halves(branch_grad))
    late_hid = after(all_hid, branch_grad)
    lasts = {key: across(late_hid[place[key]], fall_weight) for key in units}
    branch_blocks, lasts = lax.optimization_barrier((branch_blocks, lasts))
    branch_grads = joined(branch_blocks)
    block_out = residual + (total(lasts) + down_shift)

    mixed_grad = product(branch_grads, out_weight).astype(BF16)
    mixed_grad = after(mixed_grad, fall_rows)
    own_out = block_out.astype(BF16)
    qkv_grads = attend_backward(here_ref, qkv, mixed_grad, mixed, log_total, ctx)
    qkv_grads = after(qkv_grads, rise_rows, own_out)
    first_terms = {key: across(qkv_grads[place[key]], qkv_weight) for key in units}
    first_grad = total(first_terms)
    late_grads = after(qkv_grads, first_terms)
    qkv_parts = weight_grad(ones, late_grads)
    out_parts = weight_grad(branch_grads, after(mixed, first_terms))
    qkv_bias = jnp.sum(late_grads.astype(F32), axis=0)
    qkv_both = over_cores(*qkv_parts)
    out_both = over_cores(*out_parts)
    first_grad = after(first_grad, qkv_both, out_both, qkv_bias)
    qkv_grad = to_shards(over_dp(qkv_both))
    out_grad = to_shards(over_dp(out_both))
    fall_grad = to_shards(fall_rows)
    rise_grad = to_shards(rise_rows)
    gain_one_sum = jnp.sum(first_grad * normed_one, axis=0)
    bias_one_sum = jnp.sum(first_grad, axis=0)
    token_grad = residual_grad + norm_back(first_grad * gain_one, normed_one, spread_one)
    own_grad = token_grad.astype(BF16)

    def both_sequences(own):
        other = swap(own, "tp", 1)
        first = core == 0
        return jnp.stack([jnp.where(first, own, other), jnp.where(first, other, own)])

    def spread_columns(vector):
        own, other = jnp.split(vector, 2)
        whole = jnp.zeros((2, ctx, own.shape[0]), F32)
        whole = lax.dynamic_update_slice(whole, own[None, None], (core, here, 0))
        return lax.dynamic_update_slice(whole, other[None, None], (1 - core, here, 0))

    everywhere = ("tp", "ctx", "dp")
    early = jnp.stack(
        [
            gain_two_sum,
            bias_two_sum,
            jnp.sum(branch_grad.astype(F32), axis=0),
            jnp.sum(wide_incoming, axis=0),
        ]
    )
    features = jnp.concatenate(
        [
            summed(jnp.stack([gain_one_sum, bias_one_sum]), everywhere),
            summed(early, everywhere),
        ]
    )
    qkv_bias = summed(spread_columns(qkv_bias), everywhere)
    rise_bias = summed(spread_columns(rise_bias[0]), everywhere)
    features = lax.dynamic_slice(features, (0, shard * thin), (6, thin))
    qkv_bias = lax.dynamic_index_in_dim(qkv_bias, core, 0, keepdims=False)
    qkv_bias = qkv_bias.reshape(ctx * heads, 3, HEAD_DIM)
    rise_bias = lax.dynamic_index_in_dim(rise_bias, core, 0, keepdims=False).reshape(-1)

    qkv_grad = qkv_grad.reshape(ctx, thin, heads, 3, HEAD_DIM).transpose(3, 1, 0, 2, 4)
    qkv_grad = qkv_grad.reshape(3, thin, ctx * heads * HEAD_DIM).astype(F32)
    return (
        both_sequences(own_out),
        both_sequences(own_grad),
        features[0],
        features[1],
        features[2],
        features[3],
        qkv_grad[0],
        qkv_bias[:, 0].reshape(-1),
        qkv_grad[1],
        qkv_grad[2],
        qkv_bias[:, 2].reshape(-1),
        out_grad.transpose(0, 2, 1).reshape(-1, thin).astype(F32),
        features[4],
        rise_grad.transpose(1, 0, 2).reshape(thin, -1).astype(F32),
        rise_bias,
        fall_grad.transpose(0, 2, 1).reshape(-1, thin).astype(F32),
        features[5],
    )


def solution(mesh):
    placed = (
        P("dp", "ctx", None),
        P("dp", "ctx", None),
        P(("dp", "ctx")),
        P(("dp", "ctx")),
        P(("dp", "ctx")),
        P(("dp", "ctx")),
        P(("dp", "ctx"), "tp"),
        P("tp"),
        P(("dp", "ctx"), "tp"),
        P(("dp", "ctx"), "tp"),
        P("tp"),
        P("tp", ("dp", "ctx")),
        P(("dp", "ctx")),
        P(("dp", "ctx"), "tp"),
        P("tp"),
        P("tp", ("dp", "ctx")),
        P(("dp", "ctx")),
    )
    return jax.shard_map(
        body,
        mesh=mesh,
        in_specs=placed,
        out_specs=(
            P("dp", "ctx", None),
            P("dp", "ctx", None),
            P(("dp", "ctx")),
            P(("dp", "ctx")),
            P(("dp", "ctx")),
            P(("dp", "ctx")),
            P(("dp", "ctx"), "tp"),
            P("tp"),
            P(("dp", "ctx"), "tp"),
            P(("dp", "ctx"), "tp"),
            P("tp"),
            P("tp", ("dp", "ctx")),
            P(("dp", "ctx")),
            P(("dp", "ctx"), "tp"),
            P("tp"),
            P("tp", ("dp", "ctx")),
            P(("dp", "ctx")),
        ),
        check_vma=False,
    )
```

```python
import functools

import jax
import jax.numpy as jnp
from jax import lax
from jax.experimental import pallas as pl
from jax.experimental.pallas import tpu as pltpu
from jax.sharding import PartitionSpec as P

HEAD_DIM = 128
EPSILON = 1e-05
NEGATIVE = -1e30
F32 = jnp.float32
BF16 = jnp.bfloat16
MESH = pl.DeviceIdType.MESH


def product(former, latter):
    return jnp.dot(former, latter, preferred_element_type=F32)


def inner(former, latter):
    return lax.dot_general(former, latter, (((0,), (0,)), ((), ())), preferred_element_type=F32)


def across(former, latter):
    return lax.dot_general(former, latter, (((1,), (1,)), ((), ())), preferred_element_type=F32)


def normalize(values):
    average = jnp.mean(values, axis=-1, keepdims=True)
    centred = values - average
    spread = lax.rsqrt(jnp.mean(centred * centred, axis=-1, keepdims=True) + EPSILON)
    return (centred * spread, spread)


def norm_back(gradient, normed, spread):
    first_mean = jnp.mean(gradient, axis=-1, keepdims=True)
    second_mean = jnp.mean(gradient * normed, axis=-1, keepdims=True)
    return spread * (gradient - first_mean - normed * second_mean)


def after(values, *earlier):
    return lax.optimization_barrier((values, earlier))[0]


def swap(value, axis, mask):
    size = lax.axis_size(axis)
    return lax.ppermute(value, axis, [(i, i ^ mask) for i in range(size)])


def bit_order(part):
    bits = list(range((lax.axis_size("ctx") - 1).bit_length()))
    return bits if part == 0 else bits[::-1]


def share(parts):
    found = {}
    for part in (0, 1):
        have = {0: parts[part]}
        for bit in bit_order(part):
            mask = 1 << bit
            have.update({r ^ mask: swap(have[r], "ctx", mask) for r in list(have)})
        found.update({(r, part): have[r] for r in have})
    return found


def total(partial):
    sums = []
    for part in (0, 1):
        have = {r: partial[(r, part)] for r in range(lax.axis_size("ctx"))}
        for bit in bit_order(part)[::-1]:
            mask = 1 << bit
            came = {r ^ mask: swap(have[r].astype(BF16), "ctx", mask) for r in have if r & mask}
            have = {r: have[r].astype(F32) + came[r].astype(F32) for r in came}
        sums.append(have[0])
    return jnp.concatenate(sums, axis=0)


def summed(values, axes):
    for axis in axes:
        mask = 1
        while mask < lax.axis_size(axis):
            values = values + swap(values, axis, mask)
            mask *= 2
    return values


def joined(blocks):
    return jnp.concatenate([blocks[key] for key in sorted(blocks)], axis=0)


def halves(rows):
    middle = rows.shape[0] // 2
    return (rows[:middle], rows[middle:])


def exchange(pieces):
    count = pieces.shape[0]
    here = lax.axis_index("ctx")
    result = pieces
    for mask in range(1, count):
        other = here ^ mask
        came = swap(lax.dynamic_index_in_dim(pieces, other, 0, keepdims=False), "ctx", mask)
        result = lax.dynamic_update_index_in_dim(result, came, other, 0)
    return result


def gather_weight(pieces):
    count, rows, columns = pieces.shape
    block = exchange(pieces).reshape(count * rows, columns)
    half = lax.all_gather(block, "dp", axis=0, tiled=True)
    return jnp.concatenate([half, swap(half, "tp", 1)], axis=1)


def weight_grad(former, latter):
    width = latter.shape[1] // 2
    theirs = inner(former, latter[:, width:]).astype(BF16)
    return (theirs, inner(former, latter[:, :width]))


def over_cores(theirs, ours):
    return (ours + swap(theirs, "tp", 1).astype(F32)).astype(BF16)


def over_dp(both):
    return lax.psum_scatter(both, "dp", scatter_dimension=0, tiled=True)


def to_shards(rows):
    count = lax.axis_size("ctx")
    return exchange(rows.reshape(count, rows.shape[0] // count, rows.shape[1]))


def rows_of(here, block, size):
    return pl.multiple_of(lax.bitwise_xor(here, block) * size, size)


class Links:
    def __init__(self, count, half):
        self.count, self.half = count, half
        self.bits = (count - 1).bit_length()
        self.pairs = [(i, part) for i in range(1, count) for part in (0, 1)]
        self.slot = {pair: n for n, pair in enumerate(self.pairs)}

    def block(self, i, part):
        if part == 0:
            return i
        return sum(((i >> b) & 1) << (self.bits - 1 - b) for b in range(self.bits))

    def top(self, i):
        return 1 << (i.bit_length() - 1)

    def near(self, i):
        return i ^ self.top(i)

    def given(self, i):
        return [j for j in range(self.count - 1, 0, -1) if self.near(j) == i]

    def far(self, i, part):
        mask = self.block(self.top(i), part)
        return {"ctx": lax.bitwise_xor(lax.axis_index("ctx"), mask)}

    def start_row(self, i, part):
        return (2 * self.block(i, part) + part) * self.half

    def rows(self, ref, i, part):
        return ref.at[pl.ds(self.start_row(i, part), self.half)]

    def greet(self, others=(), masks=None):
        barrier = pltpu.get_barrier_semaphore()
        masks = [1 << bit for bit in range(self.bits)] if masks is None else masks
        partners = [{"ctx": lax.bitwise_xor(lax.axis_index("ctx"), mask)} for mask in masks]
        partners += list(others)
        for partner in partners:
            pl.semaphore_signal(barrier, 1, device_id=partner, device_id_type=MESH)
        pl.semaphore_wait(barrier, len(partners))

    def sharing(self, own_ref, full_ref, send_sem, recv_sem):
        copies = {}
        for i, part in self.pairs:
            near = self.near(i)
            source = (
                own_ref.at[pl.ds(part * self.half, self.half)]
                if near == 0
                else self.rows(full_ref, near, part)
            )
            n = self.slot[(i, part)]
            copies[(i, part)] = pltpu.make_async_remote_copy(
                src_ref=source,
                dst_ref=self.rows(full_ref, i, part),
                send_sem=send_sem.at[n],
                recv_sem=recv_sem.at[n],
                device_id=self.far(i, part),
                device_id_type=MESH,
            )
        return copies

    def summing(self, send_ref, recv_ref, send_sem, recv_sem):
        copies = {}
        for i, part in self.pairs:
            n = self.slot[(i, part)]
            copies[(i, part)] = pltpu.make_async_remote_copy(
                src_ref=send_ref.at[n],
                dst_ref=recv_ref.at[n],
                send_sem=send_sem.at[n],
                recv_sem=recv_sem.at[n],
                device_id=self.far(i, part),
                device_id_type=MESH,
            )
        return copies

    def pass_on(self, copies, arrived, own=False):
        for i, part in self.pairs:
            if self.near(i) == arrived:
                copies[(i, part)].start()

    def loads(self, ref, buffer, i, sem, base):
        return [
            pltpu.make_async_copy(
                self.rows(ref, i, part),
                buffer.at[pl.ds(part * self.half, self.half)],
                sem.at[base + part],
            )
            for part in (0, 1)
        ]

    def terms(self, i, columns, width, kept_v, send_v):
        tile = min(256, width)

        def step(n, _):
            at = pl.ds(pl.multiple_of(n * tile, tile), tile)
            term = columns(at)
            for part in (0, 1):
                piece = term[part * self.half : (part + 1) * self.half]
                if i < self.count // 2:
                    kept_v[2 * i + part, :, at] = piece
                else:
                    send_v[self.slot[(i, part)], :, at] = piece.astype(BF16)
            return 0

        lax.fori_loop(0, width // tile, step, 0)

    def combine(self, copies, kept_ref, send_ref, recv_ref, result_ref, first, last):
        for i in range(first, last - 1, -1):
            for part in (0, 1):
                for j in self.given(i):
                    copies[(j, part)].wait_recv()
                chunk = min(32, self.half)

                def add(step, _, i=i, part=part):
                    at = pl.ds(pl.multiple_of(step * chunk, chunk), chunk)
                    value = kept_ref[2 * i + part, at, :]
                    for j in self.given(i):
                        value = value + recv_ref[self.slot[(j, part)], at, :].astype(F32)
                    if i == 0:
                        place = pl.ds(pl.multiple_of(part * self.half + step * chunk, chunk), chunk)
                        result_ref[place, :] = value
                    else:
                        send_ref[self.slot[(i, part)], at, :] = value.astype(BF16)
                    return 0

                lax.fori_loop(0, self.half // chunk, add, 0)
                if i:
                    copies[(i, part)].start()


def weight_grads(partner, rows_v, columns_v, theirs_v, came_v, result_ref, send_sem, recv_sem, store_sem):
    tile = 256
    width = rows_v.shape[1]
    own = columns_v.shape[1] // 2

    def place(m):
        return pl.ds(pl.multiple_of(m * tile, tile), tile)

    def swap_tile(m):
        return pltpu.make_async_remote_copy(
            src_ref=theirs_v.at[place(m)],
            dst_ref=came_v.at[place(m)],
            send_sem=send_sem.at[m],
            recv_sem=recv_sem.at[m],
            device_id=partner,
            device_id_type=MESH,
        )

    def store_tile(m):
        return pltpu.make_async_copy(came_v.at[place(m)], result_ref.at[place(m)], store_sem.at[m])

    def first(m, _):
        term = inner(rows_v[:, place(m)], columns_v[:, own : 2 * own])
        theirs_v[place(m), :] = term.astype(BF16)
        swap_tile(m).start()
        return 0

    def second(m, _):
        swap_tile(m).wait_recv()
        term = inner(rows_v[:, place(m)], columns_v[:, 0:own])
        came_v[place(m), :] = (term + came_v[place(m), :].astype(F32)).astype(BF16)
        store_tile(m).start()
        return 0

    def end(m, _):
        store_tile(m).wait()
        swap_tile(m).wait_send()
        return 0

    lax.fori_loop(0, width // tile, first, 0)
    lax.fori_loop(0, width // tile, second, 0)
    return lambda: lax.fori_loop(0, width // tile, end, 0)


def feed_forward_kernel(
    links,
    own_ref,
    grads_ref,
    both_ref,
    shift_ref,
    residual_ref,
    table_ref,
    full_ref,
    hid_ref,
    slope_ref,
    both_grad_ref,
    back_ref,
    branch_ref,
    vector_ref,
    bias_ref,
    fall_ref,
    rise_big,
    fall_big,
    rows_v,
    grads_v,
    hid_v,
    slope_v,
    kept_v,
    send_v,
    recv_v,
    theirs_v,
    came_v,
    load_sem,
    store_sem,
    pair_send,
    pair_recv,
    grad_send,
    grad_recv,
    grad_store,
    share_send,
    share_recv,
    sum_send,
    sum_recv,
):
    half, count = links.half, links.count
    width, hidden = own_ref.shape[1], hid_v.shape[1]
    length = 2 * half * count
    rise_v = rise_big.at[pl.ds(0, width), pl.ds(0, hidden)]
    fall_v = fall_big.at[pl.ds(0, width), pl.ds(0, hidden)]
    own_half = pl.ds(0, hidden // 2)
    other_half = pl.ds(hidden // 2, hidden // 2)
    partner = {"tp": 1 - lax.axis_index("tp")}
    links.greet([partner])
    swaps = [
        pltpu.make_async_remote_copy(
            src_ref=both_ref.at[:, pl.ds(n * (hidden // 2), hidden // 2)],
            dst_ref=target.at[:, other_half],
            send_sem=pair_send.at[n],
            recv_sem=pair_recv.at[n],
            device_id=partner,
            device_id_type=MESH,
        )
        for n, target in enumerate((fall_v, rise_v))
    ]
    for copy in swaps:
        copy.start()
    shares = links.sharing(own_ref, full_ref, share_send, share_recv)
    sums = links.summing(send_v, recv_v, sum_send, sum_recv)
    links.pass_on(shares, 0)
    keep = pltpu.make_async_copy(own_ref, full_ref.at[pl.ds(0, 2 * half)], load_sem.at[0])
    keep.start()
    first = pltpu.make_async_copy(own_ref, rows_v, load_sem.at[1])
    first.start()
    rise = pltpu.make_async_copy(both_ref.at[:, other_half], rise_v.at[:, own_half], load_sem.at[2])
    rise.start()
    fall = pltpu.make_async_copy(both_ref.at[:, own_half], fall_v.at[:, own_half], load_sem.at[3])
    fall.start()
    bias_ref[...] = jnp.zeros_like(bias_ref)

    grad_loads = links.loads(grads_ref, grads_v, 0, load_sem, 4)
    for copy in grad_loads:
        copy.start()
    stores = []
    tile = min(256, hidden)
    for i in range(count):
        if i == 0:
            first.wait()
            rise.wait()
            fall.wait()
            for copy in swaps:
                copy.wait_recv()
            keep_fall = pltpu.make_async_copy(fall_v, fall_ref, store_sem.at[4])
            keep_fall.start()
        else:
            for part in (0, 1):
                shares[(i, part)].wait_recv()
            links.pass_on(shares, i)
            row_loads = links.loads(full_ref, rows_v, i, load_sem, 8)
            for copy in row_loads:
                copy.start()
            for copy in row_loads:
                copy.wait()
        for copy in grad_loads + stores:
            copy.wait()

        def rise_step(step, _, i=i):
            at = pl.ds(pl.multiple_of(step * tile, tile), tile)
            pre = product(rows_v[...], rise_v[:, at]) + shift_ref[0:1, at]
            back = product(grads_v[...], fall_v[:, at])
            cumulative = 0.5 * (1.0 + lax.erf(pre * 0.7071067811865476))
            density = jnp.exp(-0.5 * pre * pre) * 0.3989422804014327
            hid_v[:, at] = (pre * cumulative).astype(BF16)
            slope = (back * (cumulative + pre * density)).astype(BF16)
            slope_v[:, at] = slope
            bias_ref[0:1, at] += jnp.sum(slope.astype(F32), axis=0, keepdims=True)
            return 0

        lax.fori_loop(0, hidden // tile, rise_step, 0)
        if i + 1 < count:
            grad_loads = links.loads(grads_ref, grads_v, i + 1, load_sem, 4)
            for copy in grad_loads:
                copy.start()
        stores = []
        for n, (buffer, ref) in enumerate(((hid_v, hid_ref), (slope_v, slope_ref))):
            for part in (0, 1):
                copy = pltpu.make_async_copy(
                    buffer.at[pl.ds(part * half, half)],
                    links.rows(ref, i, part),
                    store_sem.at[2 * n + part],
                )
                copy.start()
                stores.append(copy)

        links.terms(i, lambda at: across(slope_v[...], rise_v[at, :]), width, kept_v, send_v)
        if i >= count // 2:
            for part in (0, 1):
                sums[(i, part)].start()
    for copy in stores:
        copy.wait()
    keep.wait()
    keep_fall.wait()
    rows_big = rise_big.at[pl.ds(0, length), pl.ds(0, width)]
    columns_big = fall_big.at[pl.ds(0, length), pl.ds(0, hidden)]
    ends = []
    for n, (left, right) in enumerate(((full_ref, slope_ref), (grads_ref, hid_ref))):
        lefts = pltpu.make_async_copy(left, rows_big, load_sem.at[0])
        rights = pltpu.make_async_copy(right, columns_big, load_sem.at[1])
        lefts.start()
        rights.start()
        for end in ends:
            end()
        lefts.wait()
        rights.wait()
        ends = [
            weight_grads(
                partner,
                rows_big,
                columns_big,
                theirs_v,
                came_v.at[n],
                both_grad_ref.at[:, pl.ds((1 - n) * (hidden // 2), hidden // 2)],
                grad_send.at[n],
                grad_recv.at[n],
                grad_store.at[n],
            )
        ]
        if n == 0:
            links.combine(sums, kept_v, send_v, recv_v, None, count // 2 - 1, 1)
            finals = [
                pltpu.make_async_copy(
                    residual_ref.at[pl.ds(part * half, half)], kept_v.at[2 + part], load_sem.at[2 + part]
                )
                for part in (0, 1)
            ]
            finals.append(
                pltpu.make_async_copy(grads_ref.at[pl.ds(0, 2 * half)], rows_v, load_sem.at[4])
            )
            for copy in finals:
                copy.start()
    for copy in finals:
        copy.wait()
    vector_ref[...] = jnp.zeros_like(vector_ref)
    chunk = min(32, half)
    results = []
    for part in (0, 1):
        for j in links.given(0):
            sums[(j, part)].wait_recv()

        def last(step, _, part=part):
            at = pl.ds(pl.multiple_of(step * chunk, chunk), chunk)
            to = pl.ds(pl.multiple_of(part * half + step * chunk, chunk), chunk)
            second = kept_v[part, at, :]
            for j in links.given(0):
                second = second + recv_v[links.slot[(j, part)], at, :].astype(F32)
            normed, spread = normalize(kept_v[2 + part, at, :])
            incoming = rows_v[to, :].astype(F32)
            back = incoming + norm_back(second * table_ref[2:3, :], normed, spread)
            branch = back.astype(BF16)
            kept_v[part, at, :] = back
            rows_v[to, :] = branch
            for n, value in enumerate((second * normed, second, branch.astype(F32), incoming)):
                vector_ref[n : n + 1, :] += jnp.sum(value, axis=0, keepdims=True)
            return 0

        lax.fori_loop(0, half // chunk, last, 0)
        rows = pl.ds(part * half, half)
        for n, (source, target) in enumerate(
            ((kept_v.at[part], back_ref.at[rows]), (rows_v.at[rows], branch_ref.at[rows]))
        ):
            copy = pltpu.make_async_copy(source, target, load_sem.at[2 * part + n])
            copy.start()
            results.append(copy)
    for end in ends:
        end()
    for copy in results:
        copy.wait()
    for copy in swaps:
        copy.wait_send()
    for pair in links.pairs:
        shares[pair].wait_send()
        sums[pair].wait_send()


def feed_forward(own, grads, both_weights, shift, residual, table, count):
    rows, width = own.shape
    hidden = both_weights.shape[1]
    length = rows * count
    links = Links(count, rows // 2)
    half, copies = links.half, len(links.pairs)
    anywhere = pl.BlockSpec(memory_space=pl.ANY)
    inside = pl.BlockSpec(memory_space=pltpu.VMEM)
    dma = pltpu.SemaphoreType.DMA
    return pl.pallas_call(
        functools.partial(feed_forward_kernel, links),
        out_shape=(
            jax.ShapeDtypeStruct((length, width), BF16),
            jax.ShapeDtypeStruct((length, hidden), BF16),
            jax.ShapeDtypeStruct((length, hidden), BF16),
            jax.ShapeDtypeStruct((width, hidden), BF16),
            jax.ShapeDtypeStruct((rows, width), F32),
            jax.ShapeDtypeStruct((rows, width), BF16),
            jax.ShapeDtypeStruct((8, width), F32),
            jax.ShapeDtypeStruct((1, hidden), F32),
            jax.ShapeDtypeStruct((width, hidden), BF16),
        ),
        in_specs=[anywhere, anywhere, anywhere, inside, anywhere, inside],
        out_specs=(anywhere,) * 6 + (inside, inside, anywhere),
        scratch_shapes=[
            pltpu.VMEM((max(width, length), max(width, hidden)), BF16),
            pltpu.VMEM((max(width, length), hidden), BF16),
            pltpu.VMEM((rows, width), BF16),
            pltpu.VMEM((rows, width), BF16),
            pltpu.VMEM((rows, hidden), BF16),
            pltpu.VMEM((rows, hidden), BF16),
            pltpu.VMEM((count, half, width), F32),
            pltpu.VMEM((copies, half, width), BF16),
            pltpu.VMEM((copies, half, width), BF16),
            pltpu.VMEM((width, hidden // 2), BF16),
            pltpu.VMEM((2, width, hidden // 2), BF16),
            dma((10,)),
            dma((5,)),
            dma((2,)),
            dma((2,)),
            dma((2, width // 256)),
            dma((2, width // 256)),
            dma((2, width // 256)),
            dma((copies,)),
            dma((copies,)),
            dma((copies,)),
            dma((copies,)),
        ],
        compiler_params=pltpu.CompilerParams(
            collective_id=3, has_side_effects=True, vmem_limit_bytes=63 * 1024 * 1024
        ),
        cost_estimate=pl.CostEstimate(
            flops=10 * length * width * hidden,
            bytes_accessed=length * width * 8 + width * hidden * 4 + length * hidden * 4,
            transcendentals=length * hidden * 2,
        ),
        name="feed_forward",
    )(own, grads, both_weights, shift, residual, table)


def front_kernel(
    links,
    own_ref,
    pieces_ref,
    table_ref,
    normed_ref,
    block_ref,
    rows_v,
    normed_v,
    load_sem,
    store_sem,
    share_send,
    share_recv,
    piece_send,
    piece_recv,
):
    count, half = links.count, links.half
    size = 2 * half
    here = lax.axis_index("ctx")
    links.greet(masks=range(1, count))
    shares = links.sharing(own_ref, rows_v, share_send, share_recv)
    links.pass_on(shares, 0)
    pieces = [
        pltpu.make_async_remote_copy(
            src_ref=pieces_ref.at[lax.bitwise_xor(here, mask)],
            dst_ref=block_ref.at[here],
            send_sem=piece_send.at[mask - 1],
            recv_sem=piece_recv.at[mask - 1],
            device_id={"ctx": lax.bitwise_xor(here, mask)},
            device_id_type=MESH,
        )
        for mask in range(1, count)
    ]
    for copy in pieces:
        copy.start()
    kept = pltpu.make_async_copy(pieces_ref.at[here], block_ref.at[here], load_sem.at[0])
    kept.start()
    first = pltpu.make_async_copy(own_ref, rows_v.at[pl.ds(0, size)], load_sem.at[1])
    first.start()
    chunk = min(32, half)
    stores = []
    for i in range(count):
        if i == 0:
            first.wait()
        else:
            for part in (0, 1):
                shares[(i, part)].wait_recv()
            links.pass_on(shares, i)
        for part in (0, 1):
            base = links.start_row(i, part)

            def norm(step, _, base=base):
                at = pl.ds(pl.multiple_of(base + step * chunk, chunk), chunk)
                normed = normalize(rows_v[at, :].astype(F32))[0]
                normed_v[at, :] = (normed * table_ref[0:1, :] + table_ref[1:2, :]).astype(BF16)
                return 0

            lax.fori_loop(0, half // chunk, norm, 0)
            store = pltpu.make_async_copy(
                links.rows(normed_v, i, part), links.rows(normed_ref, i, part), store_sem.at[2 * i + part]
            )
            store.start()
            stores.append(store)
    kept.wait()
    for copy in stores:
        copy.wait()
    for copy in pieces:
        copy.wait()
    for pair in links.pairs:
        shares[pair].wait_send()


def front(own, pieces, table, count):
    rows, width = own.shape
    length = rows * count
    links = Links(count, rows // 2)
    copies = len(links.pairs)
    anywhere = pl.BlockSpec(memory_space=pl.ANY)
    dma = pltpu.SemaphoreType.DMA
    return pl.pallas_call(
        functools.partial(front_kernel, links),
        out_shape=(
            jax.ShapeDtypeStruct((length, width), BF16),
            jax.ShapeDtypeStruct(pieces.shape, BF16),
        ),
        in_specs=[anywhere, anywhere, pl.BlockSpec(memory_space=pltpu.VMEM)],
        out_specs=(anywhere, anywhere),
        scratch_shapes=[
            pltpu.VMEM((length, width), BF16),
            pltpu.VMEM((length, width), BF16),
            dma((2,)),
            dma((2 * count,)),
            dma((copies,)),
            dma((copies,)),
            dma((count - 1,)),
            dma((count - 1,)),
        ],
        compiler_params=pltpu.CompilerParams(
            collective_id=1, has_side_effects=True, vmem_limit_bytes=40 * 1024 * 1024
        ),
        cost_estimate=pl.CostEstimate(
            flops=20 * length * width, bytes_accessed=120000000, transcendentals=0
        ),
        name="front",
    )(own, pieces, table)


def attend_kernel(
    links,
    heads,
    rows_ref,
    weight_ref,
    shift_ref,
    grads_ref,
    own_ref,
    table_ref,
    qkv_ref,
    mixed_ref,
    log_ref,
    grads_full_ref,
    residual_ref,
    second_ref,
    whole_ref,
    rows_v,
    weight_v,
    qkv_v,
    mixed_v,
    scores_v,
    kept_v,
    send_v,
    recv_v,
    load_sem,
    store_sem,
    pair_send,
    pair_recv,
    share_send,
    share_recv,
    sum_send,
    sum_recv,
):
    count, half = links.count, links.half
    size = 2 * half
    here = lax.axis_index("ctx")
    partner = {"tp": 1 - lax.axis_index("tp")}
    narrow = weight_ref.shape[1]
    wide = heads * 3 * HEAD_DIM // 2
    links.greet([partner])
    theirs = pltpu.make_async_remote_copy(
        src_ref=weight_ref,
        dst_ref=weight_v.at[1],
        send_sem=pair_send.at[0],
        recv_sem=pair_recv.at[0],
        device_id=partner,
        device_id_type=MESH,
    )
    theirs.start()
    shares = links.sharing(grads_ref, grads_full_ref, share_send, share_recv)
    sums = links.summing(send_v, recv_v, sum_send, sum_recv)
    links.pass_on(shares, 0)
    ours = pltpu.make_async_copy(weight_ref, weight_v.at[0], load_sem.at[0])
    ours.start()
    keep = pltpu.make_async_copy(grads_ref, grads_full_ref.at[pl.ds(0, size)], load_sem.at[1])
    keep.start()

    def load(n):
        return pltpu.make_async_copy(
            rows_ref.at[pl.ds(n * size, size)], rows_v.at[n % 2], load_sem.at[2 + n % 2]
        )

    coming = load(0)
    coming.start()
    ours.wait()
    theirs.wait_recv()
    wholes = []
    for core in (0, 1):
        copy = pltpu.make_async_copy(weight_v.at[core], whole_ref.at[core], store_sem.at[core])
        copy.start()
        wholes.append(copy)
    tile = 256 if wide % 256 == 0 else HEAD_DIM
    for n in range(count):
        coming.wait()
        if n + 1 < count:
            coming = load(n + 1)
            coming.start()
        for core in (0, 1):

            def step(m, _, n=n, core=core):
                at = pl.ds(pl.multiple_of(m * tile, tile), tile)
                to = pl.ds(pl.multiple_of(core * wide + m * tile, tile), tile)
                value = product(rows_v[n % 2], weight_v[core, :, at]) + shift_ref[0:1, to]
                qkv_v[n * size : (n + 1) * size, to] = value.astype(BF16)
                return 0

            lax.fori_loop(0, wide // tile, step, 0)
    keep_qkv = pltpu.make_async_copy(qkv_v, qkv_ref, store_sem.at[2])
    keep_qkv.start()

    def one_head(head, _):
        @pl.when(head == heads // 2)
        def _():
            for i in range(1, (count + 1) // 2):
                for part in (0, 1):
                    shares[(i, part)].wait_recv()
                links.pass_on(shares, i)

        attend_forward_head(here, head, size, count, qkv_v, mixed_v, log_ref, scores_v)
        return 0

    lax.fori_loop(0, heads, one_head, 0)
    keep_mixed = pltpu.make_async_copy(mixed_v, mixed_ref, store_sem.at[3])
    keep_mixed.start()
    chip = heads * HEAD_DIM // 2
    for i in range(count - 1, -1, -1):

        def out_rows(core, i=i):
            at = slice(core * chip, (core + 1) * chip)
            first = [links.start_row(i, part) for part in (0, 1)]
            return jnp.concatenate([mixed_v[row : row + half, at] for row in first], axis=0)

        links.terms(
            i,
            lambda at: across(out_rows(0), weight_v[0, at, wide:narrow])
            + across(out_rows(1), weight_v[1, at, wide:narrow]),
            residual_ref.shape[1],
            kept_v,
            send_v,
        )
        if i >= count // 2:
            for part in (0, 1):
                sums[(i, part)].start()
    links.combine(sums, kept_v, send_v, recv_v, residual_ref, count // 2 - 1, 0)
    chunk = min(32, half)

    def norm(step, _):
        at = pl.ds(pl.multiple_of(step * chunk, chunk), chunk)
        residual = own_ref[at, :].astype(F32) + (residual_ref[at, :] + table_ref[4:5, :])
        residual_ref[at, :] = residual
        normed = normalize(residual)[0]
        second_ref[at, :] = (normed * table_ref[2:3, :] + table_ref[3:4, :]).astype(BF16)
        return 0

    lax.fori_loop(0, size // chunk, norm, 0)
    for i in range(1, count):
        for part in (0, 1):
            if i >= (count + 1) // 2:
                shares[(i, part)].wait_recv()
    for copy in wholes + [keep_qkv, keep_mixed, keep]:
        copy.wait()
    theirs.wait_send()
    for pair in links.pairs:
        sums[pair].wait_send()
        shares[pair].wait_send()


def attend_forward_head(here, head, size, blocks, qkv_v, mixed_v, log_ref, scores_v):
    scaling = HEAD_DIM ** (-0.5)
    behind = lax.broadcasted_iota(jnp.int32, (size, size), 1) <= lax.broadcasted_iota(
        jnp.int32, (size, size), 0
    )
    column = pl.multiple_of(head * (3 * HEAD_DIM), HEAD_DIM)
    query_at = pl.ds(column, HEAD_DIM)
    key_at = pl.ds(pl.multiple_of(column + HEAD_DIM, HEAD_DIM), HEAD_DIM)
    value_at = pl.ds(pl.multiple_of(column + 2 * HEAD_DIM, HEAD_DIM), HEAD_DIM)
    head_at = pl.ds(pl.multiple_of(head * HEAD_DIM, HEAD_DIM), HEAD_DIM)
    for i in range(blocks):
        at = pl.ds(rows_of(here, i, size), size)
        queries = qkv_v[at, query_at]
        highest = jnp.full((size, 1), NEGATIVE, F32)
        for j in range(i + 1):
            keys = qkv_v[pl.ds(rows_of(here, j, size), size), key_at]
            scores = across(queries, keys) * scaling
            if j == i:
                scores = jnp.where(behind, scores, NEGATIVE)
            scores_v[:, j * size : (j + 1) * size] = scores
            highest = jnp.maximum(highest, jnp.max(scores, axis=1, keepdims=True))
        row_total = jnp.zeros((size, 1), F32)
        mixed = jnp.zeros((size, HEAD_DIM), F32)
        for j in range(i + 1):
            exponent = jnp.exp(scores_v[:, j * size : (j + 1) * size] - highest)
            row_total = row_total + jnp.sum(exponent, axis=1, keepdims=True)
            values = qkv_v[pl.ds(rows_of(here, j, size), size), value_at]
            mixed = mixed + product(exponent.astype(BF16), values)
        mixed_v[at, head_at] = (mixed / row_total).astype(BF16)
        log_total = jnp.broadcast_to(highest + jnp.log(row_total), (size, HEAD_DIM))
        log_ref[head, :, at] = log_total.T[0:8, :]


def attend(rows, weight, shift, grads, own, table, heads, count):
    length, width = rows.shape
    size = length // count
    narrow = weight.shape[1]
    columns = heads * 3 * HEAD_DIM
    links = Links(count, size // 2)
    half, copies = links.half, len(links.pairs)
    pairs = heads * length * (length + size) // 2
    anywhere = pl.BlockSpec(memory_space=pl.ANY)
    inside = pl.BlockSpec(memory_space=pltpu.VMEM)
    dma = pltpu.SemaphoreType.DMA
    return pl.pallas_call(
        functools.partial(attend_kernel, links, heads),
        out_shape=(
            jax.ShapeDtypeStruct((length, columns), BF16),
            jax.ShapeDtypeStruct((length, heads * HEAD_DIM), BF16),
            jax.ShapeDtypeStruct((heads, 8, length), F32),
            jax.ShapeDtypeStruct((length, width), BF16),
            jax.ShapeDtypeStruct((size, width), F32),
            jax.ShapeDtypeStruct((size, width), BF16),
            jax.ShapeDtypeStruct((2, width, narrow), BF16),
        ),
        in_specs=[anywhere, anywhere, inside, anywhere, inside, inside],
        out_specs=(anywhere, anywhere, inside, anywhere, inside, inside, anywhere),
        scratch_shapes=[
            pltpu.VMEM((2, size, width), BF16),
            pltpu.VMEM((2, width, narrow), BF16),
            pltpu.VMEM((length, columns), BF16),
            pltpu.VMEM((length, heads * HEAD_DIM), BF16),
            pltpu.VMEM((size, length), F32),
            pltpu.VMEM((count, half, width), F32),
            pltpu.VMEM((copies, half, width), BF16),
            pltpu.VMEM((copies, half, width), BF16),
            dma((4,)),
            dma((4,)),
            dma((1,)),
            dma((1,)),
            dma((copies,)),
            dma((copies,)),
            dma((copies,)),
            dma((copies,)),
        ],
        compiler_params=pltpu.CompilerParams(
            collective_id=2, has_side_effects=True, vmem_limit_bytes=60 * 1024 * 1024
        ),
        cost_estimate=pl.CostEstimate(
            flops=pairs * HEAD_DIM * 8 + 2 * length * width * heads * HEAD_DIM * 4,
            bytes_accessed=length * width * 8,
            transcendentals=pairs,
        ),
        name="attend",
    )(rows, weight, shift, grads, own, table)


def attend_back_kernel(
    links,
    heads,
    own_ref,
    weight_ref,
    qkv_ref,
    mixed_ref,
    log_ref,
    hid_ref,
    fall_ref,
    first_ref,
    full_ref,
    result_ref,
    sum_ref,
    head_grad_ref,
    weight_v,
    qkv_v,
    mixed_v,
    big_v,
    theirs_v,
    came_v,
    grad_v,
    rows_v,
    hid_v,
    fall_v,
    key_v,
    value_v,
    kept_v,
    send_v,
    recv_v,
    load_sem,
    grad_send,
    grad_recv,
    grad_store,
    share_send,
    share_recv,
    sum_send,
    sum_recv,
):
    half, count = links.half, links.count
    size = 2 * half
    here = lax.axis_index("ctx")
    chip = weight_v.shape[2]
    wide = heads * 3 * HEAD_DIM // 2
    partner = {"tp": 1 - lax.axis_index("tp")}
    links.greet([partner])
    shares = links.sharing(own_ref, full_ref, share_send, share_recv)
    sums = links.summing(send_v, recv_v, sum_send, sum_recv)
    links.pass_on(shares, 0)
    narrow = fall_v.shape[0]
    loads = [
        pltpu.make_async_copy(source, target, load_sem.at[n])
        for n, (source, target) in enumerate(
            (
                (fall_ref.at[pl.ds(0, narrow)], fall_v),
                (own_ref, rows_v),
                (weight_ref.at[:, :, pl.ds(weight_ref.shape[2] - chip, chip)], weight_v),
                (qkv_ref, qkv_v),
                (mixed_ref, mixed_v),
                (own_ref, full_ref.at[pl.ds(0, size)]),
                (first_ref, big_v),
            )
        )
    ]
    for copy in loads:
        copy.start()
    loads[0].wait()
    out_terms(links, hid_ref, hid_v, fall_v, kept_v, send_v, load_sem, 7)
    for i in range(count):
        if i == 0:
            loads[1].wait()
            loads[2].wait()
        else:
            for part in (0, 1):
                shares[(i, part)].wait_recv()
            links.pass_on(shares, i)
            unit_loads = links.loads(full_ref, rows_v, i, load_sem, 7)
            for copy in unit_loads:
                copy.start()
            for copy in unit_loads:
                copy.wait()
        for core in (0, 1):
            term = product(rows_v[...], weight_v[core]).astype(BF16)
            for part in (0, 1):
                first = links.start_row(i, part)
                grad_v[first : first + half, core * chip : (core + 1) * chip] = term[
                    part * half : (part + 1) * half
                ]
    for i in range(count - 1, count // 2 - 1, -1):
        for part in (0, 1):
            sums[(i, part)].start()
    loads[3].wait()
    loads[4].wait()

    def one_head(head, _):
        @pl.when(head == heads // 2)
        def _():
            links.combine(sums, kept_v, send_v, recv_v, None, count // 2 - 1, 1)

        attend_backward_head(
            here, head, size, count, qkv_v, grad_v, mixed_v, log_ref, result_ref, key_v, value_v
        )
        return 0

    lax.fori_loop(0, heads, one_head, 0)
    loads[5].wait()
    loads[6].wait()
    end_first = weight_grads(
        partner,
        big_v,
        result_ref,
        theirs_v.at[:, pl.ds(0, wide)],
        came_v.at[:, pl.ds(0, wide)],
        head_grad_ref.at[:, pl.ds(0, wide)],
        grad_send.at[0],
        grad_recv.at[0],
        grad_store.at[0],
    )
    again = pltpu.make_async_copy(full_ref, big_v, load_sem.at[6])
    again.start()
    links.combine(sums, kept_v, send_v, recv_v, sum_ref, 0, 0)
    again.wait()
    end_second = weight_grads(
        partner,
        big_v,
        mixed_v,
        theirs_v.at[:, pl.ds(wide, chip)],
        came_v.at[:, pl.ds(wide, chip)],
        head_grad_ref.at[:, pl.ds(wide, chip)],
        grad_send.at[1],
        grad_recv.at[1],
        grad_store.at[1],
    )
    end_first()
    end_second()
    for pair in links.pairs:
        sums[pair].wait_send()
        shares[pair].wait_send()


def out_terms(links, hid_ref, hid_v, fall_v, kept_v, send_v, load_sem, base):
    count, half = links.count, links.half
    order = list(range(count - 1, -1, -1))
    unit_loads = links.loads(hid_ref, hid_v.at[0], order[0], load_sem, base)
    for copy in unit_loads:
        copy.start()
    for n, i in enumerate(order):
        for copy in unit_loads:
            copy.wait()
        if n + 1 < count:
            unit_loads = links.loads(
                hid_ref, hid_v.at[(n + 1) % 2], order[n + 1], load_sem, base + 2 * ((n + 1) % 2)
            )
            for copy in unit_loads:
                copy.start()
        links.terms(
            i, lambda at, n=n: across(hid_v[n % 2], fall_v[at, :]), fall_v.shape[0], kept_v, send_v
        )


def attend_backward_head(
    here, head, size, blocks, qkv_v, grad_v, mixed_v, log_ref, result_ref, key_v, value_v
):
    scaling = HEAD_DIM ** (-0.5)
    behind = lax.broadcasted_iota(jnp.int32, (size, size), 0) <= lax.broadcasted_iota(
        jnp.int32, (size, size), 1
    )
    column = pl.multiple_of(head * (3 * HEAD_DIM), HEAD_DIM)
    query_at = pl.ds(column, HEAD_DIM)
    key_at = pl.ds(pl.multiple_of(column + HEAD_DIM, HEAD_DIM), HEAD_DIM)
    value_at = pl.ds(pl.multiple_of(column + 2 * HEAD_DIM, HEAD_DIM), HEAD_DIM)
    head_at = pl.ds(pl.multiple_of(head * HEAD_DIM, HEAD_DIM), HEAD_DIM)
    for i in range(blocks):
        at = pl.ds(rows_of(here, i, size), size)
        queries = qkv_v[at, query_at]
        grads = grad_v[at, head_at]
        both = grads.astype(F32) * mixed_v[at, head_at].astype(F32)
        centre = jnp.sum(both.T, axis=0, keepdims=True)
        log_total = log_ref[head, 0:1, at]
        query_grad = jnp.zeros((size, HEAD_DIM), F32)
        for j in range(i + 1):
            there = pl.ds(rows_of(here, j, size), size)
            keys = qkv_v[there, key_at]
            values = qkv_v[there, value_at]
            weights = jnp.exp(across(keys, queries) * scaling - log_total)
            if j == i:
                weights = jnp.where(behind, weights, 0.0)
            slopes = (weights * (across(values, grads) - centre)).astype(BF16)
            value_term = product(weights.astype(BF16), grads)
            key_term = product(slopes, queries)
            query_grad = query_grad + inner(slopes, keys)
            place = slice(j * size, (j + 1) * size)
            if i == j:
                value_v[place, :] = value_term
                key_v[place, :] = key_term
            else:
                value_v[place, :] += value_term
                key_v[place, :] += key_term
        result_ref[at, query_at] = (query_grad * scaling).astype(BF16)
    for j in range(blocks):
        there = pl.ds(rows_of(here, j, size), size)
        place = slice(j * size, (j + 1) * size)
        result_ref[there, key_at] = (key_v[place, :] * scaling).astype(BF16)
        result_ref[there, value_at] = value_v[place, :].astype(BF16)


def attend_back(own, weight, qkv, mixed, log_total, hid, fall_weight, first, count):
    rows, width = own.shape
    length, columns = qkv.shape
    heads = columns // (3 * HEAD_DIM)
    hidden = hid.shape[1]
    links = Links(count, rows // 2)
    half, copies = links.half, len(links.pairs)
    narrow = width // 2
    pairs = heads * length * (length + rows) // 2
    anywhere = pl.BlockSpec(memory_space=pl.ANY)
    inside = pl.BlockSpec(memory_space=pltpu.VMEM)
    dma = pltpu.SemaphoreType.DMA
    return pl.pallas_call(
        functools.partial(attend_back_kernel, links, heads),
        out_shape=(
            jax.ShapeDtypeStruct((length, width), BF16),
            jax.ShapeDtypeStruct((length, columns), BF16),
            jax.ShapeDtypeStruct((rows, narrow), F32),
            jax.ShapeDtypeStruct((width, 2 * heads * HEAD_DIM), BF16),
        ),
        in_specs=[anywhere] * 4 + [inside, anywhere, anywhere, anywhere],
        out_specs=(anywhere, inside, inside, anywhere),
        scratch_shapes=[
            pltpu.VMEM((2, width, heads * HEAD_DIM // 2), BF16),
            pltpu.VMEM(qkv.shape, BF16),
            pltpu.VMEM(mixed.shape, BF16),
            pltpu.VMEM((length, width), BF16),
            pltpu.VMEM((width, 2 * heads * HEAD_DIM), BF16),
            pltpu.VMEM((width, 2 * heads * HEAD_DIM), BF16),
            pltpu.VMEM(mixed.shape, BF16),
            pltpu.VMEM((rows, width), BF16),
            pltpu.VMEM((2, rows, hidden), BF16),
            pltpu.VMEM((narrow, hidden), BF16),
            pltpu.VMEM((length, HEAD_DIM), F32),
            pltpu.VMEM((length, HEAD_DIM), F32),
            pltpu.VMEM((count, half, narrow), F32),
            pltpu.VMEM((copies, half, narrow), BF16),
            pltpu.VMEM((copies, half, narrow), BF16),
            dma((11,)),
            dma((2, width // 256)),
            dma((2, width // 256)),
            dma((2, width // 256)),
            dma((copies,)),
            dma((copies,)),
            dma((copies,)),
            dma((copies,)),
        ],
        compiler_params=pltpu.CompilerParams(
            collective_id=4, has_side_effects=True, vmem_limit_bytes=63 * 1024 * 1024
        ),
        cost_estimate=pl.CostEstimate(
            flops=pairs * HEAD_DIM * 20 + 2 * length * width * (heads * HEAD_DIM + hidden // 2),
            bytes_accessed=length * width * 6 + length * columns * 4 + length * hidden * 2,
            transcendentals=pairs,
        ),
        name="attend_back",
    )(own, weight, qkv, mixed, log_total, hid, fall_weight, first)


def first_back_kernel(
    links,
    grads_ref,
    weight_ref,
    hid_ref,
    fall_ref,
    first_ref,
    sum_ref,
    grads_v,
    weight_v,
    hid_v,
    fall_v,
    kept_v,
    send_v,
    recv_v,
    kept_w,
    send_w,
    recv_w,
    load_sem,
    sum_send,
    sum_recv,
    late_send,
    late_recv,
):
    count, half = links.count, links.half
    wide = weight_v.shape[2]
    links.greet()
    sums = links.summing(send_v, recv_v, sum_send, sum_recv)
    lates = links.summing(send_w, recv_w, late_send, late_recv)
    narrow = fall_v.shape[0]
    loads = [
        pltpu.make_async_copy(source, target, load_sem.at[n])
        for n, (source, target) in enumerate(
            (
                (weight_ref.at[:, :, pl.ds(0, wide)], weight_v),
                (fall_ref.at[pl.ds(fall_ref.shape[0] - narrow, narrow)], fall_v),
            )
        )
    ]
    for copy in loads:
        copy.start()
    order = list(range(count - 1, -1, -1))
    unit_loads = links.loads(grads_ref, grads_v.at[0], order[0], load_sem, 2)
    for copy in unit_loads:
        copy.start()
    loads[0].wait()
    for n, i in enumerate(order):
        for copy in unit_loads:
            copy.wait()
        if n + 1 < count:
            unit_loads = links.loads(
                grads_ref, grads_v.at[(n + 1) % 2], order[n + 1], load_sem, 2 + 2 * ((n + 1) % 2)
            )
            for copy in unit_loads:
                copy.start()
        links.terms(
            i,
            lambda at, n=n: across(grads_v[n % 2, :, :wide], weight_v[0, at, :])
            + across(grads_v[n % 2, :, wide:], weight_v[1, at, :]),
            weight_v.shape[1],
            kept_v,
            send_v,
        )
        if i >= count // 2:
            for part in (0, 1):
                sums[(i, part)].start()
    loads[1].wait()
    out_terms(links, hid_ref, hid_v, fall_v, kept_w, send_w, load_sem, 6)
    links.combine(sums, kept_v, send_v, recv_v, None, count // 2 - 1, 1)
    for i in range(count - 1, count // 2 - 1, -1):
        for part in (0, 1):
            lates[(i, part)].start()
    links.combine(sums, kept_v, send_v, recv_v, first_ref, 0, 0)
    links.combine(lates, kept_w, send_w, recv_w, sum_ref, count // 2 - 1, 0)
    for pair in links.pairs:
        sums[pair].wait_send()
        lates[pair].wait_send()


def first_back(grads, weight, hid, fall_weight, count):
    length, columns = grads.shape
    width, hidden = fall_weight.shape
    rows = length // count
    links = Links(count, rows // 2)
    half, copies = links.half, len(links.pairs)
    narrow = width // 2
    anywhere = pl.BlockSpec(memory_space=pl.ANY)
    inside = pl.BlockSpec(memory_space=pltpu.VMEM)
    dma = pltpu.SemaphoreType.DMA
    return pl.pallas_call(
        functools.partial(first_back_kernel, links),
        out_shape=(
            jax.ShapeDtypeStruct((rows, width), F32),
            jax.ShapeDtypeStruct((rows, narrow), F32),
        ),
        in_specs=[anywhere] * 4,
        out_specs=(inside, inside),
        scratch_shapes=[
            pltpu.VMEM((2, rows, columns), BF16),
            pltpu.VMEM((2, width, columns // 2), BF16),
            pltpu.VMEM((2, rows, hidden), BF16),
            pltpu.VMEM((narrow, hidden), BF16),
            pltpu.VMEM((count, half, width), F32),
            pltpu.VMEM((copies, half, width), BF16),
            pltpu.VMEM((copies, half, width), BF16),
            pltpu.VMEM((count, half, narrow), F32),
            pltpu.VMEM((copies, half, narrow), BF16),
            pltpu.VMEM((copies, half, narrow), BF16),
            dma((10,)),
            dma((copies,)),
            dma((copies,)),
            dma((copies,)),
            dma((copies,)),
        ],
        compiler_params=pltpu.CompilerParams(
            collective_id=5, has_side_effects=True, vmem_limit_bytes=58 * 1024 * 1024
        ),
        cost_estimate=pl.CostEstimate(
            flops=2 * length * width * (columns + hidden // 2),
            bytes_accessed=length * columns * 2 + length * hidden * 2 + width * (columns + hidden) * 2,
            transcendentals=0,
        ),
        name="first_back",
    )(grads, weight, hid, fall_weight)


def body(
    tokens,
    cotangent,
    attention_gain,
    attention_bias,
    feedforward_gain,
    feedforward_bias,
    query_weight,
    query_bias,
    key_weight,
    value_weight,
    value_bias,
    output_weight,
    output_bias,
    up_weight,
    up_bias,
    down_weight,
    down_bias,
):
    _, local_rows, model_width = tokens.shape
    ctx, dp = lax.axis_size("ctx"), lax.axis_size("dp")
    here, core = lax.axis_index("ctx"), lax.axis_index("tp")
    shard = lax.axis_index("dp") * ctx + here
    thin = query_weight.shape[0]
    heads = query_weight.shape[1] // (HEAD_DIM * ctx)
    hidden = up_weight.shape[1] // ctx
    inputs = lax.dynamic_index_in_dim(tokens, core, 0, keepdims=False)
    incoming = lax.dynamic_index_in_dim(cotangent, core, 0, keepdims=False)

    packed = jnp.stack(
        [w.reshape(thin, ctx, heads, HEAD_DIM) for w in (query_weight, key_weight, value_weight)],
        axis=3,
    ).reshape(thin, ctx, heads * 3 * HEAD_DIM)
    head_pieces = jnp.concatenate(
        [
            packed.transpose(1, 0, 2),
            output_weight.reshape(ctx, heads * HEAD_DIM, thin).transpose(0, 2, 1),
        ],
        axis=2,
    )
    hidden_pieces = jnp.concatenate(
        [
            down_weight.reshape(ctx, hidden, thin).transpose(0, 2, 1),
            up_weight.reshape(thin, ctx, hidden).transpose(1, 0, 2),
        ],
        axis=2,
    )
    head_block = exchange(head_pieces).reshape(ctx * thin, -1)
    head_weights = lax.all_gather(head_block, "dp", axis=0, tiled=True)

    small = jnp.stack(
        [attention_gain, attention_bias, feedforward_gain, feedforward_bias, output_bias, down_bias]
    ).astype(F32)
    small = jnp.concatenate([small, jnp.zeros((2, thin), F32)])
    table = jnp.zeros((8, model_width), F32)
    table = lax.dynamic_update_slice(table, small, (0, shard * thin))
    table = summed(table, ("dp", "ctx"))
    gain_one, shift_one, gain_two, shift_two, output_shift, down_shift = [
        table[n : n + 1] for n in range(6)
    ]

    def own_columns(vector):
        return lax.dynamic_index_in_dim(vector.reshape(ctx, -1), here, 0, keepdims=False)

    query_shift = own_columns(query_bias).reshape(heads, HEAD_DIM)
    value_shift = own_columns(value_bias).reshape(heads, HEAD_DIM)
    qkv_shift = jnp.stack([query_shift, jnp.zeros_like(query_shift), value_shift], axis=1)
    shifts = jnp.concatenate([qkv_shift.reshape(-1), own_columns(up_bias)])
    other_shifts = swap(shifts, "tp", 1)
    wide = heads * 3 * HEAD_DIM
    qkv_shift = jnp.concatenate([shifts[:wide], other_shifts[:wide]]).astype(F32)
    rise_shift = jnp.concatenate([shifts[wide:], other_shifts[wide:]]).astype(F32)

    wide_inputs = inputs.astype(F32)
    normed_one, spread_one = normalize(wide_inputs)
    ones, hidden_block = front(after(inputs, head_block), hidden_pieces, table, ctx)
    hidden_weights = lax.all_gather(
        hidden_block.reshape(ctx * thin, -1), "dp", axis=0, tiled=True
    )
    qkv, mixed, log_total, grads_in, residual, input_two, head_whole = attend(
        ones, head_weights, qkv_shift[None], incoming, inputs, table, 2 * heads, ctx
    )
    _, all_hid, _, hidden_both, residual_grad, branch_grad, vectors, rise_bias, fall_weight = (
        feed_forward(input_two, grads_in, hidden_weights, rise_shift[None], residual, table, ctx)
    )
    hidden_rows = over_dp(hidden_both)

    _, qkv_grads, low_columns, head_both = attend_back(
        branch_grad, head_whole, qkv, mixed, log_total, all_hid, fall_weight, ones, ctx
    )
    qkv_bias = jnp.sum(qkv_grads.astype(F32), axis=0)
    head_both = after(head_both, hidden_rows)
    late_grads = after(qkv_grads, head_both)
    first_grad, high_columns = first_back(late_grads, head_whole, all_hid, fall_weight, ctx)
    block_out = residual + (jnp.concatenate([low_columns, high_columns], axis=1) + down_shift)
    own_out = block_out.astype(BF16)
    late_both = head_both
    width = hidden
    hidden_grad = to_shards(hidden_rows)
    fall_grad, rise_grad = hidden_grad[:, :, :width], hidden_grad[:, :, width:]
    late_grad = to_shards(over_dp(late_both))
    qkv_grad, out_grad = late_grad[:, :, :wide], late_grad[:, :, wide:]
    gain_one_sum = jnp.sum(first_grad * normed_one, axis=0)
    bias_one_sum = jnp.sum(first_grad, axis=0)
    token_grad = residual_grad + norm_back(first_grad * gain_one, normed_one, spread_one)
    own_grad = token_grad.astype(BF16)

    def both_sequences(own):
        other = swap(own, "tp", 1)
        first = core == 0
        return jnp.stack([jnp.where(first, own, other), jnp.where(first, other, own)])

    def spread_columns(vector):
        own, other = jnp.split(vector, 2)
        whole = jnp.zeros((2, ctx, own.shape[0]), F32)
        whole = lax.dynamic_update_slice(whole, own[None, None], (core, here, 0))
        return lax.dynamic_update_slice(whole, other[None, None], (1 - core, here, 0))

    everywhere = ("tp", "ctx", "dp")
    early = vectors[:4]
    features = jnp.concatenate(
        [
            summed(jnp.stack([gain_one_sum, bias_one_sum]), everywhere),
            summed(early, everywhere),
        ]
    )
    qkv_bias = summed(spread_columns(qkv_bias), everywhere)
    rise_bias = summed(spread_columns(rise_bias[0]), everywhere)
    features = lax.dynamic_slice(features, (0, shard * thin), (6, thin))
    qkv_bias = lax.dynamic_index_in_dim(qkv_bias, core, 0, keepdims=False)
    qkv_bias = qkv_bias.reshape(ctx * heads, 3, HEAD_DIM)
    rise_bias = lax.dynamic_index_in_dim(rise_bias, core, 0, keepdims=False).reshape(-1)

    qkv_grad = qkv_grad.reshape(ctx, thin, heads, 3, HEAD_DIM).transpose(3, 1, 0, 2, 4)
    qkv_grad = qkv_grad.reshape(3, thin, ctx * heads * HEAD_DIM).astype(F32)
    return (
        both_sequences(own_out),
        both_sequences(own_grad),
        features[0],
        features[1],
        features[2],
        features[3],
        qkv_grad[0],
        qkv_bias[:, 0].reshape(-1),
        qkv_grad[1],
        qkv_grad[2],
        qkv_bias[:, 2].reshape(-1),
        out_grad.transpose(0, 2, 1).reshape(-1, thin).astype(F32),
        features[4],
        rise_grad.transpose(1, 0, 2).reshape(thin, -1).astype(F32),
        rise_bias,
        fall_grad.transpose(0, 2, 1).reshape(-1, thin).astype(F32),
        features[5],
    )


def solution(mesh):
    placed = (
        P("dp", "ctx", None),
        P("dp", "ctx", None),
        P(("dp", "ctx")),
        P(("dp", "ctx")),
        P(("dp", "ctx")),
        P(("dp", "ctx")),
        P(("dp", "ctx"), "tp"),
        P("tp"),
        P(("dp", "ctx"), "tp"),
        P(("dp", "ctx"), "tp"),
        P("tp"),
        P("tp", ("dp", "ctx")),
        P(("dp", "ctx")),
        P(("dp", "ctx"), "tp"),
        P("tp"),
        P("tp", ("dp", "ctx")),
        P(("dp", "ctx")),
    )
    return jax.shard_map(
        body,
        mesh=mesh,
        in_specs=placed,
        out_specs=(
            P("dp", "ctx", None),
            P("dp", "ctx", None),
            P(("dp", "ctx")),
            P(("dp", "ctx")),
            P(("dp", "ctx")),
            P(("dp", "ctx")),
            P(("dp", "ctx"), "tp"),
            P("tp"),
            P(("dp", "ctx"), "tp"),
            P(("dp", "ctx"), "tp"),
            P("tp"),
            P("tp", ("dp", "ctx")),
            P(("dp", "ctx")),
            P(("dp", "ctx"), "tp"),
            P("tp"),
            P("tp", ("dp", "ctx")),
            P(("dp", "ctx")),
        ),
        check_vma=False,
    )
```

```python
import functools

import jax
import jax.numpy as jnp
from jax import lax
from jax.experimental import pallas as pl
from jax.experimental.pallas import tpu as pltpu
from jax.sharding import PartitionSpec as P

HEAD_DIM = 128
EPSILON = 1e-05
NEGATIVE = -1e30
F32 = jnp.float32
BF16 = jnp.bfloat16
MESH = pl.DeviceIdType.MESH


def product(former, latter):
    return jnp.dot(former, latter, preferred_element_type=F32)


def inner(former, latter):
    return lax.dot_general(former, latter, (((0,), (0,)), ((), ())), preferred_element_type=F32)


def across(former, latter):
    return lax.dot_general(former, latter, (((1,), (1,)), ((), ())), preferred_element_type=F32)


def normalize(values):
    average = jnp.mean(values, axis=-1, keepdims=True)
    centred = values - average
    spread = lax.rsqrt(jnp.mean(centred * centred, axis=-1, keepdims=True) + EPSILON)
    return (centred * spread, spread)


def norm_back(gradient, normed, spread):
    first_mean = jnp.mean(gradient, axis=-1, keepdims=True)
    second_mean = jnp.mean(gradient * normed, axis=-1, keepdims=True)
    return spread * (gradient - first_mean - normed * second_mean)


def swap(value, axis, mask):
    size = lax.axis_size(axis)
    return lax.ppermute(value, axis, [(i, i ^ mask) for i in range(size)])


def over_dp(both):
    return lax.psum_scatter(both, "dp", scatter_dimension=0, tiled=True)


def rows_of(here, block, size):
    return pl.multiple_of(lax.bitwise_xor(here, block) * size, size)


class Links:
    def __init__(self, count, half):
        self.count, self.half = count, half
        self.bits = (count - 1).bit_length()
        self.pairs = [(i, part) for i in range(1, count) for part in (0, 1)]
        self.slot = {pair: n for n, pair in enumerate(self.pairs)}

    def block(self, i, part):
        if part == 0:
            return i
        return sum(((i >> b) & 1) << (self.bits - 1 - b) for b in range(self.bits))

    def top(self, i):
        return 1 << (i.bit_length() - 1)

    def near(self, i):
        return i ^ self.top(i)

    def given(self, i):
        return [j for j in range(self.count - 1, 0, -1) if self.near(j) == i]

    def far(self, i, part):
        mask = self.block(self.top(i), part)
        return {"ctx": lax.bitwise_xor(lax.axis_index("ctx"), mask)}

    def start_row(self, i, part):
        return (2 * self.block(i, part) + part) * self.half

    def rows(self, ref, i, part):
        return ref.at[pl.ds(self.start_row(i, part), self.half)]

    def greet(self, others=(), masks=None):
        barrier = pltpu.get_barrier_semaphore()
        masks = [1 << bit for bit in range(self.bits)] if masks is None else masks
        partners = [{"ctx": lax.bitwise_xor(lax.axis_index("ctx"), mask)} for mask in masks]
        partners += list(others)
        for partner in partners:
            pl.semaphore_signal(barrier, 1, device_id=partner, device_id_type=MESH)
        pl.semaphore_wait(barrier, len(partners))

    def sharing(self, own_ref, full_ref, send_sem, recv_sem):
        copies = {}
        for i, part in self.pairs:
            near = self.near(i)
            source = (
                own_ref.at[pl.ds(part * self.half, self.half)]
                if near == 0
                else self.rows(full_ref, near, part)
            )
            n = self.slot[(i, part)]
            copies[(i, part)] = pltpu.make_async_remote_copy(
                src_ref=source,
                dst_ref=self.rows(full_ref, i, part),
                send_sem=send_sem.at[n],
                recv_sem=recv_sem.at[n],
                device_id=self.far(i, part),
                device_id_type=MESH,
            )
        return copies

    def summing(self, send_ref, recv_ref, send_sem, recv_sem):
        copies = {}
        for i, part in self.pairs:
            n = self.slot[(i, part)]
            copies[(i, part)] = pltpu.make_async_remote_copy(
                src_ref=send_ref.at[n],
                dst_ref=recv_ref.at[n],
                send_sem=send_sem.at[n],
                recv_sem=recv_sem.at[n],
                device_id=self.far(i, part),
                device_id_type=MESH,
            )
        return copies

    def pass_on(self, copies, arrived, own=False):
        for i, part in self.pairs:
            if self.near(i) == arrived:
                copies[(i, part)].start()

    def loads(self, ref, buffer, i, sem, base):
        return [
            pltpu.make_async_copy(
                self.rows(ref, i, part),
                buffer.at[pl.ds(part * self.half, self.half)],
                sem.at[base + part],
            )
            for part in (0, 1)
        ]

    def terms(self, i, columns, width, kept_v, send_v):
        tile = min(256, width)

        def step(n, _):
            at = pl.ds(pl.multiple_of(n * tile, tile), tile)
            term = columns(at)
            for part in (0, 1):
                piece = term[part * self.half : (part + 1) * self.half]
                if i < self.count // 2:
                    kept_v[2 * i + part, :, at] = piece
                else:
                    send_v[self.slot[(i, part)], :, at] = piece.astype(BF16)
            return 0

        lax.fori_loop(0, width // tile, step, 0)

    def combine(self, copies, kept_ref, send_ref, recv_ref, first, last, final=None, then=None):
        for i in range(first, last - 1, -1):
            for part in (0, 1):
                for j in self.given(i):
                    copies[(j, part)].wait_recv()
                chunk = min(32, self.half)

                def add(step, _, i=i, part=part):
                    at = pl.ds(pl.multiple_of(step * chunk, chunk), chunk)
                    value = kept_ref[2 * i + part, at, :]
                    for j in self.given(i):
                        value = value + recv_ref[self.slot[(j, part)], at, :].astype(F32)
                    if i == 0:
                        to = pl.ds(pl.multiple_of(part * self.half + step * chunk, chunk), chunk)
                        final(part, at, to, value)
                    else:
                        send_ref[self.slot[(i, part)], at, :] = value.astype(BF16)
                    return 0

                lax.fori_loop(0, self.half // chunk, add, 0)
                if i:
                    copies[(i, part)].start()
                elif then:
                    then(part)


def weight_grads(partner, rows_v, columns_v, theirs_v, came_v, result_ref, send_sem, recv_sem, store_sem):
    tile = 256
    width = rows_v.shape[1]
    own = columns_v.shape[1] // 2

    def place(m):
        return pl.ds(pl.multiple_of(m * tile, tile), tile)

    def swap_tile(m):
        return pltpu.make_async_remote_copy(
            src_ref=theirs_v.at[place(m)],
            dst_ref=came_v.at[place(m)],
            send_sem=send_sem.at[m],
            recv_sem=recv_sem.at[m],
            device_id=partner,
            device_id_type=MESH,
        )

    def store_tile(m):
        return pltpu.make_async_copy(came_v.at[place(m)], result_ref.at[place(m)], store_sem.at[m])

    def first(m, _):
        term = inner(rows_v[:, place(m)], columns_v[:, own : 2 * own])
        theirs_v[place(m), :] = term.astype(BF16)
        swap_tile(m).start()
        return 0

    def second(m, _):
        swap_tile(m).wait_recv()
        term = inner(rows_v[:, place(m)], columns_v[:, 0:own])
        came_v[place(m), :] = (term + came_v[place(m), :].astype(F32)).astype(BF16)
        store_tile(m).start()
        return 0

    def end(m, _):
        store_tile(m).wait()
        swap_tile(m).wait_send()
        return 0

    lax.fori_loop(0, width // tile, first, 0)
    lax.fori_loop(0, width // tile, second, 0)
    return lambda: lax.fori_loop(0, width // tile, end, 0)


def feed_forward_kernel(
    links,
    own_ref,
    grads_ref,
    both_ref,
    shift_ref,
    residual_ref,
    table_ref,
    full_ref,
    hid_ref,
    slope_ref,
    both_grad_ref,
    back_ref,
    branch_ref,
    vector_ref,
    bias_ref,
    fall_ref,
    rise_big,
    fall_big,
    rows_v,
    grads_v,
    hid_v,
    slope_v,
    kept_v,
    send_v,
    recv_v,
    theirs_v,
    came_v,
    load_sem,
    store_sem,
    pair_send,
    pair_recv,
    grad_send,
    grad_recv,
    grad_store,
    share_send,
    share_recv,
    sum_send,
    sum_recv,
):
    half, count = links.half, links.count
    width, hidden = own_ref.shape[1], hid_v.shape[1]
    length = 2 * half * count
    rise_v = rise_big.at[pl.ds(0, width), pl.ds(0, hidden)]
    fall_v = fall_big.at[pl.ds(0, width), pl.ds(0, hidden)]
    own_half = pl.ds(0, hidden // 2)
    other_half = pl.ds(hidden // 2, hidden // 2)
    partner = {"tp": 1 - lax.axis_index("tp")}
    links.greet([partner])
    swaps = [
        pltpu.make_async_remote_copy(
            src_ref=both_ref.at[:, pl.ds(n * (hidden // 2), hidden // 2)],
            dst_ref=target.at[:, other_half],
            send_sem=pair_send.at[n],
            recv_sem=pair_recv.at[n],
            device_id=partner,
            device_id_type=MESH,
        )
        for n, target in enumerate((fall_v, rise_v))
    ]
    for copy in swaps:
        copy.start()
    shares = links.sharing(own_ref, full_ref, share_send, share_recv)
    sums = links.summing(send_v, recv_v, sum_send, sum_recv)
    links.pass_on(shares, 0)
    keep = pltpu.make_async_copy(own_ref, full_ref.at[pl.ds(0, 2 * half)], load_sem.at[0])
    keep.start()
    first = pltpu.make_async_copy(own_ref, rows_v, load_sem.at[1])
    first.start()
    rise = pltpu.make_async_copy(both_ref.at[:, other_half], rise_v.at[:, own_half], load_sem.at[2])
    rise.start()
    fall = pltpu.make_async_copy(both_ref.at[:, own_half], fall_v.at[:, own_half], load_sem.at[3])
    fall.start()
    bias_ref[...] = jnp.zeros_like(bias_ref)

    grad_loads = links.loads(grads_ref, grads_v, 0, load_sem, 4)
    for copy in grad_loads:
        copy.start()
    stores = []
    tile = min(256, hidden)
    for i in range(count):
        if i == 0:
            first.wait()
            rise.wait()
            fall.wait()
            for copy in swaps:
                copy.wait_recv()
            keep_fall = pltpu.make_async_copy(fall_v, fall_ref, store_sem.at[4])
            keep_fall.start()
        else:
            for part in (0, 1):
                shares[(i, part)].wait_recv()
            links.pass_on(shares, i)
            row_loads = links.loads(full_ref, rows_v, i, load_sem, 8)
            for copy in row_loads:
                copy.start()
            for copy in row_loads:
                copy.wait()
        for copy in grad_loads + stores:
            copy.wait()

        def rise_step(step, _, i=i):
            at = pl.ds(pl.multiple_of(step * tile, tile), tile)
            pre = product(rows_v[...], rise_v[:, at]) + shift_ref[0:1, at]
            back = product(grads_v[...], fall_v[:, at])
            cumulative = 0.5 * (1.0 + lax.erf(pre * 0.7071067811865476))
            density = jnp.exp(-0.5 * pre * pre) * 0.3989422804014327
            hid_v[:, at] = (pre * cumulative).astype(BF16)
            slope = (back * (cumulative + pre * density)).astype(BF16)
            slope_v[:, at] = slope
            bias_ref[0:1, at] += jnp.sum(slope.astype(F32), axis=0, keepdims=True)
            return 0

        lax.fori_loop(0, hidden // tile, rise_step, 0)
        if i + 1 < count:
            grad_loads = links.loads(grads_ref, grads_v, i + 1, load_sem, 4)
            for copy in grad_loads:
                copy.start()
        stores = []
        for n, (buffer, ref) in enumerate(((hid_v, hid_ref), (slope_v, slope_ref))):
            for part in (0, 1):
                copy = pltpu.make_async_copy(
                    buffer.at[pl.ds(part * half, half)],
                    links.rows(ref, i, part),
                    store_sem.at[2 * n + part],
                )
                copy.start()
                stores.append(copy)

        links.terms(i, lambda at: across(slope_v[...], rise_v[at, :]), width, kept_v, send_v)
        if i >= count // 2:
            for part in (0, 1):
                sums[(i, part)].start()
    for copy in stores:
        copy.wait()
    keep.wait()
    keep_fall.wait()
    rows_big = rise_big.at[pl.ds(0, length), pl.ds(0, width)]
    columns_big = fall_big.at[pl.ds(0, length), pl.ds(0, hidden)]
    ends = []
    for n, (left, right) in enumerate(((full_ref, slope_ref), (grads_ref, hid_ref))):
        lefts = pltpu.make_async_copy(left, rows_big, load_sem.at[0])
        rights = pltpu.make_async_copy(right, columns_big, load_sem.at[1])
        lefts.start()
        rights.start()
        for end in ends:
            end()
        lefts.wait()
        rights.wait()
        ends = [
            weight_grads(
                partner,
                rows_big,
                columns_big,
                theirs_v,
                came_v.at[n],
                both_grad_ref.at[:, pl.ds((1 - n) * (hidden // 2), hidden // 2)],
                grad_send.at[n],
                grad_recv.at[n],
                grad_store.at[n],
            )
        ]
        if n == 0:
            links.combine(sums, kept_v, send_v, recv_v, count // 2 - 1, 1)
            finals = [
                pltpu.make_async_copy(
                    residual_ref.at[pl.ds(part * half, half)], kept_v.at[2 + part], load_sem.at[2 + part]
                )
                for part in (0, 1)
            ]
            finals.append(
                pltpu.make_async_copy(grads_ref.at[pl.ds(0, 2 * half)], rows_v, load_sem.at[4])
            )
            for copy in finals:
                copy.start()
    for copy in finals:
        copy.wait()
    vector_ref[...] = jnp.zeros_like(vector_ref)
    results = []

    def last(part, at, to, second):
        normed, spread = normalize(kept_v[2 + part, at, :])
        incoming = rows_v[to, :].astype(F32)
        back = incoming + norm_back(second * table_ref[2:3, :], normed, spread)
        branch = back.astype(BF16)
        kept_v[part, at, :] = back
        rows_v[to, :] = branch
        for n, value in enumerate((second * normed, second, branch.astype(F32), incoming)):
            vector_ref[n : n + 1, :] += jnp.sum(value, axis=0, keepdims=True)

    def store_part(part):
        rows = pl.ds(part * half, half)
        for n, (source, target) in enumerate(
            ((kept_v.at[part], back_ref.at[rows]), (rows_v.at[rows], branch_ref.at[rows]))
        ):
            copy = pltpu.make_async_copy(source, target, load_sem.at[2 * part + n])
            copy.start()
            results.append(copy)

    links.combine(sums, kept_v, send_v, recv_v, 0, 0, last, store_part)
    for end in ends:
        end()
    for copy in results:
        copy.wait()
    for copy in swaps:
        copy.wait_send()
    for pair in links.pairs:
        shares[pair].wait_send()
        sums[pair].wait_send()


def feed_forward(own, grads, both_weights, shift, residual, table, count):
    rows, width = own.shape
    hidden = both_weights.shape[1]
    length = rows * count
    links = Links(count, rows // 2)
    half, copies = links.half, len(links.pairs)
    anywhere = pl.BlockSpec(memory_space=pl.ANY)
    inside = pl.BlockSpec(memory_space=pltpu.VMEM)
    dma = pltpu.SemaphoreType.DMA
    return pl.pallas_call(
        functools.partial(feed_forward_kernel, links),
        out_shape=(
            jax.ShapeDtypeStruct((length, width), BF16),
            jax.ShapeDtypeStruct((length, hidden), BF16),
            jax.ShapeDtypeStruct((length, hidden), BF16),
            jax.ShapeDtypeStruct((width, hidden), BF16),
            jax.ShapeDtypeStruct((rows, width), F32),
            jax.ShapeDtypeStruct((rows, width), BF16),
            jax.ShapeDtypeStruct((8, width), F32),
            jax.ShapeDtypeStruct((1, hidden), F32),
            jax.ShapeDtypeStruct((width, hidden), BF16),
        ),
        in_specs=[anywhere, anywhere, anywhere, inside, anywhere, inside],
        out_specs=(anywhere,) * 6 + (inside, inside, anywhere),
        scratch_shapes=[
            pltpu.VMEM((max(width, length), max(width, hidden)), BF16),
            pltpu.VMEM((max(width, length), hidden), BF16),
            pltpu.VMEM((rows, width), BF16),
            pltpu.VMEM((rows, width), BF16),
            pltpu.VMEM((rows, hidden), BF16),
            pltpu.VMEM((rows, hidden), BF16),
            pltpu.VMEM((count, half, width), F32),
            pltpu.VMEM((copies, half, width), BF16),
            pltpu.VMEM((copies, half, width), BF16),
            pltpu.VMEM((width, hidden // 2), BF16),
            pltpu.VMEM((2, width, hidden // 2), BF16),
            dma((10,)),
            dma((5,)),
            dma((2,)),
            dma((2,)),
            dma((2, width // 256)),
            dma((2, width // 256)),
            dma((2, width // 256)),
            dma((copies,)),
            dma((copies,)),
            dma((copies,)),
            dma((copies,)),
        ],
        compiler_params=pltpu.CompilerParams(
            collective_id=3, has_side_effects=True, vmem_limit_bytes=63 * 1024 * 1024
        ),
        cost_estimate=pl.CostEstimate(
            flops=10 * length * width * hidden,
            bytes_accessed=length * width * 8 + width * hidden * 4 + length * hidden * 4,
            transcendentals=length * hidden * 2,
        ),
        name="feed_forward",
    )(own, grads, both_weights, shift, residual, table)


def greet_all(partners):
    barrier = pltpu.get_barrier_semaphore()
    for partner in partners:
        pl.semaphore_signal(barrier, 1, device_id=partner, device_id_type=MESH)
    pl.semaphore_wait(barrier, len(partners))


def others(axis, count):
    return [{axis: lax.bitwise_xor(lax.axis_index(axis), mask)} for mask in range(1, count)]


def axis_bits(axis, size):
    return [
        {axis: lax.bitwise_xor(lax.axis_index(axis), 1 << bit)}
        for bit in range((size - 1).bit_length())
    ]


def piece_copies(count, source, target_ref, send_sem, recv_sem, local_sem):
    here = lax.axis_index("ctx")
    copies = [
        pltpu.make_async_remote_copy(
            src_ref=source(lax.bitwise_xor(here, mask)),
            dst_ref=target_ref.at[here],
            send_sem=send_sem.at[mask - 1],
            recv_sem=recv_sem.at[mask - 1],
            device_id={"ctx": lax.bitwise_xor(here, mask)},
            device_id_type=MESH,
        )
        for mask in range(1, count)
    ]
    return copies + [pltpu.make_async_copy(source(here), target_ref.at[here], local_sem)]


class Line:
    def __init__(self, whole_ref, depth, send_sem, recv_sem):
        self.whole, self.depth = whole_ref, depth
        self.send_sem, self.recv_sem = send_sem, recv_sem
        self.me = lax.axis_index("dp")

    def copy(self, way, step, block):
        block = jnp.clip(block, 0, self.depth - 1)
        target = jnp.clip(self.me + way, 0, self.depth - 1)
        n = 0 if way > 0 else 1
        return pltpu.make_async_remote_copy(
            src_ref=self.whole.at[block],
            dst_ref=self.whole.at[block],
            send_sem=self.send_sem.at[n, step - 1],
            recv_sem=self.recv_sem.at[n, step - 1],
            device_id={"dp": target},
            device_id_type=MESH,
        )

    def sends(self, step, act):
        me, depth = self.me, self.depth

        @pl.when((me + 1 < depth) & (me - step + 1 >= 0))
        def _():
            act(self.copy(1, step, me - step + 1))

        @pl.when((me >= 1) & (me + step - 1 < depth))
        def _():
            act(self.copy(-1, step, me + step - 1))

    def start(self, step):
        self.sends(step, lambda copy: copy.start())

    def arrive(self, step):
        @pl.when(self.me - step >= 0)
        def _():
            self.copy(1, step, self.me - step).wait_recv()

        @pl.when(self.me + step < self.depth)
        def _():
            self.copy(-1, step, self.me + step).wait_recv()

    def finish(self):
        for step in range(1, self.depth):
            self.sends(step, lambda copy: copy.wait_send())


def front_kernel(
    links,
    depth,
    tokens_ref,
    head_pieces_ref,
    pieces_ref,
    small_ref,
    normed_ref,
    head_ref,
    block_ref,
    table_ref,
    rows_v,
    normed_v,
    shards_v,
    load_sem,
    store_sem,
    share_send,
    share_recv,
    head_send,
    head_recv,
    piece_send,
    piece_recv,
    line_send,
    line_recv,
    shard_send,
    shard_recv,
):
    count, half = links.count, links.half
    size = 2 * half
    here, layer = lax.axis_index("ctx"), lax.axis_index("dp")
    shard = here * depth + layer
    thin = small_ref.shape[1]
    own_ref = tokens_ref.at[lax.axis_index("tp")]
    greet_all(others("ctx", count) + others("dp", depth))
    heads = piece_copies(
        count, lambda i: head_pieces_ref.at[i], head_ref.at[layer], head_send, head_recv, load_sem.at[2]
    )
    for copy in heads:
        copy.start()
    first = pltpu.make_async_copy(own_ref, rows_v.at[pl.ds(0, size)], load_sem.at[1])
    first.start()
    shards_v[shard] = small_ref[...]
    for bit, device in enumerate(axis_bits("dp", depth) + axis_bits("ctx", count)):
        reach = 1 << bit
        mine = pl.ds(shard // reach * reach, reach)
        theirs = pl.ds((shard // reach ^ 1) * reach, reach)
        copies = [
            pltpu.make_async_remote_copy(
                src_ref=shards_v.at[mine],
                dst_ref=shards_v.at[place],
                send_sem=shard_send.at[bit],
                recv_sem=shard_recv.at[bit],
                device_id=device,
                device_id_type=MESH,
            )
            for place in (mine, theirs)
        ]
        copies[0].start()
        copies[0].wait_send()
        copies[1].wait_recv()
    shares = links.sharing(own_ref, rows_v, share_send, share_recv)
    links.pass_on(shares, 0)
    line = Line(head_ref, depth, line_send, line_recv)
    for copy in heads:
        copy.wait()
    line.start(1)
    pieces = piece_copies(
        count, lambda i: pieces_ref.at[i], block_ref, piece_send, piece_recv, load_sem.at[0]
    )
    for copy in pieces:
        copy.start()
    for c in range(count):
        for d in range(depth):
            n = d * count + c
            table_ref[:, n * thin : (n + 1) * thin] = shards_v[c * depth + d]
    chunk = min(32, half)
    stores = []
    for i in range(max(count, depth)):
        if 0 < i < depth:
            line.arrive(i)
            if i + 1 < depth:
                line.start(i + 1)
        if i >= count:
            continue
        if i == 0:
            first.wait()
        else:
            for part in (0, 1):
                shares[(i, part)].wait_recv()
            links.pass_on(shares, i)
        for part in (0, 1):
            base = links.start_row(i, part)

            def norm(step, _, base=base):
                at = pl.ds(pl.multiple_of(base + step * chunk, chunk), chunk)
                normed = normalize(rows_v[at, :].astype(F32))[0]
                normed_v[at, :] = (normed * table_ref[0:1, :] + table_ref[1:2, :]).astype(BF16)
                return 0

            lax.fori_loop(0, half // chunk, norm, 0)
            store = pltpu.make_async_copy(
                links.rows(normed_v, i, part), links.rows(normed_ref, i, part), store_sem.at[2 * i + part]
            )
            store.start()
            stores.append(store)
    for copy in stores + pieces:
        copy.wait()
    line.finish()
    for pair in links.pairs:
        shares[pair].wait_send()


def front(tokens, head_pieces, pieces, small, count, depth):
    _, rows, width = tokens.shape
    length = rows * count
    links = Links(count, rows // 2)
    copies = len(links.pairs)
    bits = (count - 1).bit_length() + (depth - 1).bit_length()
    anywhere = pl.BlockSpec(memory_space=pl.ANY)
    inside = pl.BlockSpec(memory_space=pltpu.VMEM)
    dma = pltpu.SemaphoreType.DMA
    return pl.pallas_call(
        functools.partial(front_kernel, links, depth),
        out_shape=(
            jax.ShapeDtypeStruct((length, width), BF16),
            jax.ShapeDtypeStruct((depth, *head_pieces.shape), BF16),
            jax.ShapeDtypeStruct(pieces.shape, BF16),
            jax.ShapeDtypeStruct((8, width), F32),
        ),
        in_specs=[anywhere, anywhere, anywhere, inside],
        out_specs=(anywhere, anywhere, anywhere, inside),
        scratch_shapes=[
            pltpu.VMEM((length, width), BF16),
            pltpu.VMEM((length, width), BF16),
            pltpu.VMEM((count * depth, *small.shape), F32),
            dma((3,)),
            dma((2 * count,)),
            dma((copies,)),
            dma((copies,)),
            dma((count - 1,)),
            dma((count - 1,)),
            dma((count - 1,)),
            dma((count - 1,)),
            dma((2, depth - 1)),
            dma((2, depth - 1)),
            dma((bits,)),
            dma((bits,)),
        ],
        compiler_params=pltpu.CompilerParams(
            collective_id=1, has_side_effects=True, vmem_limit_bytes=40 * 1024 * 1024
        ),
        cost_estimate=pl.CostEstimate(
            flops=20 * length * width, bytes_accessed=120000000, transcendentals=0
        ),
        name="front",
    )(tokens, head_pieces, pieces, small)


def end_kernel(
    count,
    depth,
    heads,
    rows_ref,
    vectors_ref,
    firsts_ref,
    biases_ref,
    query_ref,
    key_ref,
    value_ref,
    out_ref,
    features_ref,
    totals_ref,
    block_v,
    shards_v,
    pair_v,
    landing_v,
    bias_v,
    load_sem,
    piece_send,
    piece_recv,
    shard_send,
    shard_recv,
    bias_send,
    bias_recv,
    total_send,
    total_recv,
):
    here, layer = lax.axis_index("ctx"), lax.axis_index("dp")
    shard = layer * count + here
    partner = {"tp": 1 - lax.axis_index("tp")}
    thin = query_ref.shape[0]
    wide = heads * 3 * HEAD_DIM
    low, high = (count - 1).bit_length(), (depth - 1).bit_length()
    greet_all([partner] + others("ctx", count) + others("dp", depth))
    pieces = piece_copies(
        count,
        lambda i: rows_ref.at[pl.ds(pl.multiple_of(i * thin, thin), thin)],
        block_v,
        piece_send,
        piece_recv,
        load_sem.at[0],
    )
    for copy in pieces:
        copy.start()
    for n in range(count * depth):
        at = slice(n * thin, (n + 1) * thin)
        shards_v[n, 0:4, :] = vectors_ref[0:4, at]
        shards_v[n, 4:8, :] = firsts_ref[0:4, at]

    def exchange(source, target, device, send, recv):
        copy = pltpu.make_async_remote_copy(
            src_ref=source,
            dst_ref=target,
            send_sem=send,
            recv_sem=recv,
            device_id=device,
            device_id_type=MESH,
        )
        copy.start()
        return copy

    bias_v[0] = biases_ref[0]
    bias_v[1] = biases_ref[1]
    stage = [
        exchange(shards_v, pair_v, partner, shard_send.at[low + high], shard_recv.at[low + high]),
        exchange(bias_v.at[1], bias_v.at[2], partner, bias_send.at[high], bias_recv.at[high]),
    ]
    for copy in stage:
        copy.wait()
    shards_v[...] += pair_v[...]
    bias_v[0] += bias_v[2]
    totals = []
    devices = axis_bits("ctx", count) + axis_bits("dp", depth)
    for bit in range(low + high - 1, -1, -1):
        reach = 1 << bit
        mine = shard // reach * reach
        theirs = (shard // reach ^ 1) * reach
        stage = [
            exchange(
                shards_v.at[pl.ds(theirs, reach)],
                landing_v.at[pl.ds(reach, reach)],
                devices[bit],
                shard_send.at[bit],
                shard_recv.at[bit],
            )
        ]
        if bit >= low:
            n = bit - low
            stage.append(
                exchange(bias_v.at[0], bias_v.at[3 + n], devices[bit], bias_send.at[n], bias_recv.at[n])
            )
        for copy in stage:
            copy.wait()
        shards_v[pl.ds(mine, reach)] += landing_v[reach : 2 * reach]
        if bit >= low:
            bias_v[0] += bias_v[3 + bit - low]
        if bit == low:
            totals_ref[here] = bias_v[0]
            totals = [
                exchange(
                    bias_v.at[0], totals_ref.at[here], device, total_send.at[n], total_recv.at[n]
                )
                for n, device in enumerate(others("ctx", count))
            ]
    features_ref[...] = shards_v[shard]
    for copy in pieces + totals:
        copy.wait()
    for c in range(count):
        for j in range(heads):
            to = slice((c * heads + j) * HEAD_DIM, (c * heads + j + 1) * HEAD_DIM)
            for n, ref in enumerate((query_ref, key_ref, value_ref)):
                column = (3 * j + n) * HEAD_DIM
                ref[:, to] = block_v[c, :, column : column + HEAD_DIM].astype(F32)
        rows = slice(c * heads * HEAD_DIM, (c + 1) * heads * HEAD_DIM)
        out_ref[rows, :] = block_v[c, :, wide:].astype(F32).T


def end(rows, vectors, firsts, biases, heads, count, depth):
    low, high = (count - 1).bit_length(), (depth - 1).bit_length()
    thin = rows.shape[0] // count
    columns = rows.shape[1]
    local = count * heads * HEAD_DIM
    inside = pl.BlockSpec(memory_space=pltpu.VMEM)
    dma = pltpu.SemaphoreType.DMA
    shards = (count * depth, 8, thin)
    return pl.pallas_call(
        functools.partial(end_kernel, count, depth, heads),
        out_shape=(
            jax.ShapeDtypeStruct((thin, local), F32),
            jax.ShapeDtypeStruct((thin, local), F32),
            jax.ShapeDtypeStruct((thin, local), F32),
            jax.ShapeDtypeStruct((local, thin), F32),
            jax.ShapeDtypeStruct((8, thin), F32),
            jax.ShapeDtypeStruct((count, 1, biases.shape[2]), F32),
        ),
        in_specs=[pl.BlockSpec(memory_space=pl.ANY), inside, inside, inside],
        out_specs=(inside,) * 6,
        scratch_shapes=[
            pltpu.VMEM((count, thin, columns), BF16),
            pltpu.VMEM(shards, F32),
            pltpu.VMEM(shards, F32),
            pltpu.VMEM(shards, F32),
            pltpu.VMEM((3 + high, 1, biases.shape[2]), F32),
            dma((1,)),
            dma((count - 1,)),
            dma((count - 1,)),
            dma((low + high + 1,)),
            dma((low + high + 1,)),
            dma((high + 1,)),
            dma((high + 1,)),
            dma((count - 1,)),
            dma((count - 1,)),
        ],
        compiler_params=pltpu.CompilerParams(
            collective_id=7, has_side_effects=True, vmem_limit_bytes=24 * 1024 * 1024
        ),
        cost_estimate=pl.CostEstimate(flops=0, bytes_accessed=40000000, transcendentals=0),
        name="end",
    )(rows, vectors, firsts, biases)


def attend_kernel(
    links,
    heads,
    rows_ref,
    weight_ref,
    shift_ref,
    cotangent_ref,
    tokens_ref,
    table_ref,
    qkv_ref,
    mixed_ref,
    log_ref,
    grads_full_ref,
    residual_ref,
    second_ref,
    whole_ref,
    own_v,
    rows_v,
    weight_v,
    qkv_v,
    mixed_v,
    scores_v,
    kept_v,
    send_v,
    recv_v,
    load_sem,
    store_sem,
    pair_send,
    pair_recv,
    share_send,
    share_recv,
    sum_send,
    sum_recv,
):
    count, half = links.count, links.half
    size = 2 * half
    here = lax.axis_index("ctx")
    core = lax.axis_index("tp")
    partner = {"tp": 1 - core}
    grads_ref = cotangent_ref.at[core]
    narrow = weight_ref.shape[1]
    wide = heads * 3 * HEAD_DIM // 2
    links.greet([partner])
    theirs = pltpu.make_async_remote_copy(
        src_ref=weight_ref,
        dst_ref=weight_v.at[1],
        send_sem=pair_send.at[0],
        recv_sem=pair_recv.at[0],
        device_id=partner,
        device_id_type=MESH,
    )
    theirs.start()
    shares = links.sharing(grads_ref, grads_full_ref, share_send, share_recv)
    sums = links.summing(send_v, recv_v, sum_send, sum_recv)
    links.pass_on(shares, 0)
    ours = pltpu.make_async_copy(weight_ref, weight_v.at[0], load_sem.at[0])
    ours.start()
    keep = pltpu.make_async_copy(grads_ref, grads_full_ref.at[pl.ds(0, size)], load_sem.at[1])
    keep.start()
    own = pltpu.make_async_copy(tokens_ref.at[core], own_v, load_sem.at[4])
    own.start()

    def load(n):
        return pltpu.make_async_copy(
            rows_ref.at[pl.ds(n * size, size)], rows_v.at[n % 2], load_sem.at[2 + n % 2]
        )

    coming = load(0)
    coming.start()
    ours.wait()
    theirs.wait_recv()
    wholes = []
    for core in (0, 1):
        copy = pltpu.make_async_copy(weight_v.at[core], whole_ref.at[core], store_sem.at[core])
        copy.start()
        wholes.append(copy)
    tile = 256 if wide % 256 == 0 else HEAD_DIM
    for n in range(count):
        coming.wait()
        if n + 1 < count:
            coming = load(n + 1)
            coming.start()
        for core in (0, 1):

            def step(m, _, n=n, core=core):
                at = pl.ds(pl.multiple_of(m * tile, tile), tile)
                to = pl.ds(pl.multiple_of(core * wide + m * tile, tile), tile)
                value = product(rows_v[n % 2], weight_v[core, :, at]) + shift_ref[0:1, to]
                qkv_v[n * size : (n + 1) * size, to] = value.astype(BF16)
                return 0

            lax.fori_loop(0, wide // tile, step, 0)
    keep_qkv = pltpu.make_async_copy(qkv_v, qkv_ref, store_sem.at[2])
    keep_qkv.start()

    def one_head(head, _):
        @pl.when(head == heads // 2)
        def _():
            for i in range(1, (count + 1) // 2):
                for part in (0, 1):
                    shares[(i, part)].wait_recv()
                links.pass_on(shares, i)

        attend_forward_head(here, head, size, count, qkv_v, mixed_v, log_ref, scores_v)
        return 0

    lax.fori_loop(0, heads, one_head, 0)
    keep_mixed = pltpu.make_async_copy(mixed_v, mixed_ref, store_sem.at[3])
    keep_mixed.start()
    chip = heads * HEAD_DIM // 2
    for i in range(count - 1, -1, -1):

        def out_rows(core, i=i):
            at = slice(core * chip, (core + 1) * chip)
            first = [links.start_row(i, part) for part in (0, 1)]
            return jnp.concatenate([mixed_v[row : row + half, at] for row in first], axis=0)

        links.terms(
            i,
            lambda at: across(out_rows(0), weight_v[0, at, wide:narrow])
            + across(out_rows(1), weight_v[1, at, wide:narrow]),
            residual_ref.shape[1],
            kept_v,
            send_v,
        )
        if i >= count // 2:
            for part in (0, 1):
                sums[(i, part)].start()

    def norm(part, at, to, value):
        residual = own_v[to, :].astype(F32) + (value + table_ref[4:5, :])
        residual_ref[to, :] = residual
        normed = normalize(residual)[0]
        second_ref[to, :] = (normed * table_ref[2:3, :] + table_ref[3:4, :]).astype(BF16)

    own.wait()
    links.combine(sums, kept_v, send_v, recv_v, count // 2 - 1, 0, norm)
    for i in range(1, count):
        for part in (0, 1):
            if i >= (count + 1) // 2:
                shares[(i, part)].wait_recv()
    for copy in wholes + [keep_qkv, keep_mixed, keep]:
        copy.wait()
    theirs.wait_send()
    for pair in links.pairs:
        sums[pair].wait_send()
        shares[pair].wait_send()


def attend_forward_head(here, head, size, blocks, qkv_v, mixed_v, log_ref, scores_v):
    scaling = HEAD_DIM ** (-0.5)
    behind = lax.broadcasted_iota(jnp.int32, (size, size), 1) <= lax.broadcasted_iota(
        jnp.int32, (size, size), 0
    )
    column = pl.multiple_of(head * (3 * HEAD_DIM), HEAD_DIM)
    query_at = pl.ds(column, HEAD_DIM)
    key_at = pl.ds(pl.multiple_of(column + HEAD_DIM, HEAD_DIM), HEAD_DIM)
    value_at = pl.ds(pl.multiple_of(column + 2 * HEAD_DIM, HEAD_DIM), HEAD_DIM)
    head_at = pl.ds(pl.multiple_of(head * HEAD_DIM, HEAD_DIM), HEAD_DIM)
    for i in range(blocks):
        at = pl.ds(rows_of(here, i, size), size)
        queries = qkv_v[at, query_at]
        highest = jnp.full((size, 1), NEGATIVE, F32)
        for j in range(i + 1):
            keys = qkv_v[pl.ds(rows_of(here, j, size), size), key_at]
            scores = across(queries, keys) * scaling
            if j == i:
                scores = jnp.where(behind, scores, NEGATIVE)
            scores_v[:, j * size : (j + 1) * size] = scores
            highest = jnp.maximum(highest, jnp.max(scores, axis=1, keepdims=True))
        row_total = jnp.zeros((size, 1), F32)
        mixed = jnp.zeros((size, HEAD_DIM), F32)
        for j in range(i + 1):
            exponent = jnp.exp(scores_v[:, j * size : (j + 1) * size] - highest)
            row_total = row_total + jnp.sum(exponent, axis=1, keepdims=True)
            values = qkv_v[pl.ds(rows_of(here, j, size), size), value_at]
            mixed = mixed + product(exponent.astype(BF16), values)
        mixed_v[at, head_at] = (mixed / row_total).astype(BF16)
        log_total = jnp.broadcast_to(highest + jnp.log(row_total), (size, HEAD_DIM))
        log_ref[head, :, at] = log_total.T[0:8, :]


def attend(rows, weight, shift, cotangent, tokens, table, heads, count):
    length, width = rows.shape
    size = length // count
    narrow = weight.shape[1]
    columns = heads * 3 * HEAD_DIM
    links = Links(count, size // 2)
    half, copies = links.half, len(links.pairs)
    pairs = heads * length * (length + size) // 2
    anywhere = pl.BlockSpec(memory_space=pl.ANY)
    inside = pl.BlockSpec(memory_space=pltpu.VMEM)
    dma = pltpu.SemaphoreType.DMA
    return pl.pallas_call(
        functools.partial(attend_kernel, links, heads),
        out_shape=(
            jax.ShapeDtypeStruct((length, columns), BF16),
            jax.ShapeDtypeStruct((length, heads * HEAD_DIM), BF16),
            jax.ShapeDtypeStruct((heads, 8, length), F32),
            jax.ShapeDtypeStruct((length, width), BF16),
            jax.ShapeDtypeStruct((size, width), F32),
            jax.ShapeDtypeStruct((size, width), BF16),
            jax.ShapeDtypeStruct((2, width, narrow), BF16),
        ),
        in_specs=[anywhere, anywhere, inside, anywhere, anywhere, inside],
        out_specs=(anywhere, anywhere, inside, anywhere, inside, inside, anywhere),
        scratch_shapes=[
            pltpu.VMEM((size, width), BF16),
            pltpu.VMEM((2, size, width), BF16),
            pltpu.VMEM((2, width, narrow), BF16),
            pltpu.VMEM((length, columns), BF16),
            pltpu.VMEM((length, heads * HEAD_DIM), BF16),
            pltpu.VMEM((size, length), F32),
            pltpu.VMEM((count, half, width), F32),
            pltpu.VMEM((copies, half, width), BF16),
            pltpu.VMEM((copies, half, width), BF16),
            dma((5,)),
            dma((4,)),
            dma((1,)),
            dma((1,)),
            dma((copies,)),
            dma((copies,)),
            dma((copies,)),
            dma((copies,)),
        ],
        compiler_params=pltpu.CompilerParams(
            collective_id=2, has_side_effects=True, vmem_limit_bytes=60 * 1024 * 1024
        ),
        cost_estimate=pl.CostEstimate(
            flops=pairs * HEAD_DIM * 8 + 2 * length * width * heads * HEAD_DIM * 4,
            bytes_accessed=length * width * 8,
            transcendentals=pairs,
        ),
        name="attend",
    )(rows, weight, shift, cotangent, tokens, table)


def attend_back_kernel(
    links,
    heads,
    own_ref,
    weight_ref,
    qkv_ref,
    mixed_ref,
    log_ref,
    hid_ref,
    fall_ref,
    first_ref,
    residual_ref,
    table_ref,
    full_ref,
    result_ref,
    low_ref,
    head_grad_ref,
    residual_v,
    weight_v,
    qkv_v,
    mixed_v,
    big_v,
    theirs_v,
    came_v,
    grad_v,
    rows_v,
    hid_v,
    fall_v,
    key_v,
    value_v,
    kept_v,
    send_v,
    recv_v,
    load_sem,
    grad_send,
    grad_recv,
    grad_store,
    share_send,
    share_recv,
    sum_send,
    sum_recv,
):
    half, count = links.half, links.count
    size = 2 * half
    here = lax.axis_index("ctx")
    chip = weight_v.shape[2]
    wide = heads * 3 * HEAD_DIM // 2
    partner = {"tp": 1 - lax.axis_index("tp")}
    links.greet([partner])
    shares = links.sharing(own_ref, full_ref, share_send, share_recv)
    sums = links.summing(send_v, recv_v, sum_send, sum_recv)
    links.pass_on(shares, 0)
    narrow = fall_v.shape[0]
    loads = [
        pltpu.make_async_copy(source, target, load_sem.at[n])
        for n, (source, target) in enumerate(
            (
                (fall_ref.at[pl.ds(0, narrow)], fall_v),
                (own_ref, rows_v),
                (weight_ref.at[:, :, pl.ds(weight_ref.shape[2] - chip, chip)], weight_v),
                (qkv_ref, qkv_v),
                (mixed_ref, mixed_v),
                (own_ref, full_ref.at[pl.ds(0, size)]),
                (first_ref, big_v),
                (residual_ref.at[:, pl.ds(0, narrow)], residual_v),
            )
        )
    ]
    for copy in loads:
        copy.start()
    loads[0].wait()
    out_terms(links, hid_ref, hid_v, fall_v, kept_v, send_v, load_sem, 8)
    for i in range(count):
        if i == 0:
            loads[1].wait()
            loads[2].wait()
        else:
            for part in (0, 1):
                shares[(i, part)].wait_recv()
            links.pass_on(shares, i)
            unit_loads = links.loads(full_ref, rows_v, i, load_sem, 8)
            for copy in unit_loads:
                copy.start()
            for copy in unit_loads:
                copy.wait()
        for core in (0, 1):
            term = product(rows_v[...], weight_v[core]).astype(BF16)
            for part in (0, 1):
                first = links.start_row(i, part)
                grad_v[first : first + half, core * chip : (core + 1) * chip] = term[
                    part * half : (part + 1) * half
                ]
    for i in range(count - 1, count // 2 - 1, -1):
        for part in (0, 1):
            sums[(i, part)].start()
    loads[3].wait()
    loads[4].wait()

    def one_head(head, _):
        @pl.when(head == heads // 2)
        def _():
            links.combine(sums, kept_v, send_v, recv_v, count // 2 - 1, 1)

        attend_backward_head(
            here, head, size, count, qkv_v, grad_v, mixed_v, log_ref, result_ref, key_v, value_v
        )
        return 0

    lax.fori_loop(0, heads, one_head, 0)
    loads[5].wait()
    loads[6].wait()
    end_first = weight_grads(
        partner,
        big_v,
        result_ref,
        theirs_v.at[:, pl.ds(0, wide)],
        came_v.at[:, pl.ds(0, wide)],
        head_grad_ref.at[:, pl.ds(0, wide)],
        grad_send.at[0],
        grad_recv.at[0],
        grad_store.at[0],
    )
    again = pltpu.make_async_copy(full_ref, big_v, load_sem.at[6])
    again.start()
    loads[7].wait()

    def low(part, at, to, value):
        low_ref[to, :] = (residual_v[to, :] + (value + table_ref[5:6, 0:narrow])).astype(BF16)

    links.combine(sums, kept_v, send_v, recv_v, 0, 0, low)
    again.wait()
    end_second = weight_grads(
        partner,
        big_v,
        mixed_v,
        theirs_v.at[:, pl.ds(wide, chip)],
        came_v.at[:, pl.ds(wide, chip)],
        head_grad_ref.at[:, pl.ds(wide, chip)],
        grad_send.at[1],
        grad_recv.at[1],
        grad_store.at[1],
    )
    end_first()
    end_second()
    for pair in links.pairs:
        sums[pair].wait_send()
        shares[pair].wait_send()


def out_terms(links, hid_ref, hid_v, fall_v, kept_v, send_v, load_sem, base):
    count, half = links.count, links.half
    order = list(range(count - 1, -1, -1))
    unit_loads = links.loads(hid_ref, hid_v.at[0], order[0], load_sem, base)
    for copy in unit_loads:
        copy.start()
    for n, i in enumerate(order):
        for copy in unit_loads:
            copy.wait()
        if n + 1 < count:
            unit_loads = links.loads(
                hid_ref, hid_v.at[(n + 1) % 2], order[n + 1], load_sem, base + 2 * ((n + 1) % 2)
            )
            for copy in unit_loads:
                copy.start()
        links.terms(
            i, lambda at, n=n: across(hid_v[n % 2], fall_v[at, :]), fall_v.shape[0], kept_v, send_v
        )


def attend_backward_head(
    here, head, size, blocks, qkv_v, grad_v, mixed_v, log_ref, result_ref, key_v, value_v
):
    scaling = HEAD_DIM ** (-0.5)
    behind = lax.broadcasted_iota(jnp.int32, (size, size), 0) <= lax.broadcasted_iota(
        jnp.int32, (size, size), 1
    )
    column = pl.multiple_of(head * (3 * HEAD_DIM), HEAD_DIM)
    query_at = pl.ds(column, HEAD_DIM)
    key_at = pl.ds(pl.multiple_of(column + HEAD_DIM, HEAD_DIM), HEAD_DIM)
    value_at = pl.ds(pl.multiple_of(column + 2 * HEAD_DIM, HEAD_DIM), HEAD_DIM)
    head_at = pl.ds(pl.multiple_of(head * HEAD_DIM, HEAD_DIM), HEAD_DIM)
    for i in range(blocks):
        at = pl.ds(rows_of(here, i, size), size)
        queries = qkv_v[at, query_at]
        grads = grad_v[at, head_at]
        both = grads.astype(F32) * mixed_v[at, head_at].astype(F32)
        centre = jnp.sum(both.T, axis=0, keepdims=True)
        log_total = log_ref[head, 0:1, at]
        query_grad = jnp.zeros((size, HEAD_DIM), F32)
        for j in range(i + 1):
            there = pl.ds(rows_of(here, j, size), size)
            keys = qkv_v[there, key_at]
            values = qkv_v[there, value_at]
            weights = jnp.exp(across(keys, queries) * scaling - log_total)
            if j == i:
                weights = jnp.where(behind, weights, 0.0)
            slopes = (weights * (across(values, grads) - centre)).astype(BF16)
            value_term = product(weights.astype(BF16), grads)
            key_term = product(slopes, queries)
            query_grad = query_grad + inner(slopes, keys)
            place = slice(j * size, (j + 1) * size)
            if i == j:
                value_v[place, :] = value_term
                key_v[place, :] = key_term
            else:
                value_v[place, :] += value_term
                key_v[place, :] += key_term
        result_ref[at, query_at] = (query_grad * scaling).astype(BF16)
    for j in range(blocks):
        there = pl.ds(rows_of(here, j, size), size)
        place = slice(j * size, (j + 1) * size)
        result_ref[there, key_at] = (key_v[place, :] * scaling).astype(BF16)
        result_ref[there, value_at] = value_v[place, :].astype(BF16)


def attend_back(
    own, weight, qkv, mixed, log_total, hid, fall_weight, first, residual, table, count
):
    rows, width = own.shape
    length, columns = qkv.shape
    heads = columns // (3 * HEAD_DIM)
    hidden = hid.shape[1]
    links = Links(count, rows // 2)
    half, copies = links.half, len(links.pairs)
    narrow = width // 2
    pairs = heads * length * (length + rows) // 2
    anywhere = pl.BlockSpec(memory_space=pl.ANY)
    inside = pl.BlockSpec(memory_space=pltpu.VMEM)
    dma = pltpu.SemaphoreType.DMA
    return pl.pallas_call(
        functools.partial(attend_back_kernel, links, heads),
        out_shape=(
            jax.ShapeDtypeStruct((length, width), BF16),
            jax.ShapeDtypeStruct((length, columns), BF16),
            jax.ShapeDtypeStruct((rows, narrow), BF16),
            jax.ShapeDtypeStruct((width, 2 * heads * HEAD_DIM), BF16),
        ),
        in_specs=[anywhere] * 4 + [inside] + [anywhere] * 4 + [inside],
        out_specs=(anywhere, inside, inside, anywhere),
        scratch_shapes=[
            pltpu.VMEM((rows, narrow), F32),
            pltpu.VMEM((2, width, heads * HEAD_DIM // 2), BF16),
            pltpu.VMEM(qkv.shape, BF16),
            pltpu.VMEM(mixed.shape, BF16),
            pltpu.VMEM((length, width), BF16),
            pltpu.VMEM((width, 2 * heads * HEAD_DIM), BF16),
            pltpu.VMEM((width, 2 * heads * HEAD_DIM), BF16),
            pltpu.VMEM(mixed.shape, BF16),
            pltpu.VMEM((rows, width), BF16),
            pltpu.VMEM((2, rows, hidden), BF16),
            pltpu.VMEM((narrow, hidden), BF16),
            pltpu.VMEM((length, HEAD_DIM), F32),
            pltpu.VMEM((length, HEAD_DIM), F32),
            pltpu.VMEM((count, half, narrow), F32),
            pltpu.VMEM((copies, half, narrow), BF16),
            pltpu.VMEM((copies, half, narrow), BF16),
            dma((12,)),
            dma((2, width // 256)),
            dma((2, width // 256)),
            dma((2, width // 256)),
            dma((copies,)),
            dma((copies,)),
            dma((copies,)),
            dma((copies,)),
        ],
        compiler_params=pltpu.CompilerParams(
            collective_id=4, has_side_effects=True, vmem_limit_bytes=63 * 1024 * 1024
        ),
        cost_estimate=pl.CostEstimate(
            flops=pairs * HEAD_DIM * 20 + 2 * length * width * (heads * HEAD_DIM + hidden // 2),
            bytes_accessed=length * width * 6 + length * columns * 4 + length * hidden * 2,
            transcendentals=pairs,
        ),
        name="attend_back",
    )(own, weight, qkv, mixed, log_total, hid, fall_weight, first, residual, table)


def first_back_kernel(
    links,
    grads_ref,
    weight_ref,
    hid_ref,
    fall_ref,
    low_ref,
    residual_ref,
    back_ref,
    tokens_ref,
    table_ref,
    hidden_ref,
    out_ref,
    input_ref,
    vector_ref,
    bias_ref,
    fall_grad_ref,
    rise_grad_ref,
    grads_v,
    weight_v,
    hid_v,
    fall_v,
    kept_v,
    send_v,
    recv_v,
    kept_w,
    send_w,
    recv_w,
    residual_v,
    tokens_v,
    high_v,
    block_v,
    load_sem,
    pair_send,
    pair_recv,
    piece_send,
    piece_recv,
    sum_send,
    sum_recv,
    late_send,
    late_recv,
):
    count, half = links.count, links.half
    size = 2 * half
    wide = weight_v.shape[2]
    thin = hidden_ref.shape[0] // count
    hidden = hidden_ref.shape[1] // 2
    narrow = fall_v.shape[0]
    core = lax.axis_index("tp")
    partner = {"tp": 1 - core}
    links.greet([partner], range(1, count))
    sums = links.summing(send_v, recv_v, sum_send, sum_recv)
    lates = links.summing(send_w, recv_w, late_send, late_recv)
    pieces = piece_copies(
        count,
        lambda i: hidden_ref.at[pl.ds(pl.multiple_of(i * thin, thin), thin)],
        block_v,
        piece_send,
        piece_recv,
        load_sem.at[10],
    )
    right = pl.ds(narrow, narrow)
    left = pl.ds(0, narrow)

    def both_cores(n, source, target_ref, rows, columns):
        target = target_ref.at[core, rows, columns]
        return [
            pltpu.make_async_copy(source, target, load_sem.at[11 + n]),
            pltpu.make_async_remote_copy(
                src_ref=source,
                dst_ref=target,
                send_sem=pair_send.at[n],
                recv_sem=pair_recv.at[n],
                device_id=partner,
                device_id_type=MESH,
            ),
        ]

    outs = both_cores(0, low_ref, out_ref, pl.ds(0, size), left)
    loads = [
        pltpu.make_async_copy(source, target, load_sem.at[n])
        for n, (source, target) in enumerate(
            (
                (weight_ref.at[:, :, pl.ds(0, wide)], weight_v),
                (fall_ref.at[right], fall_v),
            )
        )
    ]
    more = [
        pltpu.make_async_copy(source, target, load_sem.at[15 + n])
        for n, (source, target) in enumerate(
            ((residual_ref.at[:, right], residual_v), (tokens_ref.at[core], tokens_v))
        )
    ]
    for copy in loads:
        copy.start()
    order = list(range(count - 1, -1, -1))
    unit_loads = links.loads(grads_ref, grads_v.at[0], order[0], load_sem, 2)
    for copy in unit_loads + pieces + more + outs:
        copy.start()
    bias_ref[...] = jnp.zeros_like(bias_ref)
    vector_ref[...] = jnp.zeros_like(vector_ref)
    loads[0].wait()
    for n, i in enumerate(order):
        for copy in unit_loads:
            copy.wait()
        if n + 1 < count:
            unit_loads = links.loads(
                grads_ref, grads_v.at[(n + 1) % 2], order[n + 1], load_sem, 2 + 2 * ((n + 1) % 2)
            )
            for copy in unit_loads:
                copy.start()
        links.terms(
            i,
            lambda at, n=n: across(grads_v[n % 2, :, :wide], weight_v[0, at, :])
            + across(grads_v[n % 2, :, wide:], weight_v[1, at, :]),
            weight_v.shape[1],
            kept_v,
            send_v,
        )
        if i >= count // 2:
            for part in (0, 1):
                sums[(i, part)].start()
        chunk = min(64, half)

        def bias(step, _, n=n):
            rows = pl.ds(pl.multiple_of(step * chunk, chunk), chunk)
            value = grads_v[n % 2, rows, :].astype(F32)
            bias_ref[0:1, :] += jnp.sum(value, axis=0, keepdims=True)
            return 0

        lax.fori_loop(0, size // chunk, bias, 0)
    loads[1].wait()
    out_terms(links, hid_ref, hid_v, fall_v, kept_w, send_w, load_sem, 6)
    for copy in pieces:
        copy.wait()
    for c in range(count):
        rows = slice(c * hidden, (c + 1) * hidden)
        fall_grad_ref[rows, :] = block_v[c, :, 0:hidden].astype(F32).T
        rise_grad_ref[:, rows] = block_v[c, :, hidden : 2 * hidden].astype(F32)
    links.combine(sums, kept_v, send_v, recv_v, count // 2 - 1, 1)
    backs = [
        pltpu.make_async_copy(
            back_ref.at[pl.ds(part * half, half)], kept_v.at[2 + part], load_sem.at[2 + part]
        )
        for part in (0, 1)
    ]
    for copy in backs:
        copy.start()
    for i in range(count - 1, count // 2 - 1, -1):
        for part in (0, 1):
            lates[(i, part)].start()
    for copy in more + backs:
        copy.wait()

    def last(part, at, to, first):
        normed, spread = normalize(tokens_v[to, :].astype(F32))
        grad = kept_v[2 + part, at, :] + norm_back(first * table_ref[0:1, :], normed, spread)
        tokens_v[to, :] = grad.astype(BF16)
        for n, value in enumerate((first * normed, first)):
            vector_ref[n : n + 1, :] += jnp.sum(value, axis=0, keepdims=True)

    def send_part(part):
        rows = pl.ds(part * half, half)
        copies = both_cores(
            1 + part, tokens_v.at[rows], input_ref, rows, pl.ds(0, 2 * narrow)
        )
        for copy in copies:
            copy.start()
        outs.extend(copies)

    links.combine(sums, kept_v, send_v, recv_v, 0, 0, last, send_part)

    def high(part, at, to, value):
        high_v[to, :] = (
            residual_v[to, :] + (value + table_ref[5:6, narrow : 2 * narrow])
        ).astype(BF16)

    links.combine(lates, kept_w, send_w, recv_w, count // 2 - 1, 0, high)
    copies = both_cores(3, high_v, out_ref, pl.ds(0, size), right)
    for copy in copies:
        copy.start()
    for copy in outs + copies:
        copy.wait()
    for pair in links.pairs:
        sums[pair].wait_send()
        lates[pair].wait_send()


def first_back(
    grads, weight, hid, fall_weight, low, residual, back, tokens, table, hidden_rows, count
):
    length, columns = grads.shape
    width, hidden = fall_weight.shape
    rows = length // count
    links = Links(count, rows // 2)
    half, copies = links.half, len(links.pairs)
    narrow = width // 2
    thin, piece = hidden_rows.shape[0] // count, hidden_rows.shape[1] // 2
    anywhere = pl.BlockSpec(memory_space=pl.ANY)
    inside = pl.BlockSpec(memory_space=pltpu.VMEM)
    dma = pltpu.SemaphoreType.DMA
    return pl.pallas_call(
        functools.partial(first_back_kernel, links),
        out_shape=(
            jax.ShapeDtypeStruct((2, rows, width), BF16),
            jax.ShapeDtypeStruct((2, rows, width), BF16),
            jax.ShapeDtypeStruct((8, width), F32),
            jax.ShapeDtypeStruct((1, columns), F32),
            jax.ShapeDtypeStruct((count * piece, thin), F32),
            jax.ShapeDtypeStruct((thin, count * piece), F32),
        ),
        in_specs=[anywhere] * 8 + [inside, anywhere],
        out_specs=(anywhere, anywhere, inside, inside, inside, inside),
        scratch_shapes=[
            pltpu.VMEM((2, rows, columns), BF16),
            pltpu.VMEM((2, width, columns // 2), BF16),
            pltpu.VMEM((2, rows, hidden), BF16),
            pltpu.VMEM((narrow, hidden), BF16),
            pltpu.VMEM((count, half, width), F32),
            pltpu.VMEM((copies, half, width), BF16),
            pltpu.VMEM((copies, half, width), BF16),
            pltpu.VMEM((count, half, narrow), F32),
            pltpu.VMEM((copies, half, narrow), BF16),
            pltpu.VMEM((copies, half, narrow), BF16),
            pltpu.VMEM((rows, narrow), F32),
            pltpu.VMEM((rows, width), BF16),
            pltpu.VMEM((rows, narrow), BF16),
            pltpu.VMEM((count, thin, 2 * piece), BF16),
            dma((17,)),
            dma((4,)),
            dma((4,)),
            dma((count - 1,)),
            dma((count - 1,)),
            dma((copies,)),
            dma((copies,)),
            dma((copies,)),
            dma((copies,)),
        ],
        compiler_params=pltpu.CompilerParams(
            collective_id=5, has_side_effects=True, vmem_limit_bytes=63 * 1024 * 1024
        ),
        cost_estimate=pl.CostEstimate(
            flops=2 * length * width * (columns + hidden // 2),
            bytes_accessed=length * columns * 2 + length * hidden * 2 + width * (columns + hidden) * 2,
            transcendentals=0,
        ),
        name="first_back",
    )(grads, weight, hid, fall_weight, low, residual, back, tokens, table, hidden_rows)


def body(
    tokens,
    cotangent,
    attention_gain,
    attention_bias,
    feedforward_gain,
    feedforward_bias,
    query_weight,
    query_bias,
    key_weight,
    value_weight,
    value_bias,
    output_weight,
    output_bias,
    up_weight,
    up_bias,
    down_weight,
    down_bias,
):
    _, local_rows, model_width = tokens.shape
    ctx, dp = lax.axis_size("ctx"), lax.axis_size("dp")
    here, core = lax.axis_index("ctx"), lax.axis_index("tp")
    thin = query_weight.shape[0]
    heads = query_weight.shape[1] // (HEAD_DIM * ctx)
    hidden = up_weight.shape[1] // ctx
    packed = jnp.stack(
        [w.reshape(thin, ctx, heads, HEAD_DIM) for w in (query_weight, key_weight, value_weight)],
        axis=3,
    ).reshape(thin, ctx, heads * 3 * HEAD_DIM)
    head_pieces = jnp.concatenate(
        [
            packed.transpose(1, 0, 2),
            output_weight.reshape(ctx, heads * HEAD_DIM, thin).transpose(0, 2, 1),
        ],
        axis=2,
    )
    hidden_pieces = jnp.concatenate(
        [
            down_weight.reshape(ctx, hidden, thin).transpose(0, 2, 1),
            up_weight.reshape(thin, ctx, hidden).transpose(1, 0, 2),
        ],
        axis=2,
    )

    small = jnp.stack(
        [attention_gain, attention_bias, feedforward_gain, feedforward_bias, output_bias, down_bias]
    ).astype(F32)
    small = jnp.concatenate([small, jnp.zeros((2, thin), F32)])
    def own_columns(vector):
        return lax.dynamic_index_in_dim(vector.reshape(ctx, -1), here, 0, keepdims=False)

    query_shift = own_columns(query_bias).reshape(heads, HEAD_DIM)
    value_shift = own_columns(value_bias).reshape(heads, HEAD_DIM)
    qkv_shift = jnp.stack([query_shift, jnp.zeros_like(query_shift), value_shift], axis=1)
    shifts = jnp.concatenate([qkv_shift.reshape(-1), own_columns(up_bias)])
    other_shifts = swap(shifts, "tp", 1)
    wide = heads * 3 * HEAD_DIM
    qkv_shift = jnp.concatenate([shifts[:wide], other_shifts[:wide]]).astype(F32)
    rise_shift = jnp.concatenate([shifts[wide:], other_shifts[wide:]]).astype(F32)

    ones, head_weights, hidden_block, table = front(
        tokens, head_pieces, hidden_pieces, small, ctx, dp
    )
    head_weights = head_weights.reshape(model_width, -1)
    hidden_weights = lax.all_gather(
        hidden_block.reshape(ctx * thin, -1), "dp", axis=0, tiled=True
    )
    qkv, mixed, log_total, grads_in, residual, input_two, head_whole = attend(
        ones, head_weights, qkv_shift[None], cotangent, tokens, table, 2 * heads, ctx
    )
    _, hid, _, hidden_both, residual_grad, branch_grad, vectors, rise_bias, fall_weight = (
        feed_forward(input_two, grads_in, hidden_weights, rise_shift[None], residual, table, ctx)
    )
    hidden_rows = over_dp(hidden_both)

    _, qkv_grads, low_columns, head_both = attend_back(
        branch_grad, head_whole, qkv, mixed, log_total, hid, fall_weight, ones, residual, table, ctx
    )
    head_both, hidden_rows = lax.optimization_barrier((head_both, hidden_rows))
    head_rows = over_dp(head_both)
    outputs, input_grads, firsts, qkv_bias, fall_grad, rise_grad = first_back(
        qkv_grads,
        head_whole,
        hid,
        fall_weight,
        low_columns,
        residual,
        residual_grad,
        tokens,
        table,
        hidden_rows,
        ctx,
    )
    biases = jnp.concatenate(
        [rise_bias.reshape(2, 1, hidden), qkv_bias.reshape(2, 1, wide)], axis=2
    )
    query_grad, key_grad, value_grad, out_grad, features, totals = end(
        head_rows, vectors, firsts, biases, heads, ctx, dp
    )
    totals = totals[:, 0]
    qkv_bias = totals[:, hidden:].reshape(ctx * heads, 3, HEAD_DIM)
    return (
        outputs,
        input_grads,
        features[4],
        features[5],
        features[0],
        features[1],
        query_grad,
        qkv_bias[:, 0].reshape(-1),
        key_grad,
        value_grad,
        qkv_bias[:, 2].reshape(-1),
        out_grad,
        features[2],
        rise_grad,
        totals[:, :hidden].reshape(-1),
        fall_grad,
        features[3],
    )


def solution(mesh):
    placed = (
        P("dp", "ctx", None),
        P("dp", "ctx", None),
        P(("dp", "ctx")),
        P(("dp", "ctx")),
        P(("dp", "ctx")),
        P(("dp", "ctx")),
        P(("dp", "ctx"), "tp"),
        P("tp"),
        P(("dp", "ctx"), "tp"),
        P(("dp", "ctx"), "tp"),
        P("tp"),
        P("tp", ("dp", "ctx")),
        P(("dp", "ctx")),
        P(("dp", "ctx"), "tp"),
        P("tp"),
        P("tp", ("dp", "ctx")),
        P(("dp", "ctx")),
    )
    return jax.shard_map(
        body,
        mesh=mesh,
        in_specs=placed,
        out_specs=(
            P("dp", "ctx", None),
            P("dp", "ctx", None),
            P(("dp", "ctx")),
            P(("dp", "ctx")),
            P(("dp", "ctx")),
            P(("dp", "ctx")),
            P(("dp", "ctx"), "tp"),
            P("tp"),
            P(("dp", "ctx"), "tp"),
            P(("dp", "ctx"), "tp"),
            P("tp"),
            P("tp", ("dp", "ctx")),
            P(("dp", "ctx")),
            P(("dp", "ctx"), "tp"),
            P("tp"),
            P("tp", ("dp", "ctx")),
            P(("dp", "ctx")),
        ),
        check_vma=False,
    )
```

```python
import functools

import jax
import jax.numpy as jnp
from jax import lax
from jax.experimental import pallas as pl
from jax.experimental.pallas import tpu as pltpu
from jax.sharding import PartitionSpec as P

HEAD_DIM = 128
EPSILON = 1e-05
NEGATIVE = -1e30
F32 = jnp.float32
BF16 = jnp.bfloat16
MESH = pl.DeviceIdType.MESH


def product(former, latter):
    return jnp.dot(former, latter, preferred_element_type=F32)


def inner(former, latter):
    return lax.dot_general(former, latter, (((0,), (0,)), ((), ())), preferred_element_type=F32)


def across(former, latter):
    return lax.dot_general(former, latter, (((1,), (1,)), ((), ())), preferred_element_type=F32)


def normalize(values):
    average = jnp.mean(values, axis=-1, keepdims=True)
    centred = values - average
    spread = lax.rsqrt(jnp.mean(centred * centred, axis=-1, keepdims=True) + EPSILON)
    return (centred * spread, spread)


def norm_back(gradient, normed, spread):
    first_mean = jnp.mean(gradient, axis=-1, keepdims=True)
    second_mean = jnp.mean(gradient * normed, axis=-1, keepdims=True)
    return spread * (gradient - first_mean - normed * second_mean)


def swap(value, axis, mask):
    size = lax.axis_size(axis)
    return lax.ppermute(value, axis, [(i, i ^ mask) for i in range(size)])


def over_dp(both):
    return lax.psum_scatter(both, "dp", scatter_dimension=0, tiled=True)


def rows_of(here, block, size):
    return pl.multiple_of(lax.bitwise_xor(here, block) * size, size)


class Links:
    def __init__(self, count, half):
        self.count, self.half = count, half
        self.bits = (count - 1).bit_length()
        self.pairs = [(i, part) for i in range(1, count) for part in (0, 1)]
        self.slot = {pair: n for n, pair in enumerate(self.pairs)}

    def block(self, i, part):
        if part == 0:
            return i
        return sum(((i >> b) & 1) << (self.bits - 1 - b) for b in range(self.bits))

    def top(self, i):
        return 1 << (i.bit_length() - 1)

    def near(self, i):
        return i ^ self.top(i)

    def given(self, i):
        return [j for j in range(self.count - 1, 0, -1) if self.near(j) == i]

    def far(self, i, part):
        mask = self.block(self.top(i), part)
        return {"ctx": lax.bitwise_xor(lax.axis_index("ctx"), mask)}

    def start_row(self, i, part):
        return (2 * self.block(i, part) + part) * self.half

    def rows(self, ref, i, part):
        return ref.at[pl.ds(self.start_row(i, part), self.half)]

    def greet(self, others=(), masks=None):
        barrier = pltpu.get_barrier_semaphore()
        masks = [1 << bit for bit in range(self.bits)] if masks is None else masks
        partners = [{"ctx": lax.bitwise_xor(lax.axis_index("ctx"), mask)} for mask in masks]
        partners += list(others)
        for partner in partners:
            pl.semaphore_signal(barrier, 1, device_id=partner, device_id_type=MESH)
        pl.semaphore_wait(barrier, len(partners))

    def sharing(self, own_ref, full_ref, send_sem, recv_sem):
        copies = {}
        for i, part in self.pairs:
            near = self.near(i)
            source = (
                own_ref.at[pl.ds(part * self.half, self.half)]
                if near == 0
                else self.rows(full_ref, near, part)
            )
            n = self.slot[(i, part)]
            copies[(i, part)] = pltpu.make_async_remote_copy(
                src_ref=source,
                dst_ref=self.rows(full_ref, i, part),
                send_sem=send_sem.at[n],
                recv_sem=recv_sem.at[n],
                device_id=self.far(i, part),
                device_id_type=MESH,
            )
        return copies

    def summing(self, send_ref, recv_ref, send_sem, recv_sem):
        copies = {}
        for i, part in self.pairs:
            n = self.slot[(i, part)]
            copies[(i, part)] = pltpu.make_async_remote_copy(
                src_ref=send_ref.at[n],
                dst_ref=recv_ref.at[n],
                send_sem=send_sem.at[n],
                recv_sem=recv_sem.at[n],
                device_id=self.far(i, part),
                device_id_type=MESH,
            )
        return copies

    def pass_on(self, copies, arrived, own=False):
        for i, part in self.pairs:
            if self.near(i) == arrived:
                copies[(i, part)].start()

    def loads(self, ref, buffer, i, sem, base):
        return [
            pltpu.make_async_copy(
                self.rows(ref, i, part),
                buffer.at[pl.ds(part * self.half, self.half)],
                sem.at[base + part],
            )
            for part in (0, 1)
        ]

    def terms(self, i, columns, width, kept_v, send_v):
        tile = min(512, width)

        def step(n, _):
            at = pl.ds(pl.multiple_of(n * tile, tile), tile)
            term = columns(at)
            for part in (0, 1):
                piece = term[part * self.half : (part + 1) * self.half]
                if i < self.count // 2:
                    kept_v[2 * i + part, :, at] = piece
                else:
                    send_v[self.slot[(i, part)], :, at] = piece.astype(BF16)
            return 0

        lax.fori_loop(0, width // tile, step, 0)

    def combine(self, copies, kept_ref, send_ref, recv_ref, first, last, final=None, then=None):
        for i in range(first, last - 1, -1):
            for part in (0, 1):
                for j in self.given(i):
                    copies[(j, part)].wait_recv()
                chunk = min(32, self.half)

                def add(step, _, i=i, part=part):
                    at = pl.ds(pl.multiple_of(step * chunk, chunk), chunk)
                    value = kept_ref[2 * i + part, at, :]
                    for j in self.given(i):
                        value = value + recv_ref[self.slot[(j, part)], at, :].astype(F32)
                    if i == 0:
                        to = pl.ds(pl.multiple_of(part * self.half + step * chunk, chunk), chunk)
                        final(part, at, to, value)
                    else:
                        send_ref[self.slot[(i, part)], at, :] = value.astype(BF16)
                    return 0

                lax.fori_loop(0, self.half // chunk, add, 0)
                if i:
                    copies[(i, part)].start()
                elif then:
                    then(part)


def weight_grads(partner, rows_v, columns_v, theirs_v, came_v, results, send_sem, recv_sem, store_sem):
    tile = 512
    width = rows_v.shape[1]
    own = columns_v.shape[1] // 2

    def place(m):
        return pl.ds(pl.multiple_of(m * tile, tile), tile)

    def swap_tile(m):
        return pltpu.make_async_remote_copy(
            src_ref=theirs_v.at[place(m)],
            dst_ref=came_v.at[place(m)],
            send_sem=send_sem.at[m],
            recv_sem=recv_sem.at[m],
            device_id=partner,
            device_id_type=MESH,
        )

    def store_tile(m):
        copies, column = [], 0
        for n, result in enumerate(results):
            count = result.shape[1]
            copies.append(
                pltpu.make_async_copy(
                    came_v.at[place(m), pl.ds(column, count)], result.at[place(m)], store_sem[n].at[m]
                )
            )
            column += count
        return copies

    def first(m, _):
        term = inner(rows_v[:, place(m)], columns_v[:, own : 2 * own])
        theirs_v[place(m), :] = term.astype(BF16)
        swap_tile(m).start()
        return 0

    def second(m, _):
        swap_tile(m).wait_recv()
        term = inner(rows_v[:, place(m)], columns_v[:, 0:own])
        came_v[place(m), :] = (term + came_v[place(m), :].astype(F32)).astype(BF16)
        for copy in store_tile(m):
            copy.start()
        return 0

    def end(m, _):
        for copy in store_tile(m):
            copy.wait()
        swap_tile(m).wait_send()
        return 0

    lax.fori_loop(0, width // tile, first, 0)
    lax.fori_loop(0, width // tile, second, 0)
    return lambda: lax.fori_loop(0, width // tile, end, 0)


def feed_forward_kernel(
    links,
    own_ref,
    grads_ref,
    both_ref,
    shift_ref,
    residual_ref,
    table_ref,
    full_ref,
    hid_ref,
    slope_ref,
    both_grad_ref,
    late_grad_ref,
    back_ref,
    branch_ref,
    vector_ref,
    bias_ref,
    fall_ref,
    rise_big,
    fall_big,
    rows_v,
    grads_v,
    hid_v,
    slope_v,
    kept_v,
    send_v,
    recv_v,
    theirs_v,
    came_v,
    load_sem,
    store_sem,
    pair_send,
    pair_recv,
    grad_send,
    grad_recv,
    grad_store,
    share_send,
    share_recv,
    sum_send,
    sum_recv,
):
    half, count = links.half, links.count
    width, hidden = own_ref.shape[1], hid_v.shape[1]
    length = 2 * half * count
    rise_v = rise_big.at[pl.ds(0, width), pl.ds(0, hidden)]
    fall_v = fall_big.at[pl.ds(0, width), pl.ds(0, hidden)]
    own_half = pl.ds(0, hidden // 2)
    other_half = pl.ds(hidden // 2, hidden // 2)
    partner = {"tp": 1 - lax.axis_index("tp")}
    links.greet([partner])
    swaps = [
        pltpu.make_async_remote_copy(
            src_ref=both_ref.at[:, pl.ds(n * (hidden // 2), hidden // 2)],
            dst_ref=target.at[:, other_half],
            send_sem=pair_send.at[n],
            recv_sem=pair_recv.at[n],
            device_id=partner,
            device_id_type=MESH,
        )
        for n, target in enumerate((fall_v, rise_v))
    ]
    for copy in swaps:
        copy.start()
    shares = links.sharing(own_ref, full_ref, share_send, share_recv)
    sums = links.summing(send_v, recv_v, sum_send, sum_recv)
    links.pass_on(shares, 0)
    keep = pltpu.make_async_copy(rows_v, full_ref.at[pl.ds(0, 2 * half)], load_sem.at[0])
    first = pltpu.make_async_copy(own_ref, rows_v, load_sem.at[1])
    first.start()
    rise = pltpu.make_async_copy(both_ref.at[:, other_half], rise_v.at[:, own_half], load_sem.at[2])
    rise.start()
    fall = pltpu.make_async_copy(both_ref.at[:, own_half], fall_v.at[:, own_half], load_sem.at[3])
    fall.start()
    bias_ref[...] = jnp.zeros_like(bias_ref)

    grad_loads = links.loads(grads_ref, grads_v, 0, load_sem, 4)
    for copy in grad_loads:
        copy.start()
    stores = []
    tile = min(512, hidden)
    for i in range(count):
        if i == 0:
            first.wait()
            keep.start()
            rise.wait()
            fall.wait()
            for copy in swaps:
                copy.wait_recv()
            keep_fall = pltpu.make_async_copy(fall_v, fall_ref, store_sem.at[4])
            keep_fall.start()
        else:
            for part in (0, 1):
                shares[(i, part)].wait_recv()
            links.pass_on(shares, i)
            if i == 1:
                keep.wait()
            row_loads = links.loads(full_ref, rows_v, i, load_sem, 8)
            for copy in row_loads:
                copy.start()
            for copy in row_loads:
                copy.wait()
        for copy in grad_loads + stores:
            copy.wait()

        def rise_step(step, _, i=i):
            at = pl.ds(pl.multiple_of(step * tile, tile), tile)
            pre = product(rows_v[...], rise_v[:, at]) + shift_ref[0:1, at]
            back = product(grads_v[...], fall_v[:, at])
            cumulative = 0.5 * (1.0 + lax.erf(pre * 0.7071067811865476))
            density = jnp.exp(-0.5 * pre * pre) * 0.3989422804014327
            hid_v[:, at] = (pre * cumulative).astype(BF16)
            slope = (back * (cumulative + pre * density)).astype(BF16)
            slope_v[:, at] = slope
            bias_ref[0:1, at] += jnp.sum(slope.astype(F32), axis=0, keepdims=True)
            return 0

        lax.fori_loop(0, hidden // tile, rise_step, 0)
        if i + 1 < count:
            grad_loads = links.loads(grads_ref, grads_v, i + 1, load_sem, 4)
            for copy in grad_loads:
                copy.start()
        stores = []
        for n, (buffer, ref) in enumerate(((hid_v, hid_ref), (slope_v, slope_ref))):
            for part in (0, 1):
                copy = pltpu.make_async_copy(
                    buffer.at[pl.ds(part * half, half)],
                    links.rows(ref, i, part),
                    store_sem.at[2 * n + part],
                )
                copy.start()
                stores.append(copy)

        links.terms(i, lambda at: across(slope_v[...], rise_v[at, :]), width, kept_v, send_v)
        if i >= count // 2:
            for part in (0, 1):
                sums[(i, part)].start()
    for copy in stores:
        copy.wait()
    keep_fall.wait()
    rows_big = rise_big.at[pl.ds(0, length), pl.ds(0, width)]
    columns_big = fall_big.at[pl.ds(0, length), pl.ds(0, hidden)]
    ends = []
    quarter = hidden // 4
    results = (
        (both_grad_ref.at[:, own_half],),
        (both_grad_ref.at[:, pl.ds(hidden // 2, quarter)], late_grad_ref),
    )
    stores = ((grad_store.at[0],), (grad_store.at[1], grad_store.at[2]))
    for n, (left, right) in enumerate(((full_ref, slope_ref), (grads_ref, hid_ref))):
        lefts = pltpu.make_async_copy(left, rows_big, load_sem.at[0])
        rights = pltpu.make_async_copy(right, columns_big, load_sem.at[1])
        lefts.start()
        rights.start()
        for end in ends:
            end()
        lefts.wait()
        rights.wait()
        ends = [
            weight_grads(
                partner,
                rows_big,
                columns_big,
                theirs_v,
                came_v.at[n],
                results[n],
                grad_send.at[n],
                grad_recv.at[n],
                stores[n],
            )
        ]
        if n == 0:
            links.combine(sums, kept_v, send_v, recv_v, count // 2 - 1, 1)
            finals = [
                pltpu.make_async_copy(
                    residual_ref.at[pl.ds(part * half, half)], kept_v.at[2 + part], load_sem.at[2 + part]
                )
                for part in (0, 1)
            ]
            finals.append(
                pltpu.make_async_copy(grads_ref.at[pl.ds(0, 2 * half)], rows_v, load_sem.at[4])
            )
            for copy in finals:
                copy.start()
    for copy in finals:
        copy.wait()
    vector_ref[...] = jnp.zeros_like(vector_ref)
    results = []

    def last(part, at, to, second):
        normed, spread = normalize(kept_v[2 + part, at, :])
        incoming = rows_v[to, :].astype(F32)
        back = incoming + norm_back(second * table_ref[2:3, :], normed, spread)
        branch = back.astype(BF16)
        kept_v[part, at, :] = back
        rows_v[to, :] = branch
        for n, value in enumerate((second * normed, second, branch.astype(F32), incoming)):
            vector_ref[n : n + 1, :] += jnp.sum(value, axis=0, keepdims=True)

    def store_part(part):
        rows = pl.ds(part * half, half)
        for n, (source, target) in enumerate(
            ((kept_v.at[part], back_ref.at[rows]), (rows_v.at[rows], branch_ref.at[rows]))
        ):
            copy = pltpu.make_async_copy(source, target, load_sem.at[2 * part + n])
            copy.start()
            results.append(copy)

    links.combine(sums, kept_v, send_v, recv_v, 0, 0, last, store_part)
    for end in ends:
        end()
    for copy in results:
        copy.wait()
    for copy in swaps:
        copy.wait_send()
    for pair in links.pairs:
        shares[pair].wait_send()
        sums[pair].wait_send()


def feed_forward(own, grads, both_weights, shift, residual, table, count):
    rows, width = own.shape
    hidden = both_weights.shape[1]
    length = rows * count
    links = Links(count, rows // 2)
    half, copies = links.half, len(links.pairs)
    anywhere = pl.BlockSpec(memory_space=pl.ANY)
    inside = pl.BlockSpec(memory_space=pltpu.VMEM)
    dma = pltpu.SemaphoreType.DMA
    return pl.pallas_call(
        functools.partial(feed_forward_kernel, links),
        out_shape=(
            jax.ShapeDtypeStruct((length, width), BF16),
            jax.ShapeDtypeStruct((length, hidden), BF16),
            jax.ShapeDtypeStruct((length, hidden), BF16),
            jax.ShapeDtypeStruct((width, hidden * 3 // 4), BF16),
            jax.ShapeDtypeStruct((width, hidden // 4), BF16),
            jax.ShapeDtypeStruct((rows, width), F32),
            jax.ShapeDtypeStruct((rows, width), BF16),
            jax.ShapeDtypeStruct((8, width), F32),
            jax.ShapeDtypeStruct((1, hidden), F32),
            jax.ShapeDtypeStruct((width, hidden), BF16),
        ),
        in_specs=[anywhere, anywhere, anywhere, inside, anywhere, inside],
        out_specs=(anywhere,) * 7 + (inside, inside, anywhere),
        scratch_shapes=[
            pltpu.VMEM((max(width, length), max(width, hidden)), BF16),
            pltpu.VMEM((max(width, length), hidden), BF16),
            pltpu.VMEM((rows, width), BF16),
            pltpu.VMEM((rows, width), BF16),
            pltpu.VMEM((rows, hidden), BF16),
            pltpu.VMEM((rows, hidden), BF16),
            pltpu.VMEM((count, half, width), F32),
            pltpu.VMEM((copies, half, width), BF16),
            pltpu.VMEM((copies, half, width), BF16),
            pltpu.VMEM((width, hidden // 2), BF16),
            pltpu.VMEM((2, width, hidden // 2), BF16),
            dma((10,)),
            dma((5,)),
            dma((2,)),
            dma((2,)),
            dma((3, width // 512)),
            dma((3, width // 512)),
            dma((3, width // 512)),
            dma((copies,)),
            dma((copies,)),
            dma((copies,)),
            dma((copies,)),
        ],
        compiler_params=pltpu.CompilerParams(
            collective_id=3, has_side_effects=True, vmem_limit_bytes=63 * 1024 * 1024
        ),
        cost_estimate=pl.CostEstimate(
            flops=10 * length * width * hidden,
            bytes_accessed=length * width * 8 + width * hidden * 4 + length * hidden * 4,
            transcendentals=length * hidden * 2,
        ),
        name="feed_forward",
    )(own, grads, both_weights, shift, residual, table)


def greet_all(partners):
    barrier = pltpu.get_barrier_semaphore()
    for partner in partners:
        pl.semaphore_signal(barrier, 1, device_id=partner, device_id_type=MESH)
    pl.semaphore_wait(barrier, len(partners))


def others(axis, count):
    return [{axis: lax.bitwise_xor(lax.axis_index(axis), mask)} for mask in range(1, count)]


def axis_bits(axis, size):
    return [
        {axis: lax.bitwise_xor(lax.axis_index(axis), 1 << bit)}
        for bit in range((size - 1).bit_length())
    ]


def piece_copies(count, source, target_ref, send_sem, recv_sem):
    here = lax.axis_index("ctx")
    return [
        pltpu.make_async_remote_copy(
            src_ref=source(lax.bitwise_xor(here, mask)),
            dst_ref=target_ref.at[here],
            send_sem=send_sem.at[mask - 1],
            recv_sem=recv_sem.at[mask - 1],
            device_id={"ctx": lax.bitwise_xor(here, mask)},
            device_id_type=MESH,
        )
        for mask in range(1, count)
    ]


class Line:
    def __init__(self, whole_ref, depth, send_sem, recv_sem):
        self.whole, self.depth = whole_ref, depth
        self.send_sem, self.recv_sem = send_sem, recv_sem
        self.me = lax.axis_index("dp")

    def copy(self, way, step, block):
        block = jnp.clip(block, 0, self.depth - 1)
        target = jnp.clip(self.me + way, 0, self.depth - 1)
        n = 0 if way > 0 else 1
        return pltpu.make_async_remote_copy(
            src_ref=self.whole.at[block],
            dst_ref=self.whole.at[block],
            send_sem=self.send_sem.at[n, step - 1],
            recv_sem=self.recv_sem.at[n, step - 1],
            device_id={"dp": target},
            device_id_type=MESH,
        )

    def sends(self, step, act):
        me, depth = self.me, self.depth

        @pl.when((me + 1 < depth) & (me - step + 1 >= 0))
        def _():
            act(self.copy(1, step, me - step + 1))

        @pl.when((me >= 1) & (me + step - 1 < depth))
        def _():
            act(self.copy(-1, step, me + step - 1))

    def start(self, step):
        self.sends(step, lambda copy: copy.start())

    def arrive(self, step):
        @pl.when(self.me - step >= 0)
        def _():
            self.copy(1, step, self.me - step).wait_recv()

        @pl.when(self.me + step < self.depth)
        def _():
            self.copy(-1, step, self.me + step).wait_recv()

    def finish(self):
        for step in range(1, self.depth):
            self.sends(step, lambda copy: copy.wait_send())


def front_kernel(
    links,
    depth,
    tokens_ref,
    head_pieces_ref,
    pieces_ref,
    small_ref,
    normed_ref,
    head_ref,
    block_ref,
    table_ref,
    rows_v,
    normed_v,
    head_v,
    piece_v,
    shards_v,
    load_sem,
    store_sem,
    share_send,
    share_recv,
    head_send,
    head_recv,
    piece_send,
    piece_recv,
    line_send,
    line_recv,
    shard_send,
    shard_recv,
):
    count, half = links.count, links.half
    size = 2 * half
    here, layer = lax.axis_index("ctx"), lax.axis_index("dp")
    shard = here * depth + layer
    thin = small_ref.shape[1]
    own_ref = tokens_ref.at[lax.axis_index("tp")]
    greet_all(others("ctx", count) + others("dp", depth))
    heads = piece_copies(
        count, lambda i: head_pieces_ref.at[i], head_ref.at[layer], head_send, head_recv
    )
    pieces = piece_copies(
        count, lambda i: pieces_ref.at[i], block_ref, piece_send, piece_recv
    )
    for copy in heads:
        copy.start()
    own_pieces = [
        pltpu.make_async_copy(head_pieces_ref.at[here], head_v, load_sem.at[2]),
        pltpu.make_async_copy(pieces_ref.at[here], piece_v, load_sem.at[0]),
    ]
    for copy in own_pieces:
        copy.start()
    first = pltpu.make_async_copy(own_ref, rows_v.at[pl.ds(0, size)], load_sem.at[1])
    first.start()
    shards_v[shard] = small_ref[...]
    for bit, device in enumerate(axis_bits("dp", depth) + axis_bits("ctx", count)):
        reach = 1 << bit
        mine = pl.ds(shard // reach * reach, reach)
        theirs = pl.ds((shard // reach ^ 1) * reach, reach)
        copies = [
            pltpu.make_async_remote_copy(
                src_ref=shards_v.at[mine],
                dst_ref=shards_v.at[place],
                send_sem=shard_send.at[bit],
                recv_sem=shard_recv.at[bit],
                device_id=device,
                device_id_type=MESH,
            )
            for place in (mine, theirs)
        ]
        copies[0].start()
        copies[0].wait_send()
        copies[1].wait_recv()
    shares = links.sharing(own_ref, rows_v, share_send, share_recv)
    links.pass_on(shares, 0)
    line = Line(head_ref, depth, line_send, line_recv)
    own_stores = [
        pltpu.make_async_copy(head_v, head_ref.at[layer, here], load_sem.at[2]),
        pltpu.make_async_copy(piece_v, block_ref.at[here], load_sem.at[0]),
    ]
    for load, store in zip(own_pieces, own_stores):
        load.wait()
        store.start()
    for copy in heads:
        copy.wait()
    own_stores[0].wait()
    line.start(1)
    for copy in pieces:
        copy.start()
    for c in range(count):
        for d in range(depth):
            n = d * count + c
            table_ref[:, n * thin : (n + 1) * thin] = shards_v[c * depth + d]
    chunk = min(32, half)
    stores = []
    for i in range(max(count, depth)):
        if 0 < i < depth:
            line.arrive(i)
            if i + 1 < depth:
                line.start(i + 1)
        if i >= count:
            continue
        if i == 0:
            first.wait()
        else:
            for part in (0, 1):
                shares[(i, part)].wait_recv()
            links.pass_on(shares, i)
        for part in (0, 1):
            base = links.start_row(i, part)

            def norm(step, _, base=base):
                at = pl.ds(pl.multiple_of(base + step * chunk, chunk), chunk)
                normed = normalize(rows_v[at, :].astype(F32))[0]
                normed_v[at, :] = (normed * table_ref[0:1, :] + table_ref[1:2, :]).astype(BF16)
                return 0

            lax.fori_loop(0, half // chunk, norm, 0)
            store = pltpu.make_async_copy(
                links.rows(normed_v, i, part), links.rows(normed_ref, i, part), store_sem.at[2 * i + part]
            )
            store.start()
            stores.append(store)
    for copy in stores + pieces + own_stores[1:]:
        copy.wait()
    line.finish()
    for pair in links.pairs:
        shares[pair].wait_send()


def front(tokens, head_pieces, pieces, small, count, depth):
    _, rows, width = tokens.shape
    length = rows * count
    links = Links(count, rows // 2)
    copies = len(links.pairs)
    bits = (count - 1).bit_length() + (depth - 1).bit_length()
    anywhere = pl.BlockSpec(memory_space=pl.ANY)
    inside = pl.BlockSpec(memory_space=pltpu.VMEM)
    dma = pltpu.SemaphoreType.DMA
    return pl.pallas_call(
        functools.partial(front_kernel, links, depth),
        out_shape=(
            jax.ShapeDtypeStruct((length, width), BF16),
            jax.ShapeDtypeStruct((depth, *head_pieces.shape), BF16),
            jax.ShapeDtypeStruct(pieces.shape, BF16),
            jax.ShapeDtypeStruct((8, width), F32),
        ),
        in_specs=[anywhere, anywhere, anywhere, inside],
        out_specs=(anywhere, anywhere, anywhere, inside),
        scratch_shapes=[
            pltpu.VMEM((length, width), BF16),
            pltpu.VMEM((length, width), BF16),
            pltpu.VMEM(head_pieces.shape[1:], BF16),
            pltpu.VMEM(pieces.shape[1:], BF16),
            pltpu.VMEM((count * depth, *small.shape), F32),
            dma((3,)),
            dma((2 * count,)),
            dma((copies,)),
            dma((copies,)),
            dma((count - 1,)),
            dma((count - 1,)),
            dma((count - 1,)),
            dma((count - 1,)),
            dma((2, depth - 1)),
            dma((2, depth - 1)),
            dma((bits,)),
            dma((bits,)),
        ],
        compiler_params=pltpu.CompilerParams(
            collective_id=1, has_side_effects=True, vmem_limit_bytes=40 * 1024 * 1024
        ),
        cost_estimate=pl.CostEstimate(
            flops=20 * length * width, bytes_accessed=120000000, transcendentals=0
        ),
        name="front",
    )(tokens, head_pieces, pieces, small)


def end_kernel(
    count,
    depth,
    heads,
    rows_ref,
    vectors_ref,
    firsts_ref,
    biases_ref,
    query_ref,
    key_ref,
    value_ref,
    out_ref,
    fall_ref,
    features_ref,
    totals_ref,
    block_v,
    shards_v,
    pair_v,
    landing_v,
    bias_v,
    load_sem,
    piece_send,
    piece_recv,
    shard_send,
    shard_recv,
    bias_send,
    bias_recv,
    total_send,
    total_recv,
):
    here, layer = lax.axis_index("ctx"), lax.axis_index("dp")
    shard = layer * count + here
    partner = {"tp": 1 - lax.axis_index("tp")}
    thin = query_ref.shape[0]
    wide = heads * 3 * HEAD_DIM
    low, high = (count - 1).bit_length(), (depth - 1).bit_length()
    greet_all([partner] + others("ctx", count) + others("dp", depth))
    pieces = piece_copies(
        count,
        lambda i: rows_ref.at[pl.ds(pl.multiple_of(i * thin, thin), thin)],
        block_v,
        piece_send,
        piece_recv,
    )
    pieces.append(
        pltpu.make_async_copy(
            rows_ref.at[pl.ds(pl.multiple_of(here * thin, thin), thin)], block_v.at[here], load_sem.at[0]
        )
    )
    for copy in pieces:
        copy.start()
    for n in range(count * depth):
        at = slice(n * thin, (n + 1) * thin)
        shards_v[n, 0:4, :] = vectors_ref[0:4, at]
        shards_v[n, 4:8, :] = firsts_ref[0:4, at]

    def exchange(source, target, device, send, recv):
        copy = pltpu.make_async_remote_copy(
            src_ref=source,
            dst_ref=target,
            send_sem=send,
            recv_sem=recv,
            device_id=device,
            device_id_type=MESH,
        )
        copy.start()
        return copy

    bias_v[0] = biases_ref[0]
    bias_v[1] = biases_ref[1]
    stage = [
        exchange(shards_v, pair_v, partner, shard_send.at[low + high], shard_recv.at[low + high]),
        exchange(bias_v.at[1], bias_v.at[2], partner, bias_send.at[high], bias_recv.at[high]),
    ]
    for copy in stage:
        copy.wait()
    shards_v[...] += pair_v[...]
    bias_v[0] += bias_v[2]
    totals = []
    devices = axis_bits("ctx", count) + axis_bits("dp", depth)
    for bit in range(low + high - 1, -1, -1):
        reach = 1 << bit
        mine = shard // reach * reach
        theirs = (shard // reach ^ 1) * reach
        stage = [
            exchange(
                shards_v.at[pl.ds(theirs, reach)],
                landing_v.at[pl.ds(reach, reach)],
                devices[bit],
                shard_send.at[bit],
                shard_recv.at[bit],
            )
        ]
        if bit >= low:
            n = bit - low
            stage.append(
                exchange(bias_v.at[0], bias_v.at[3 + n], devices[bit], bias_send.at[n], bias_recv.at[n])
            )
        for copy in stage:
            copy.wait()
        shards_v[pl.ds(mine, reach)] += landing_v[reach : 2 * reach]
        if bit >= low:
            bias_v[0] += bias_v[3 + bit - low]
        if bit == low:
            totals_ref[here] = bias_v[0]
            totals = [
                exchange(
                    bias_v.at[0], totals_ref.at[here], device, total_send.at[n], total_recv.at[n]
                )
                for n, device in enumerate(others("ctx", count))
            ]
    features_ref[...] = shards_v[shard]
    for copy in pieces + totals:
        copy.wait()
    for c in range(count):
        for j in range(heads):
            to = slice((c * heads + j) * HEAD_DIM, (c * heads + j + 1) * HEAD_DIM)
            for n, ref in enumerate((query_ref, key_ref, value_ref)):
                column = (3 * j + n) * HEAD_DIM
                ref[:, to] = block_v[c, :, column : column + HEAD_DIM].astype(F32)
        rows = slice(c * heads * HEAD_DIM, (c + 1) * heads * HEAD_DIM)
        out_ref[rows, :] = block_v[c, :, wide : wide + heads * HEAD_DIM].astype(F32).T
        fall_ref[c] = block_v[c, :, wide + heads * HEAD_DIM :].astype(F32).T


def end(rows, vectors, firsts, biases, heads, count, depth):
    low, high = (count - 1).bit_length(), (depth - 1).bit_length()
    thin = rows.shape[0] // count
    columns = rows.shape[1]
    local = count * heads * HEAD_DIM
    inside = pl.BlockSpec(memory_space=pltpu.VMEM)
    dma = pltpu.SemaphoreType.DMA
    shards = (count * depth, 8, thin)
    return pl.pallas_call(
        functools.partial(end_kernel, count, depth, heads),
        out_shape=(
            jax.ShapeDtypeStruct((thin, local), F32),
            jax.ShapeDtypeStruct((thin, local), F32),
            jax.ShapeDtypeStruct((thin, local), F32),
            jax.ShapeDtypeStruct((local, thin), F32),
            jax.ShapeDtypeStruct((count, columns - heads * 4 * HEAD_DIM, thin), F32),
            jax.ShapeDtypeStruct((8, thin), F32),
            jax.ShapeDtypeStruct((count, 1, biases.shape[2]), F32),
        ),
        in_specs=[pl.BlockSpec(memory_space=pl.ANY), inside, inside, inside],
        out_specs=(inside,) * 7,
        scratch_shapes=[
            pltpu.VMEM((count, thin, columns), BF16),
            pltpu.VMEM(shards, F32),
            pltpu.VMEM(shards, F32),
            pltpu.VMEM(shards, F32),
            pltpu.VMEM((3 + high, 1, biases.shape[2]), F32),
            dma((1,)),
            dma((count - 1,)),
            dma((count - 1,)),
            dma((low + high + 1,)),
            dma((low + high + 1,)),
            dma((high + 1,)),
            dma((high + 1,)),
            dma((count - 1,)),
            dma((count - 1,)),
        ],
        compiler_params=pltpu.CompilerParams(
            collective_id=7, has_side_effects=True, vmem_limit_bytes=24 * 1024 * 1024
        ),
        cost_estimate=pl.CostEstimate(flops=0, bytes_accessed=40000000, transcendentals=0),
        name="end",
    )(rows, vectors, firsts, biases)


def attend_kernel(
    links,
    heads,
    rows_ref,
    weight_ref,
    shift_ref,
    cotangent_ref,
    tokens_ref,
    table_ref,
    qkv_ref,
    mixed_ref,
    log_ref,
    grads_full_ref,
    residual_ref,
    second_ref,
    whole_ref,
    own_v,
    rows_v,
    weight_v,
    qkv_v,
    mixed_v,
    scores_v,
    kept_v,
    send_v,
    recv_v,
    load_sem,
    store_sem,
    pair_send,
    pair_recv,
    share_send,
    share_recv,
    sum_send,
    sum_recv,
):
    count, half = links.count, links.half
    size = 2 * half
    here = lax.axis_index("ctx")
    core = lax.axis_index("tp")
    partner = {"tp": 1 - core}
    grads_ref = cotangent_ref.at[core]
    narrow = weight_ref.shape[1]
    wide = heads * 3 * HEAD_DIM // 2
    links.greet([partner])
    theirs = pltpu.make_async_remote_copy(
        src_ref=weight_ref,
        dst_ref=weight_v.at[1],
        send_sem=pair_send.at[0],
        recv_sem=pair_recv.at[0],
        device_id=partner,
        device_id_type=MESH,
    )
    theirs.start()
    shares = links.sharing(grads_ref, grads_full_ref, share_send, share_recv)
    sums = links.summing(send_v, recv_v, sum_send, sum_recv)
    links.pass_on(shares, 0)
    ours = pltpu.make_async_copy(weight_ref, weight_v.at[0], load_sem.at[0])
    ours.start()
    own = pltpu.make_async_copy(tokens_ref.at[core], own_v, load_sem.at[4])
    own.start()

    def load(n):
        return pltpu.make_async_copy(
            rows_ref.at[pl.ds(n * size, size)], rows_v.at[n % 2], load_sem.at[2 + n % 2]
        )

    coming = load(0)
    coming.start()
    ours.wait()
    theirs.wait_recv()
    wholes = []
    for core in (0, 1):
        copy = pltpu.make_async_copy(weight_v.at[core], whole_ref.at[core], store_sem.at[core])
        copy.start()
        wholes.append(copy)
    tile = 256 if wide % 256 == 0 else HEAD_DIM
    for n in range(count):
        coming.wait()
        if n + 1 < count:
            coming = load(n + 1)
            coming.start()
        for core in (0, 1):

            def step(m, _, n=n, core=core):
                at = pl.ds(pl.multiple_of(m * tile, tile), tile)
                to = pl.ds(pl.multiple_of(core * wide + m * tile, tile), tile)
                value = product(rows_v[n % 2], weight_v[core, :, at]) + shift_ref[0:1, to]
                qkv_v[n * size : (n + 1) * size, to] = value.astype(BF16)
                return 0

            lax.fori_loop(0, wide // tile, step, 0)
    keep_qkv = pltpu.make_async_copy(qkv_v, qkv_ref, store_sem.at[2])
    keep_qkv.start()
    own_grads = pltpu.make_async_copy(grads_ref, rows_v.at[0], load_sem.at[1])
    own_grads.start()
    keep = pltpu.make_async_copy(rows_v.at[0], grads_full_ref.at[pl.ds(0, size)], load_sem.at[1])

    def one_head(head, _):
        @pl.when(head == heads // 2)
        def _():
            for i in range(1, (count + 1) // 2):
                for part in (0, 1):
                    shares[(i, part)].wait_recv()
                links.pass_on(shares, i)

        attend_forward_head(here, head, size, count, qkv_v, mixed_v, log_ref, scores_v)
        return 0

    lax.fori_loop(0, heads, one_head, 0)
    keep_mixed = pltpu.make_async_copy(mixed_v, mixed_ref, store_sem.at[3])
    keep_mixed.start()
    own_grads.wait()
    keep.start()
    chip = heads * HEAD_DIM // 2
    for i in range(count - 1, -1, -1):

        def out_rows(core, i=i):
            at = slice(core * chip, (core + 1) * chip)
            first = [links.start_row(i, part) for part in (0, 1)]
            return jnp.concatenate([mixed_v[row : row + half, at] for row in first], axis=0)

        links.terms(
            i,
            lambda at: across(out_rows(0), weight_v[0, at, wide:narrow])
            + across(out_rows(1), weight_v[1, at, wide:narrow]),
            residual_ref.shape[1],
            kept_v,
            send_v,
        )
        if i >= count // 2:
            for part in (0, 1):
                sums[(i, part)].start()

    def norm(part, at, to, value):
        residual = own_v[to, :].astype(F32) + (value + table_ref[4:5, :])
        residual_ref[to, :] = residual
        normed = normalize(residual)[0]
        second_ref[to, :] = (normed * table_ref[2:3, :] + table_ref[3:4, :]).astype(BF16)

    own.wait()
    links.combine(sums, kept_v, send_v, recv_v, count // 2 - 1, 0, norm)
    for i in range(1, count):
        for part in (0, 1):
            if i >= (count + 1) // 2:
                shares[(i, part)].wait_recv()
    for copy in wholes + [keep_qkv, keep_mixed, keep]:
        copy.wait()
    theirs.wait_send()
    for pair in links.pairs:
        sums[pair].wait_send()
        shares[pair].wait_send()


def attend_forward_head(here, head, size, blocks, qkv_v, mixed_v, log_ref, scores_v):
    scaling = HEAD_DIM ** (-0.5)
    behind = lax.broadcasted_iota(jnp.int32, (size, size), 1) <= lax.broadcasted_iota(
        jnp.int32, (size, size), 0
    )
    column = pl.multiple_of(head * (3 * HEAD_DIM), HEAD_DIM)
    query_at = pl.ds(column, HEAD_DIM)
    key_at = pl.ds(pl.multiple_of(column + HEAD_DIM, HEAD_DIM), HEAD_DIM)
    value_at = pl.ds(pl.multiple_of(column + 2 * HEAD_DIM, HEAD_DIM), HEAD_DIM)
    head_at = pl.ds(pl.multiple_of(head * HEAD_DIM, HEAD_DIM), HEAD_DIM)
    for i in range(blocks):
        at = pl.ds(rows_of(here, i, size), size)
        queries = qkv_v[at, query_at]
        highest = jnp.full((size, 1), NEGATIVE, F32)
        for j in range(i + 1):
            keys = qkv_v[pl.ds(rows_of(here, j, size), size), key_at]
            scores = across(queries, keys) * scaling
            if j == i:
                scores = jnp.where(behind, scores, NEGATIVE)
            scores_v[:, j * size : (j + 1) * size] = scores
            highest = jnp.maximum(highest, jnp.max(scores, axis=1, keepdims=True))
        row_total = jnp.zeros((size, 1), F32)
        mixed = jnp.zeros((size, HEAD_DIM), F32)
        for j in range(i + 1):
            exponent = jnp.exp(scores_v[:, j * size : (j + 1) * size] - highest)
            row_total = row_total + jnp.sum(exponent, axis=1, keepdims=True)
            values = qkv_v[pl.ds(rows_of(here, j, size), size), value_at]
            mixed = mixed + product(exponent.astype(BF16), values)
        mixed_v[at, head_at] = (mixed / row_total).astype(BF16)
        log_total = jnp.broadcast_to(highest + jnp.log(row_total), (size, HEAD_DIM))
        log_ref[head, :, at] = log_total.T[0:8, :]


def attend(rows, weight, shift, cotangent, tokens, table, heads, count):
    length, width = rows.shape
    size = length // count
    narrow = weight.shape[1]
    columns = heads * 3 * HEAD_DIM
    links = Links(count, size // 2)
    half, copies = links.half, len(links.pairs)
    pairs = heads * length * (length + size) // 2
    anywhere = pl.BlockSpec(memory_space=pl.ANY)
    inside = pl.BlockSpec(memory_space=pltpu.VMEM)
    dma = pltpu.SemaphoreType.DMA
    return pl.pallas_call(
        functools.partial(attend_kernel, links, heads),
        out_shape=(
            jax.ShapeDtypeStruct((length, columns), BF16),
            jax.ShapeDtypeStruct((length, heads * HEAD_DIM), BF16),
            jax.ShapeDtypeStruct((heads, 8, length), F32),
            jax.ShapeDtypeStruct((length, width), BF16),
            jax.ShapeDtypeStruct((size, width), F32),
            jax.ShapeDtypeStruct((size, width), BF16),
            jax.ShapeDtypeStruct((2, width, narrow), BF16),
        ),
        in_specs=[anywhere, anywhere, inside, anywhere, anywhere, inside],
        out_specs=(anywhere, anywhere, inside, anywhere, inside, inside, anywhere),
        scratch_shapes=[
            pltpu.VMEM((size, width), BF16),
            pltpu.VMEM((2, size, width), BF16),
            pltpu.VMEM((2, width, narrow), BF16),
            pltpu.VMEM((length, columns), BF16),
            pltpu.VMEM((length, heads * HEAD_DIM), BF16),
            pltpu.VMEM((size, length), F32),
            pltpu.VMEM((count, half, width), F32),
            pltpu.VMEM((copies, half, width), BF16),
            pltpu.VMEM((copies, half, width), BF16),
            dma((5,)),
            dma((4,)),
            dma((1,)),
            dma((1,)),
            dma((copies,)),
            dma((copies,)),
            dma((copies,)),
            dma((copies,)),
        ],
        compiler_params=pltpu.CompilerParams(
            collective_id=2, has_side_effects=True, vmem_limit_bytes=60 * 1024 * 1024
        ),
        cost_estimate=pl.CostEstimate(
            flops=pairs * HEAD_DIM * 8 + 2 * length * width * heads * HEAD_DIM * 4,
            bytes_accessed=length * width * 8,
            transcendentals=pairs,
        ),
        name="attend",
    )(rows, weight, shift, cotangent, tokens, table)


def attend_back_kernel(
    links,
    heads,
    own_ref,
    weight_ref,
    qkv_ref,
    mixed_ref,
    log_ref,
    hid_ref,
    fall_ref,
    first_ref,
    residual_ref,
    late_ref,
    table_ref,
    full_ref,
    result_ref,
    low_ref,
    late_grad_ref,
    residual_v,
    weight_v,
    qkv_v,
    mixed_v,
    big_v,
    shared_v,
    came_v,
    grad_v,
    rows_v,
    hid_v,
    key_v,
    value_v,
    kept_v,
    send_v,
    recv_v,
    load_sem,
    grad_send,
    grad_recv,
    grad_store,
    share_send,
    share_recv,
    sum_send,
    sum_recv,
):
    half, count = links.half, links.count
    size = 2 * half
    here = lax.axis_index("ctx")
    chip = weight_v.shape[2]
    wide = heads * 3 * HEAD_DIM // 2
    narrow = residual_v.shape[1]
    middle = hid_v.shape[2] // 2
    partner = {"tp": 1 - lax.axis_index("tp")}
    links.greet([partner])
    shares = links.sharing(own_ref, full_ref, share_send, share_recv)
    sums = links.summing(send_v, recv_v, sum_send, sum_recv)
    links.pass_on(shares, 0)
    falls = [shared_v.at[pl.ds(n * narrow, narrow), pl.ds(0, middle)] for n in (0, 1)]
    theirs_v = shared_v.at[pl.ds(0, big_v.shape[1])]
    late_v = shared_v.at[pl.ds(0, big_v.shape[1]), pl.ds(0, late_ref.shape[1])]
    loads = [
        pltpu.make_async_copy(source, target, load_sem.at[n])
        for n, (source, target) in enumerate(
            (
                (fall_ref.at[pl.ds(0, narrow), pl.ds(0, middle)], falls[0]),
                (fall_ref.at[pl.ds(0, narrow), pl.ds(middle, middle)], falls[1]),
                (own_ref, rows_v),
                (weight_ref.at[:, :, pl.ds(weight_ref.shape[2] - chip, chip)], weight_v),
                (qkv_ref, qkv_v),
                (mixed_ref, mixed_v),
                (rows_v, full_ref.at[pl.ds(0, size)]),
                (first_ref, big_v),
                (residual_ref.at[:, pl.ds(0, narrow)], residual_v),
                (late_ref, late_v),
                (late_v, late_grad_ref.at[:, pl.ds(wide + chip, late_ref.shape[1])]),
            )
        )
    ]
    for n in (0, 1, 2, 3, 4, 5, 7, 8):
        loads[n].start()
    key_v[...] = jnp.zeros_like(key_v)
    value_v[...] = jnp.zeros_like(value_v)
    for copy in loads[:2]:
        copy.wait()
    out_terms(
        links,
        hid_ref,
        hid_v,
        lambda rows, at: across(rows[:, 0:middle], falls[0][at, :])
        + across(rows[:, middle : 2 * middle], falls[1][at, :]),
        narrow,
        kept_v,
        send_v,
        load_sem,
        11,
    )
    loads[9].start()
    for copy in loads[2:6]:
        copy.wait()
    loads[6].start()
    loads[9].wait()
    loads[10].start()
    together = min(2, heads)
    for i in range(count):
        if i:
            for part in (0, 1):
                shares[(i, part)].wait_recv()
            links.pass_on(shares, i)
            if i == 1:
                loads[6].wait()
            unit_loads = links.loads(full_ref, rows_v, i, load_sem, 11)
            for copy in unit_loads:
                copy.start()
            for copy in unit_loads:
                copy.wait()
        if i + 1 == count:
            for j in range(count - 1, count // 2 - 1, -1):
                for part in (0, 1):
                    sums[(j, part)].start()
        for core in (0, 1):
            term = product(rows_v[...], weight_v[core]).astype(BF16)
            for part in (0, 1):
                row = links.start_row(i, part)
                grad_v[row : row + half, core * chip : (core + 1) * chip] = term[
                    part * half : (part + 1) * half
                ]
        blocks = [links.block(i, part) for part in (0, 1)]
        firsts = [links.start_row(i, part) for part in (0, 1)]

        def one(n, _, blocks=blocks, firsts=firsts):
            part, first_head = n // (heads // together), n % (heads // together) * together
            row = pl.multiple_of(firsts[0] + part * (firsts[1] - firsts[0]), half)
            block = lax.bitwise_xor(here, blocks[0] + part * (blocks[1] - blocks[0]))
            attend_backward_unit(
                here,
                [first_head + m for m in range(together)],
                block,
                part * half,
                row,
                half,
                qkv_v,
                grad_v,
                mixed_v,
                log_ref,
                result_ref,
                key_v,
                value_v,
            )
            return 0

        lax.fori_loop(0, 2 * heads // together, one, 0)

    def store_head(head, _):
        at = pl.ds(pl.multiple_of(head * HEAD_DIM, HEAD_DIM), HEAD_DIM)
        column = head * (3 * HEAD_DIM)
        key_at = pl.ds(pl.multiple_of(column + HEAD_DIM, HEAD_DIM), HEAD_DIM)
        value_at = pl.ds(pl.multiple_of(column + 2 * HEAD_DIM, HEAD_DIM), HEAD_DIM)
        result_ref[:, key_at] = (key_v[:, at] * HEAD_DIM ** (-0.5)).astype(BF16)
        result_ref[:, value_at] = value_v[:, at].astype(BF16)
        return 0

    lax.fori_loop(0, heads, store_head, 0)
    loads[10].wait()
    loads[7].wait()
    end_first = weight_grads(
        partner,
        big_v,
        result_ref,
        theirs_v.at[:, pl.ds(0, wide)],
        came_v.at[:, pl.ds(0, wide)],
        (late_grad_ref.at[:, pl.ds(0, wide)],),
        grad_send.at[0],
        grad_recv.at[0],
        (grad_store.at[0],),
    )
    again = pltpu.make_async_copy(full_ref, big_v, load_sem.at[7])
    again.start()
    links.combine(sums, kept_v, send_v, recv_v, count // 2 - 1, 1)
    again.wait()
    end_second = weight_grads(
        partner,
        big_v,
        mixed_v,
        theirs_v.at[:, pl.ds(wide, chip)],
        came_v.at[:, pl.ds(wide, chip)],
        (late_grad_ref.at[:, pl.ds(wide, chip)],),
        grad_send.at[1],
        grad_recv.at[1],
        (grad_store.at[1],),
    )
    loads[8].wait()

    def low(part, at, to, value):
        low_ref[to, :] = (residual_v[to, :] + (value + table_ref[5:6, 0:narrow])).astype(BF16)

    links.combine(sums, kept_v, send_v, recv_v, 0, 0, low)
    end_first()
    end_second()
    for pair in links.pairs:
        sums[pair].wait_send()
        shares[pair].wait_send()


def attend_backward_unit(
    here, heads, block, offset, row, half, qkv_v, grad_v, mixed_v, log_ref, result_ref, key_v, value_v
):
    size = 2 * half
    scaling = HEAD_DIM ** (-0.5)
    at = pl.ds(row, half)

    def columns(head, n):
        return pl.ds(pl.multiple_of(head * (3 * HEAD_DIM) + n * HEAD_DIM, HEAD_DIM), HEAD_DIM)

    places = [pl.ds(pl.multiple_of(head * HEAD_DIM, HEAD_DIM), HEAD_DIM) for head in heads]
    queries = [qkv_v[at, columns(head, 0)] for head in heads]
    grads = [grad_v[at, place] for place in places]
    centres = [
        jnp.sum((grad.astype(F32) * mixed_v[at, place].astype(F32)).T, axis=0, keepdims=True)
        for grad, place in zip(grads, places)
    ]
    logs = [log_ref[head, 0:1, at] for head in heads]

    def step(j, query_grads, last):
        there = pl.ds(rows_of(here, j, size), size)
        results = []
        for n, head in enumerate(heads):
            keys = qkv_v[there, columns(head, 1)]
            values = qkv_v[there, columns(head, 2)]
            weights = jnp.exp(across(keys, queries[n]) * scaling - logs[n])
            if last:
                behind = lax.broadcasted_iota(jnp.int32, (size, half), 0) <= offset + (
                    lax.broadcasted_iota(jnp.int32, (size, half), 1)
                )
                weights = jnp.where(behind, weights, 0.0)
            slopes = (weights * (across(values, grads[n]) - centres[n])).astype(BF16)
            value_v[there, places[n]] += product(weights.astype(BF16), grads[n])
            key_v[there, places[n]] += product(slopes, queries[n])
            results.append(query_grads[n] + inner(slopes, keys))
        return tuple(results)

    query_grads = lax.fori_loop(
        0,
        block,
        lambda j, found: step(j, found, False),
        tuple(jnp.zeros((half, HEAD_DIM), F32) for _ in heads),
    )
    query_grads = step(block, query_grads, True)
    for n, head in enumerate(heads):
        result_ref[at, columns(head, 0)] = (query_grads[n] * scaling).astype(BF16)


def out_terms(links, hid_ref, hid_v, columns, narrow, kept_v, send_v, load_sem, base):
    count, slots = links.count, hid_v.shape[0]
    order = list(range(count - 1, -1, -1))

    def load(n):
        slot = n % slots
        copies = links.loads(hid_ref, hid_v.at[slot], order[n], load_sem, base + 2 * slot)
        for copy in copies:
            copy.start()
        return copies

    coming = [load(n) for n in range(slots)]
    for n, i in enumerate(order):
        for copy in coming[n]:
            copy.wait()
        links.terms(i, lambda at, n=n: columns(hid_v.at[n % slots], at), narrow, kept_v, send_v)
        if n + slots < count:
            coming.append(load(n + slots))


def attend_back(
    own, weight, qkv, mixed, log_total, hid, fall_weight, first, residual, late, table, count
):
    rows, width = own.shape
    length, columns = qkv.shape
    heads = columns // (3 * HEAD_DIM)
    hidden = hid.shape[1]
    links = Links(count, rows // 2)
    half, copies = links.half, len(links.pairs)
    narrow = width // 2
    pairs = heads * length * (length + rows) // 2
    anywhere = pl.BlockSpec(memory_space=pl.ANY)
    inside = pl.BlockSpec(memory_space=pltpu.VMEM)
    dma = pltpu.SemaphoreType.DMA
    return pl.pallas_call(
        functools.partial(attend_back_kernel, links, heads),
        out_shape=(
            jax.ShapeDtypeStruct((length, width), BF16),
            jax.ShapeDtypeStruct((length, columns), BF16),
            jax.ShapeDtypeStruct((rows, narrow), BF16),
            jax.ShapeDtypeStruct((width, 2 * heads * HEAD_DIM + late.shape[1]), BF16),
        ),
        in_specs=[anywhere] * 4 + [inside] + [anywhere] * 5 + [inside],
        out_specs=(anywhere, inside, inside, anywhere),
        scratch_shapes=[
            pltpu.VMEM((rows, narrow), F32),
            pltpu.VMEM((2, width, heads * HEAD_DIM // 2), BF16),
            pltpu.VMEM(qkv.shape, BF16),
            pltpu.VMEM(mixed.shape, BF16),
            pltpu.VMEM((length, width), BF16),
            pltpu.VMEM((width, max(2 * heads * HEAD_DIM, hidden // 2)), BF16),
            pltpu.VMEM((width, 2 * heads * HEAD_DIM), BF16),
            pltpu.VMEM(mixed.shape, BF16),
            pltpu.VMEM((rows, width), BF16),
            pltpu.VMEM((1, rows, hidden), BF16),
            pltpu.VMEM(mixed.shape, F32),
            pltpu.VMEM(mixed.shape, F32),
            pltpu.VMEM((count, half, narrow), F32),
            pltpu.VMEM((copies, half, narrow), BF16),
            pltpu.VMEM((copies, half, narrow), BF16),
            dma((13,)),
            dma((3, width // 512)),
            dma((3, width // 512)),
            dma((3, width // 512)),
            dma((copies,)),
            dma((copies,)),
            dma((copies,)),
            dma((copies,)),
        ],
        compiler_params=pltpu.CompilerParams(
            collective_id=4, has_side_effects=True, vmem_limit_bytes=63 * 1024 * 1024
        ),
        cost_estimate=pl.CostEstimate(
            flops=pairs * HEAD_DIM * 20 + 2 * length * width * (heads * HEAD_DIM + hidden // 2),
            bytes_accessed=length * width * 6 + length * columns * 4 + length * hidden * 2,
            transcendentals=pairs,
        ),
        name="attend_back",
    )(own, weight, qkv, mixed, log_total, hid, fall_weight, first, residual, late, table)


def first_back_kernel(
    links,
    grads_ref,
    weight_ref,
    hid_ref,
    fall_ref,
    low_ref,
    residual_ref,
    back_ref,
    tokens_ref,
    table_ref,
    hidden_ref,
    out_ref,
    input_ref,
    vector_ref,
    bias_ref,
    fall_grad_ref,
    rise_grad_ref,
    grads_v,
    weight_v,
    hid_v,
    fall_v,
    kept_v,
    send_v,
    recv_v,
    kept_w,
    send_w,
    recv_w,
    residual_v,
    tokens_v,
    high_v,
    block_v,
    load_sem,
    pair_send,
    pair_recv,
    piece_send,
    piece_recv,
    sum_send,
    sum_recv,
    late_send,
    late_recv,
):
    count, half = links.count, links.half
    size = 2 * half
    wide = weight_v.shape[2]
    thin = hidden_ref.shape[0] // count
    hidden = hidden_ref.shape[1] * 2 // 3
    narrow = fall_v.shape[0]
    core = lax.axis_index("tp")
    partner = {"tp": 1 - core}
    links.greet([partner], range(1, count))
    sums = links.summing(send_v, recv_v, sum_send, sum_recv)
    lates = links.summing(send_w, recv_w, late_send, late_recv)
    pieces = piece_copies(
        count,
        lambda i: hidden_ref.at[pl.ds(pl.multiple_of(i * thin, thin), thin)],
        block_v,
        piece_send,
        piece_recv,
    )
    here = lax.axis_index("ctx")
    pieces.append(
        pltpu.make_async_copy(
            hidden_ref.at[pl.ds(pl.multiple_of(here * thin, thin), thin)],
            block_v.at[here],
            load_sem.at[10],
        )
    )
    right = pl.ds(narrow, narrow)
    left = pl.ds(0, narrow)

    def both_cores(n, source, target_ref, rows, columns):
        target = target_ref.at[core, rows, columns]
        return [
            pltpu.make_async_copy(source, target, load_sem.at[11 + n]),
            pltpu.make_async_remote_copy(
                src_ref=source,
                dst_ref=target,
                send_sem=pair_send.at[n],
                recv_sem=pair_recv.at[n],
                device_id=partner,
                device_id_type=MESH,
            ),
        ]

    lows = both_cores(0, high_v, out_ref, pl.ds(0, size), left)
    low = pltpu.make_async_copy(low_ref, high_v, load_sem.at[11])
    low.start()
    outs = []
    loads = [
        pltpu.make_async_copy(source, target, load_sem.at[n])
        for n, (source, target) in enumerate(
            (
                (weight_ref.at[:, :, pl.ds(0, wide)], weight_v),
                (fall_ref.at[right], fall_v),
            )
        )
    ]
    more = [
        pltpu.make_async_copy(source, target, load_sem.at[15 + n])
        for n, (source, target) in enumerate(
            ((residual_ref.at[:, right], residual_v), (tokens_ref.at[core], tokens_v))
        )
    ]
    for copy in loads:
        copy.start()
    order = list(range(count - 1, -1, -1))
    unit_loads = links.loads(grads_ref, grads_v.at[0], order[0], load_sem, 2)
    for copy in unit_loads + pieces + more:
        copy.start()
    low.wait()
    for copy in lows:
        copy.start()
    bias_ref[...] = jnp.zeros_like(bias_ref)
    vector_ref[...] = jnp.zeros_like(vector_ref)
    loads[0].wait()
    for n, i in enumerate(order):
        for copy in unit_loads:
            copy.wait()
        if n + 1 < count:
            unit_loads = links.loads(
                grads_ref, grads_v.at[(n + 1) % 2], order[n + 1], load_sem, 2 + 2 * ((n + 1) % 2)
            )
            for copy in unit_loads:
                copy.start()
        links.terms(
            i,
            lambda at, n=n: across(grads_v[n % 2, :, :wide], weight_v[0, at, :])
            + across(grads_v[n % 2, :, wide:], weight_v[1, at, :]),
            weight_v.shape[1],
            kept_v,
            send_v,
        )
        if i >= count // 2:
            for part in (0, 1):
                sums[(i, part)].start()
        chunk = min(64, half)

        def bias(step, _, n=n):
            rows = pl.ds(pl.multiple_of(step * chunk, chunk), chunk)
            value = grads_v[n % 2, rows, :].astype(F32)
            bias_ref[0:1, :] += jnp.sum(value, axis=0, keepdims=True)
            return 0

        lax.fori_loop(0, size // chunk, bias, 0)
    loads[1].wait()
    out_terms(
        links,
        hid_ref,
        hid_v,
        lambda rows, at: across(rows[...], fall_v[at, :]),
        narrow,
        kept_w,
        send_w,
        load_sem,
        6,
    )
    for copy in pieces:
        copy.wait()
    for c in range(count):
        rise_grad_ref[:, c * hidden : (c + 1) * hidden] = block_v[c, :, 0:hidden].astype(F32)
        fall_grad_ref[c] = block_v[c, :, hidden:].astype(F32).T
    links.combine(sums, kept_v, send_v, recv_v, count // 2 - 1, 1)
    backs = [
        pltpu.make_async_copy(
            back_ref.at[pl.ds(part * half, half)], kept_v.at[2 + part], load_sem.at[2 + part]
        )
        for part in (0, 1)
    ]
    for copy in backs:
        copy.start()
    for i in range(count - 1, count // 2 - 1, -1):
        for part in (0, 1):
            lates[(i, part)].start()
    for copy in more + backs:
        copy.wait()

    def last(part, at, to, first):
        normed, spread = normalize(tokens_v[to, :].astype(F32))
        grad = kept_v[2 + part, at, :] + norm_back(first * table_ref[0:1, :], normed, spread)
        tokens_v[to, :] = grad.astype(BF16)
        for n, value in enumerate((first * normed, first)):
            vector_ref[n : n + 1, :] += jnp.sum(value, axis=0, keepdims=True)

    def send_part(part):
        rows = pl.ds(part * half, half)
        copies = both_cores(
            1 + part, tokens_v.at[rows], input_ref, rows, pl.ds(0, 2 * narrow)
        )
        for copy in copies:
            copy.start()
        outs.extend(copies)

    links.combine(sums, kept_v, send_v, recv_v, 0, 0, last, send_part)

    def high(part, at, to, value):
        high_v[to, :] = (
            residual_v[to, :] + (value + table_ref[5:6, narrow : 2 * narrow])
        ).astype(BF16)

    for copy in lows:
        copy.wait()
    links.combine(lates, kept_w, send_w, recv_w, count // 2 - 1, 0, high)
    copies = both_cores(3, high_v, out_ref, pl.ds(0, size), right)
    for copy in copies:
        copy.start()
    for copy in outs + copies:
        copy.wait()
    for pair in links.pairs:
        sums[pair].wait_send()
        lates[pair].wait_send()


def first_back(
    grads, weight, hid, fall_weight, low, residual, back, tokens, table, hidden_rows, count
):
    length, columns = grads.shape
    width, hidden = fall_weight.shape
    rows = length // count
    links = Links(count, rows // 2)
    half, copies = links.half, len(links.pairs)
    narrow = width // 2
    thin, piece = hidden_rows.shape[0] // count, hidden_rows.shape[1] * 2 // 3
    anywhere = pl.BlockSpec(memory_space=pl.ANY)
    inside = pl.BlockSpec(memory_space=pltpu.VMEM)
    dma = pltpu.SemaphoreType.DMA
    return pl.pallas_call(
        functools.partial(first_back_kernel, links),
        out_shape=(
            jax.ShapeDtypeStruct((2, rows, width), BF16),
            jax.ShapeDtypeStruct((2, rows, width), BF16),
            jax.ShapeDtypeStruct((8, width), F32),
            jax.ShapeDtypeStruct((1, columns), F32),
            jax.ShapeDtypeStruct((count, piece // 2, thin), F32),
            jax.ShapeDtypeStruct((thin, count * piece), F32),
        ),
        in_specs=[anywhere] * 8 + [inside, anywhere],
        out_specs=(anywhere, anywhere, inside, inside, inside, inside),
        scratch_shapes=[
            pltpu.VMEM((2, rows, columns), BF16),
            pltpu.VMEM((2, width, columns // 2), BF16),
            pltpu.VMEM((2, rows, hidden), BF16),
            pltpu.VMEM((narrow, hidden), BF16),
            pltpu.VMEM((count, half, width), F32),
            pltpu.VMEM((copies, half, width), BF16),
            pltpu.VMEM((copies, half, width), BF16),
            pltpu.VMEM((count, half, narrow), F32),
            pltpu.VMEM((copies, half, narrow), BF16),
            pltpu.VMEM((copies, half, narrow), BF16),
            pltpu.VMEM((rows, narrow), F32),
            pltpu.VMEM((rows, width), BF16),
            pltpu.VMEM((rows, narrow), BF16),
            pltpu.VMEM((count, thin, piece * 3 // 2), BF16),
            dma((17,)),
            dma((4,)),
            dma((4,)),
            dma((count - 1,)),
            dma((count - 1,)),
            dma((copies,)),
            dma((copies,)),
            dma((copies,)),
            dma((copies,)),
        ],
        compiler_params=pltpu.CompilerParams(
            collective_id=5, has_side_effects=True, vmem_limit_bytes=63 * 1024 * 1024
        ),
        cost_estimate=pl.CostEstimate(
            flops=2 * length * width * (columns + hidden // 2),
            bytes_accessed=length * columns * 2 + length * hidden * 2 + width * (columns + hidden) * 2,
            transcendentals=0,
        ),
        name="first_back",
    )(grads, weight, hid, fall_weight, low, residual, back, tokens, table, hidden_rows)


def body(
    tokens,
    cotangent,
    attention_gain,
    attention_bias,
    feedforward_gain,
    feedforward_bias,
    query_weight,
    query_bias,
    key_weight,
    value_weight,
    value_bias,
    output_weight,
    output_bias,
    up_weight,
    up_bias,
    down_weight,
    down_bias,
):
    _, local_rows, model_width = tokens.shape
    ctx, dp = lax.axis_size("ctx"), lax.axis_size("dp")
    here, core = lax.axis_index("ctx"), lax.axis_index("tp")
    thin = query_weight.shape[0]
    heads = query_weight.shape[1] // (HEAD_DIM * ctx)
    hidden = up_weight.shape[1] // ctx
    packed = jnp.stack(
        [w.reshape(thin, ctx, heads, HEAD_DIM) for w in (query_weight, key_weight, value_weight)],
        axis=3,
    ).reshape(thin, ctx, heads * 3 * HEAD_DIM)
    head_pieces = jnp.concatenate(
        [
            packed.transpose(1, 0, 2),
            output_weight.reshape(ctx, heads * HEAD_DIM, thin).transpose(0, 2, 1),
        ],
        axis=2,
    )
    hidden_pieces = jnp.concatenate(
        [
            down_weight.reshape(ctx, hidden, thin).transpose(0, 2, 1),
            up_weight.reshape(thin, ctx, hidden).transpose(1, 0, 2),
        ],
        axis=2,
    )

    small = jnp.stack(
        [attention_gain, attention_bias, feedforward_gain, feedforward_bias, output_bias, down_bias]
    ).astype(F32)
    small = jnp.concatenate([small, jnp.zeros((2, thin), F32)])
    def own_columns(vector):
        return lax.dynamic_index_in_dim(vector.reshape(ctx, -1), here, 0, keepdims=False)

    query_shift = own_columns(query_bias).reshape(heads, HEAD_DIM)
    value_shift = own_columns(value_bias).reshape(heads, HEAD_DIM)
    qkv_shift = jnp.stack([query_shift, jnp.zeros_like(query_shift), value_shift], axis=1)
    shifts = jnp.concatenate([qkv_shift.reshape(-1), own_columns(up_bias)])
    other_shifts = swap(shifts, "tp", 1)
    wide = heads * 3 * HEAD_DIM
    qkv_shift = jnp.concatenate([shifts[:wide], other_shifts[:wide]]).astype(F32)
    rise_shift = jnp.concatenate([shifts[wide:], other_shifts[wide:]]).astype(F32)

    ones, head_weights, hidden_block, table = front(
        tokens, head_pieces, hidden_pieces, small, ctx, dp
    )
    head_weights = head_weights.reshape(model_width, -1)
    hidden_weights = lax.all_gather(
        hidden_block.reshape(ctx * thin, -1), "dp", axis=0, tiled=True
    )
    qkv, mixed, log_total, grads_in, residual, input_two, head_whole = attend(
        ones, head_weights, qkv_shift[None], cotangent, tokens, table, 2 * heads, ctx
    )
    _, hid, _, hidden_both, late, residual_grad, branch_grad, vectors, rise_bias, fall_weight = (
        feed_forward(input_two, grads_in, hidden_weights, rise_shift[None], residual, table, ctx)
    )
    hidden_rows = over_dp(hidden_both)

    _, qkv_grads, low_columns, head_both = attend_back(
        branch_grad,
        head_whole,
        qkv,
        mixed,
        log_total,
        hid,
        fall_weight,
        ones,
        residual,
        late,
        table,
        ctx,
    )
    head_both, hidden_rows = lax.optimization_barrier((head_both, hidden_rows))
    head_rows = over_dp(head_both)
    outputs, input_grads, firsts, qkv_bias, fall_first, rise_grad = first_back(
        qkv_grads,
        head_whole,
        hid,
        fall_weight,
        low_columns,
        residual,
        residual_grad,
        tokens,
        table,
        hidden_rows,
        ctx,
    )
    biases = jnp.concatenate(
        [rise_bias.reshape(2, 1, hidden), qkv_bias.reshape(2, 1, wide)], axis=2
    )
    query_grad, key_grad, value_grad, out_grad, fall_second, features, totals = end(
        head_rows, vectors, firsts, biases, heads, ctx, dp
    )
    fall_grad = jnp.concatenate([fall_first, fall_second], axis=1).reshape(-1, thin)
    totals = totals[:, 0]
    qkv_bias = totals[:, hidden:].reshape(ctx * heads, 3, HEAD_DIM)
    return (
        outputs,
        input_grads,
        features[4],
        features[5],
        features[0],
        features[1],
        query_grad,
        qkv_bias[:, 0].reshape(-1),
        key_grad,
        value_grad,
        qkv_bias[:, 2].reshape(-1),
        out_grad,
        features[2],
        rise_grad,
        totals[:, :hidden].reshape(-1),
        fall_grad,
        features[3],
    )


def solution(mesh):
    placed = (
        P("dp", "ctx", None),
        P("dp", "ctx", None),
        P(("dp", "ctx")),
        P(("dp", "ctx")),
        P(("dp", "ctx")),
        P(("dp", "ctx")),
        P(("dp", "ctx"), "tp"),
        P("tp"),
        P(("dp", "ctx"), "tp"),
        P(("dp", "ctx"), "tp"),
        P("tp"),
        P("tp", ("dp", "ctx")),
        P(("dp", "ctx")),
        P(("dp", "ctx"), "tp"),
        P("tp"),
        P("tp", ("dp", "ctx")),
        P(("dp", "ctx")),
    )
    return jax.shard_map(
        body,
        mesh=mesh,
        in_specs=placed,
        out_specs=(
            P("dp", "ctx", None),
            P("dp", "ctx", None),
            P(("dp", "ctx")),
            P(("dp", "ctx")),
            P(("dp", "ctx")),
            P(("dp", "ctx")),
            P(("dp", "ctx"), "tp"),
            P("tp"),
            P(("dp", "ctx"), "tp"),
            P(("dp", "ctx"), "tp"),
            P("tp"),
            P("tp", ("dp", "ctx")),
            P(("dp", "ctx")),
            P(("dp", "ctx"), "tp"),
            P("tp"),
            P("tp", ("dp", "ctx")),
            P(("dp", "ctx")),
        ),
        check_vma=False,
    )
```

```python
import functools

import jax
import jax.numpy as jnp
from jax import lax
from jax.experimental import pallas as pl
from jax.experimental.pallas import tpu as pltpu
from jax.sharding import PartitionSpec as P

HEAD_DIM = 128
EPSILON = 1e-05
NEGATIVE = -1e30
F32 = jnp.float32
BF16 = jnp.bfloat16
MESH = pl.DeviceIdType.MESH


def product(former, latter):
    return jnp.dot(former, latter, preferred_element_type=F32)


def inner(former, latter):
    return lax.dot_general(former, latter, (((0,), (0,)), ((), ())), preferred_element_type=F32)


def across(former, latter):
    return lax.dot_general(former, latter, (((1,), (1,)), ((), ())), preferred_element_type=F32)


def normalize(values):
    average = jnp.mean(values, axis=-1, keepdims=True)
    centred = values - average
    spread = lax.rsqrt(jnp.mean(centred * centred, axis=-1, keepdims=True) + EPSILON)
    return (centred * spread, spread)


def norm_back(gradient, normed, spread):
    first_mean = jnp.mean(gradient, axis=-1, keepdims=True)
    second_mean = jnp.mean(gradient * normed, axis=-1, keepdims=True)
    return spread * (gradient - first_mean - normed * second_mean)


def swap(value, axis, mask):
    size = lax.axis_size(axis)
    return lax.ppermute(value, axis, [(i, i ^ mask) for i in range(size)])


def over_dp(both):
    return lax.psum_scatter(both, "dp", scatter_dimension=0, tiled=True)


def rows_of(here, block, size):
    return pl.multiple_of(lax.bitwise_xor(here, block) * size, size)


class Links:
    def __init__(self, count, half):
        self.count, self.half = count, half
        self.bits = (count - 1).bit_length()
        self.pairs = [(i, part) for i in range(1, count) for part in (0, 1)]
        self.slot = {pair: n for n, pair in enumerate(self.pairs)}

    def block(self, i, part):
        if part == 0:
            return i
        return sum(((i >> b) & 1) << (self.bits - 1 - b) for b in range(self.bits))

    def top(self, i):
        return 1 << (i.bit_length() - 1)

    def near(self, i):
        return i ^ self.top(i)

    def given(self, i):
        return [j for j in range(self.count - 1, 0, -1) if self.near(j) == i]

    def far(self, i, part):
        mask = self.block(self.top(i), part)
        return {"ctx": lax.bitwise_xor(lax.axis_index("ctx"), mask)}

    def start_row(self, i, part):
        return (2 * self.block(i, part) + part) * self.half

    def rows(self, ref, i, part):
        return ref.at[pl.ds(self.start_row(i, part), self.half)]

    def greet(self, others=(), masks=None):
        barrier = pltpu.get_barrier_semaphore()
        masks = [1 << bit for bit in range(self.bits)] if masks is None else masks
        partners = [{"ctx": lax.bitwise_xor(lax.axis_index("ctx"), mask)} for mask in masks]
        partners += list(others)
        for partner in partners:
            pl.semaphore_signal(barrier, 1, device_id=partner, device_id_type=MESH)
        pl.semaphore_wait(barrier, len(partners))

    def sharing(self, own_ref, full_ref, send_sem, recv_sem):
        copies = {}
        for i, part in self.pairs:
            near = self.near(i)
            source = (
                own_ref.at[pl.ds(part * self.half, self.half)]
                if near == 0
                else self.rows(full_ref, near, part)
            )
            n = self.slot[(i, part)]
            copies[(i, part)] = pltpu.make_async_remote_copy(
                src_ref=source,
                dst_ref=self.rows(full_ref, i, part),
                send_sem=send_sem.at[n],
                recv_sem=recv_sem.at[n],
                device_id=self.far(i, part),
                device_id_type=MESH,
            )
        return copies

    def summing(self, send_ref, recv_ref, send_sem, recv_sem):
        copies = {}
        for i, part in self.pairs:
            n = self.slot[(i, part)]
            copies[(i, part)] = pltpu.make_async_remote_copy(
                src_ref=send_ref.at[n],
                dst_ref=recv_ref.at[n],
                send_sem=send_sem.at[n],
                recv_sem=recv_sem.at[n],
                device_id=self.far(i, part),
                device_id_type=MESH,
            )
        return copies

    def pass_on(self, copies, arrived, own=False):
        for i, part in self.pairs:
            if self.near(i) == arrived:
                copies[(i, part)].start()

    def loads(self, ref, buffer, i, sem, base):
        return [
            pltpu.make_async_copy(
                self.rows(ref, i, part),
                buffer.at[pl.ds(part * self.half, self.half)],
                sem.at[base + part],
            )
            for part in (0, 1)
        ]

    def terms(self, i, columns, width, kept_v, send_v):
        tile = min(512, width)

        def step(n, _):
            at = pl.ds(pl.multiple_of(n * tile, tile), tile)
            term = columns(at)
            for part in (0, 1):
                piece = term[part * self.half : (part + 1) * self.half]
                if i < self.count // 2:
                    kept_v[2 * i + part, :, at] = piece
                else:
                    send_v[self.slot[(i, part)], :, at] = piece.astype(BF16)
            return 0

        lax.fori_loop(0, width // tile, step, 0)

    def combine(self, copies, kept_ref, send_ref, recv_ref, first, last, final=None, then=None):
        for i in range(first, last - 1, -1):
            for part in (0, 1):
                for j in self.given(i):
                    copies[(j, part)].wait_recv()
                chunk = min(32, self.half)

                def add(step, _, i=i, part=part):
                    at = pl.ds(pl.multiple_of(step * chunk, chunk), chunk)
                    value = kept_ref[2 * i + part, at, :]
                    for j in self.given(i):
                        value = value + recv_ref[self.slot[(j, part)], at, :].astype(F32)
                    if i == 0:
                        to = pl.ds(pl.multiple_of(part * self.half + step * chunk, chunk), chunk)
                        final(part, at, to, value)
                    else:
                        send_ref[self.slot[(i, part)], at, :] = value.astype(BF16)
                    return 0

                lax.fori_loop(0, self.half // chunk, add, 0)
                if i:
                    copies[(i, part)].start()
                elif then:
                    then(part)


def weight_grads(partner, rows_v, columns_v, theirs_v, came_v, results, send_sem, recv_sem, store_sem):
    tile = 512
    width = rows_v.shape[1]
    own = columns_v.shape[1] // 2

    def place(m):
        return pl.ds(pl.multiple_of(m * tile, tile), tile)

    def swap_tile(m):
        return pltpu.make_async_remote_copy(
            src_ref=theirs_v.at[place(m)],
            dst_ref=came_v.at[place(m)],
            send_sem=send_sem.at[m],
            recv_sem=recv_sem.at[m],
            device_id=partner,
            device_id_type=MESH,
        )

    def store_tile(m):
        copies, column = [], 0
        for n, result in enumerate(results):
            count = result.shape[1]
            copies.append(
                pltpu.make_async_copy(
                    came_v.at[place(m), pl.ds(column, count)], result.at[place(m)], store_sem[n].at[m]
                )
            )
            column += count
        return copies

    def first(m, _):
        term = inner(rows_v[:, place(m)], columns_v[:, own : 2 * own])
        theirs_v[place(m), :] = term.astype(BF16)
        swap_tile(m).start()
        return 0

    def second(m, _):
        swap_tile(m).wait_recv()
        term = inner(rows_v[:, place(m)], columns_v[:, 0:own])
        came_v[place(m), :] = (term + came_v[place(m), :].astype(F32)).astype(BF16)
        for copy in store_tile(m):
            copy.start()
        return 0

    def end(m, _):
        for copy in store_tile(m):
            copy.wait()
        swap_tile(m).wait_send()
        return 0

    lax.fori_loop(0, width // tile, first, 0)
    lax.fori_loop(0, width // tile, second, 0)
    return lambda: lax.fori_loop(0, width // tile, end, 0)


def feed_forward_kernel(
    links,
    own_ref,
    grads_ref,
    both_ref,
    shift_ref,
    residual_ref,
    table_ref,
    full_ref,
    hid_ref,
    slope_ref,
    both_grad_ref,
    late_grad_ref,
    back_ref,
    branch_ref,
    vector_ref,
    bias_ref,
    fall_ref,
    rise_big,
    fall_big,
    rows_v,
    grads_v,
    hid_v,
    slope_v,
    kept_v,
    send_v,
    recv_v,
    theirs_v,
    came_v,
    load_sem,
    store_sem,
    pair_send,
    pair_recv,
    grad_send,
    grad_recv,
    grad_store,
    share_send,
    share_recv,
    sum_send,
    sum_recv,
):
    half, count = links.half, links.count
    width, hidden = own_ref.shape[1], hid_v.shape[1]
    length = 2 * half * count
    rise_v = rise_big.at[pl.ds(0, width), pl.ds(0, hidden)]
    fall_v = fall_big.at[pl.ds(0, width), pl.ds(0, hidden)]
    own_half = pl.ds(0, hidden // 2)
    other_half = pl.ds(hidden // 2, hidden // 2)
    partner = {"tp": 1 - lax.axis_index("tp")}
    links.greet([partner])
    swaps = [
        pltpu.make_async_remote_copy(
            src_ref=both_ref.at[:, pl.ds(n * (hidden // 2), hidden // 2)],
            dst_ref=target.at[:, other_half],
            send_sem=pair_send.at[n],
            recv_sem=pair_recv.at[n],
            device_id=partner,
            device_id_type=MESH,
        )
        for n, target in enumerate((fall_v, rise_v))
    ]
    for copy in swaps:
        copy.start()
    shares = links.sharing(own_ref, full_ref, share_send, share_recv)
    sums = links.summing(send_v, recv_v, sum_send, sum_recv)
    links.pass_on(shares, 0)
    keep = pltpu.make_async_copy(rows_v, full_ref.at[pl.ds(0, 2 * half)], load_sem.at[0])
    first = pltpu.make_async_copy(own_ref, rows_v, load_sem.at[1])
    first.start()
    rise = pltpu.make_async_copy(both_ref.at[:, other_half], rise_v.at[:, own_half], load_sem.at[2])
    rise.start()
    fall = pltpu.make_async_copy(both_ref.at[:, own_half], fall_v.at[:, own_half], load_sem.at[3])
    fall.start()
    bias_ref[...] = jnp.zeros_like(bias_ref)

    grad_loads = links.loads(grads_ref, grads_v, 0, load_sem, 4)
    for copy in grad_loads:
        copy.start()
    stores = []
    tile = min(512, hidden // 2)
    rows_big = rise_big.at[pl.ds(0, length), pl.ds(0, width)]
    columns_big = fall_big.at[pl.ds(0, length), pl.ds(0, hidden)]
    early = pltpu.make_async_copy(slope_ref, columns_big, load_sem.at[1])
    for i in range(count):
        if i == 0:
            first.wait()
            keep.start()
            rise.wait()
            fall.wait()
        else:
            for part in (0, 1):
                shares[(i, part)].wait_recv()
            links.pass_on(shares, i)
            if i == 1:
                keep.wait()
            row_loads = links.loads(full_ref, rows_v, i, load_sem, 8)
            for copy in row_loads:
                copy.start()
            for copy in row_loads:
                copy.wait()
        for copy in grad_loads + stores:
            copy.wait()

        def rise_step(step, _, i=i):
            at = pl.ds(pl.multiple_of(step * tile, tile), tile)
            pre = product(rows_v[...], rise_v[:, at]) + shift_ref[0:1, at]
            back = product(grads_v[...], fall_v[:, at])
            cumulative = 0.5 * (1.0 + lax.erf(pre * 0.7071067811865476))
            density = jnp.exp(-0.5 * pre * pre) * 0.3989422804014327
            hid_v[:, at] = (pre * cumulative).astype(BF16)
            slope = (back * (cumulative + pre * density)).astype(BF16)
            slope_v[:, at] = slope
            bias_ref[0:1, at] += jnp.sum(slope.astype(F32), axis=0, keepdims=True)
            return 0

        lax.fori_loop(0, hidden // 2 // tile, rise_step, 0)
        if i == 0:
            for copy in swaps:
                copy.wait_recv()
            keep_fall = pltpu.make_async_copy(fall_v, fall_ref, store_sem.at[4])
            keep_fall.start()
        lax.fori_loop(hidden // 2 // tile, hidden // tile, rise_step, 0)
        if i + 1 < count:
            grad_loads = links.loads(grads_ref, grads_v, i + 1, load_sem, 4)
            for copy in grad_loads:
                copy.start()
        stores = []
        for n, (buffer, ref) in enumerate(((hid_v, hid_ref), (slope_v, slope_ref))):
            for part in (0, 1):
                copy = pltpu.make_async_copy(
                    buffer.at[pl.ds(part * half, half)],
                    links.rows(ref, i, part),
                    store_sem.at[2 * n + part],
                )
                copy.start()
                stores.append(copy)

        if i + 1 == count:
            for copy in stores + [keep_fall]:
                copy.wait()
            early.start()
        links.terms(i, lambda at: across(slope_v[...], rise_v[at, :]), width, kept_v, send_v)
        if i >= count // 2:
            for part in (0, 1):
                sums[(i, part)].start()
    ends = []
    quarter = hidden // 4
    results = (
        (both_grad_ref.at[:, own_half],),
        (both_grad_ref.at[:, pl.ds(hidden // 2, quarter)], late_grad_ref),
    )
    grad_stores = ((grad_store.at[0],), (grad_store.at[1], grad_store.at[2]))
    for n, (left, right) in enumerate(((full_ref, slope_ref), (grads_ref, hid_ref))):
        lefts = pltpu.make_async_copy(left, rows_big, load_sem.at[0])
        rights = pltpu.make_async_copy(right, columns_big, load_sem.at[1]) if n else early
        lefts.start()
        if n:
            rights.start()
        for end in ends:
            end()
        lefts.wait()
        rights.wait()
        ends = [
            weight_grads(
                partner,
                rows_big,
                columns_big,
                theirs_v,
                came_v.at[n],
                results[n],
                grad_send.at[n],
                grad_recv.at[n],
                grad_stores[n],
            )
        ]
        if n == 0:
            links.combine(sums, kept_v, send_v, recv_v, count // 2 - 1, 1)
            finals = [
                pltpu.make_async_copy(
                    residual_ref.at[pl.ds(part * half, half)], kept_v.at[2 + part], load_sem.at[2 + part]
                )
                for part in (0, 1)
            ]
            finals.append(
                pltpu.make_async_copy(grads_ref.at[pl.ds(0, 2 * half)], rows_v, load_sem.at[4])
            )
            for copy in finals:
                copy.start()
    for copy in finals:
        copy.wait()
    vector_ref[...] = jnp.zeros_like(vector_ref)
    results = []

    def last(part, at, to, second):
        normed, spread = normalize(kept_v[2 + part, at, :])
        incoming = rows_v[to, :].astype(F32)
        back = incoming + norm_back(second * table_ref[2:3, :], normed, spread)
        branch = back.astype(BF16)
        kept_v[part, at, :] = back
        rows_v[to, :] = branch
        for n, value in enumerate((second * normed, second, branch.astype(F32), incoming)):
            vector_ref[n : n + 1, :] += jnp.sum(value, axis=0, keepdims=True)

    def store_part(part):
        rows = pl.ds(part * half, half)
        for n, (source, target) in enumerate(
            ((kept_v.at[part], back_ref.at[rows]), (rows_v.at[rows], branch_ref.at[rows]))
        ):
            copy = pltpu.make_async_copy(source, target, load_sem.at[2 * part + n])
            copy.start()
            results.append(copy)

    links.combine(sums, kept_v, send_v, recv_v, 0, 0, last, store_part)
    for end in ends:
        end()
    for copy in results:
        copy.wait()
    for copy in swaps:
        copy.wait_send()
    for pair in links.pairs:
        shares[pair].wait_send()
        sums[pair].wait_send()


def feed_forward(own, grads, both_weights, shift, residual, table, count):
    rows, width = own.shape
    hidden = both_weights.shape[1]
    length = rows * count
    links = Links(count, rows // 2)
    half, copies = links.half, len(links.pairs)
    anywhere = pl.BlockSpec(memory_space=pl.ANY)
    inside = pl.BlockSpec(memory_space=pltpu.VMEM)
    dma = pltpu.SemaphoreType.DMA
    return pl.pallas_call(
        functools.partial(feed_forward_kernel, links),
        out_shape=(
            jax.ShapeDtypeStruct((length, width), BF16),
            jax.ShapeDtypeStruct((length, hidden), BF16),
            jax.ShapeDtypeStruct((length, hidden), BF16),
            jax.ShapeDtypeStruct((width, hidden * 3 // 4), BF16),
            jax.ShapeDtypeStruct((width, hidden // 4), BF16),
            jax.ShapeDtypeStruct((rows, width), F32),
            jax.ShapeDtypeStruct((rows, width), BF16),
            jax.ShapeDtypeStruct((8, width), F32),
            jax.ShapeDtypeStruct((1, hidden), F32),
            jax.ShapeDtypeStruct((width, hidden), BF16),
        ),
        in_specs=[anywhere, anywhere, anywhere, inside, anywhere, inside],
        out_specs=(anywhere,) * 7 + (inside, inside, anywhere),
        scratch_shapes=[
            pltpu.VMEM((max(width, length), max(width, hidden)), BF16),
            pltpu.VMEM((max(width, length), hidden), BF16),
            pltpu.VMEM((rows, width), BF16),
            pltpu.VMEM((rows, width), BF16),
            pltpu.VMEM((rows, hidden), BF16),
            pltpu.VMEM((rows, hidden), BF16),
            pltpu.VMEM((count, half, width), F32),
            pltpu.VMEM((copies, half, width), BF16),
            pltpu.VMEM((copies, half, width), BF16),
            pltpu.VMEM((width, hidden // 2), BF16),
            pltpu.VMEM((2, width, hidden // 2), BF16),
            dma((10,)),
            dma((5,)),
            dma((2,)),
            dma((2,)),
            dma((3, width // 512)),
            dma((3, width // 512)),
            dma((3, width // 512)),
            dma((copies,)),
            dma((copies,)),
            dma((copies,)),
            dma((copies,)),
        ],
        compiler_params=pltpu.CompilerParams(
            collective_id=3, has_side_effects=True, vmem_limit_bytes=63 * 1024 * 1024
        ),
        cost_estimate=pl.CostEstimate(
            flops=10 * length * width * hidden,
            bytes_accessed=length * width * 8 + width * hidden * 4 + length * hidden * 4,
            transcendentals=length * hidden * 2,
        ),
        name="feed_forward",
    )(own, grads, both_weights, shift, residual, table)


def greet_all(partners):
    barrier = pltpu.get_barrier_semaphore()
    for partner in partners:
        pl.semaphore_signal(barrier, 1, device_id=partner, device_id_type=MESH)
    pl.semaphore_wait(barrier, len(partners))


def others(axis, count):
    return [{axis: lax.bitwise_xor(lax.axis_index(axis), mask)} for mask in range(1, count)]


def axis_bits(axis, size):
    return [
        {axis: lax.bitwise_xor(lax.axis_index(axis), 1 << bit)}
        for bit in range((size - 1).bit_length())
    ]


def piece_copies(count, source, target_ref, send_sem, recv_sem):
    here = lax.axis_index("ctx")
    return [
        pltpu.make_async_remote_copy(
            src_ref=source(lax.bitwise_xor(here, mask)),
            dst_ref=target_ref.at[here],
            send_sem=send_sem.at[mask - 1],
            recv_sem=recv_sem.at[mask - 1],
            device_id={"ctx": lax.bitwise_xor(here, mask)},
            device_id_type=MESH,
        )
        for mask in range(1, count)
    ]


class Line:
    def __init__(self, whole_ref, depth, send_sem, recv_sem):
        self.whole, self.depth = whole_ref, depth
        self.send_sem, self.recv_sem = send_sem, recv_sem
        self.me = lax.axis_index("dp")

    def copy(self, way, step, block):
        block = jnp.clip(block, 0, self.depth - 1)
        target = jnp.clip(self.me + way, 0, self.depth - 1)
        n = 0 if way > 0 else 1
        return pltpu.make_async_remote_copy(
            src_ref=self.whole.at[block],
            dst_ref=self.whole.at[block],
            send_sem=self.send_sem.at[n, step - 1],
            recv_sem=self.recv_sem.at[n, step - 1],
            device_id={"dp": target},
            device_id_type=MESH,
        )

    def sends(self, step, act):
        me, depth = self.me, self.depth

        @pl.when((me + 1 < depth) & (me - step + 1 >= 0))
        def _():
            act(self.copy(1, step, me - step + 1))

        @pl.when((me >= 1) & (me + step - 1 < depth))
        def _():
            act(self.copy(-1, step, me + step - 1))

    def start(self, step):
        self.sends(step, lambda copy: copy.start())

    def arrive(self, step):
        @pl.when(self.me - step >= 0)
        def _():
            self.copy(1, step, self.me - step).wait_recv()

        @pl.when(self.me + step < self.depth)
        def _():
            self.copy(-1, step, self.me + step).wait_recv()

    def finish(self):
        for step in range(1, self.depth):
            self.sends(step, lambda copy: copy.wait_send())


def front_kernel(
    links,
    depth,
    tokens_ref,
    head_pieces_ref,
    pieces_ref,
    small_ref,
    normed_ref,
    head_ref,
    block_ref,
    table_ref,
    rows_v,
    normed_v,
    head_v,
    piece_v,
    shards_v,
    load_sem,
    store_sem,
    share_send,
    share_recv,
    head_send,
    head_recv,
    piece_send,
    piece_recv,
    line_send,
    line_recv,
    shard_send,
    shard_recv,
):
    count, half = links.count, links.half
    size = 2 * half
    here, layer = lax.axis_index("ctx"), lax.axis_index("dp")
    shards = count * depth
    shard = layer * count + here
    thin = small_ref.shape[1]
    own_ref = tokens_ref.at[lax.axis_index("tp")]

    def peer(mask):
        other = lax.bitwise_xor(shard, mask)
        return {"dp": other // count, "ctx": other % count}

    barrier = pltpu.get_barrier_semaphore()

    def greet_peer(mask, _):
        pl.semaphore_signal(barrier, 1, device_id=peer(mask), device_id_type=MESH)
        return 0

    lax.fori_loop(1, shards, greet_peer, 0)
    pl.semaphore_wait(barrier, shards - 1)

    def gains(mask):
        return pltpu.make_async_remote_copy(
            src_ref=small_ref,
            dst_ref=shards_v.at[shard],
            send_sem=shard_send.at[mask],
            recv_sem=shard_recv.at[mask],
            device_id=peer(mask),
            device_id_type=MESH,
        )

    def gains_start(mask, _):
        gains(mask).start()
        return 0

    def gains_wait(mask, _):
        gains(mask).wait()
        return 0

    lax.fori_loop(1, shards, gains_start, 0)
    heads = piece_copies(
        count, lambda i: head_pieces_ref.at[i], head_ref.at[layer], head_send, head_recv
    )
    pieces = piece_copies(
        count, lambda i: pieces_ref.at[i], block_ref, piece_send, piece_recv
    )
    for copy in heads:
        copy.start()
    own_pieces = [
        pltpu.make_async_copy(head_pieces_ref.at[here], head_v, load_sem.at[2]),
        pltpu.make_async_copy(pieces_ref.at[here], piece_v, load_sem.at[0]),
    ]
    for copy in own_pieces:
        copy.start()
    first = pltpu.make_async_copy(own_ref, rows_v.at[pl.ds(0, size)], load_sem.at[1])
    first.start()
    shares = links.sharing(own_ref, rows_v, share_send, share_recv)
    links.pass_on(shares, 0)
    line = Line(head_ref, depth, line_send, line_recv)
    own_stores = [
        pltpu.make_async_copy(head_v, head_ref.at[layer, here], load_sem.at[2]),
        pltpu.make_async_copy(piece_v, block_ref.at[here], load_sem.at[0]),
    ]
    for load, store in zip(own_pieces, own_stores):
        load.wait()
        store.start()
    for copy in heads:
        copy.wait()
    own_stores[0].wait()
    line.start(1)
    for copy in pieces:
        copy.start()
    shards_v[shard] = small_ref[...]
    lax.fori_loop(1, shards, gains_wait, 0)
    for n in range(shards):
        table_ref[:, n * thin : (n + 1) * thin] = shards_v[n]
    chunk = min(32, half)
    stores = []
    for i in range(max(count, depth)):
        if 0 < i < depth:
            line.arrive(i)
            if i + 1 < depth:
                line.start(i + 1)
        if i >= count:
            continue
        if i == 0:
            first.wait()
        else:
            for part in (0, 1):
                shares[(i, part)].wait_recv()
            links.pass_on(shares, i)
        for part in (0, 1):
            base = links.start_row(i, part)

            def norm(step, _, base=base):
                at = pl.ds(pl.multiple_of(base + step * chunk, chunk), chunk)
                normed = normalize(rows_v[at, :].astype(F32))[0]
                normed_v[at, :] = (normed * table_ref[0:1, :] + table_ref[1:2, :]).astype(BF16)
                return 0

            lax.fori_loop(0, half // chunk, norm, 0)
            store = pltpu.make_async_copy(
                links.rows(normed_v, i, part), links.rows(normed_ref, i, part), store_sem.at[2 * i + part]
            )
            store.start()
            stores.append(store)
    for copy in stores + pieces + own_stores[1:]:
        copy.wait()
    line.finish()
    for pair in links.pairs:
        shares[pair].wait_send()


def front(tokens, head_pieces, pieces, small, count, depth):
    _, rows, width = tokens.shape
    length = rows * count
    links = Links(count, rows // 2)
    copies = len(links.pairs)
    anywhere = pl.BlockSpec(memory_space=pl.ANY)
    inside = pl.BlockSpec(memory_space=pltpu.VMEM)
    dma = pltpu.SemaphoreType.DMA
    return pl.pallas_call(
        functools.partial(front_kernel, links, depth),
        out_shape=(
            jax.ShapeDtypeStruct((length, width), BF16),
            jax.ShapeDtypeStruct((depth, *head_pieces.shape), BF16),
            jax.ShapeDtypeStruct(pieces.shape, BF16),
            jax.ShapeDtypeStruct((8, width), F32),
        ),
        in_specs=[anywhere, anywhere, anywhere, inside],
        out_specs=(anywhere, anywhere, anywhere, inside),
        scratch_shapes=[
            pltpu.VMEM((length, width), BF16),
            pltpu.VMEM((length, width), BF16),
            pltpu.VMEM(head_pieces.shape[1:], BF16),
            pltpu.VMEM(pieces.shape[1:], BF16),
            pltpu.VMEM((count * depth, *small.shape), F32),
            dma((3,)),
            dma((2 * count,)),
            dma((copies,)),
            dma((copies,)),
            dma((count - 1,)),
            dma((count - 1,)),
            dma((count - 1,)),
            dma((count - 1,)),
            dma((2, depth - 1)),
            dma((2, depth - 1)),
            dma((count * depth,)),
            dma((count * depth,)),
        ],
        compiler_params=pltpu.CompilerParams(
            collective_id=1, has_side_effects=True, vmem_limit_bytes=40 * 1024 * 1024
        ),
        cost_estimate=pl.CostEstimate(
            flops=20 * length * width, bytes_accessed=120000000, transcendentals=0
        ),
        name="front",
    )(tokens, head_pieces, pieces, small)


def end_kernel(
    count,
    depth,
    heads,
    rows_ref,
    vectors_ref,
    firsts_ref,
    biases_ref,
    query_ref,
    key_ref,
    value_ref,
    out_ref,
    fall_ref,
    features_ref,
    totals_ref,
    block_v,
    shards_v,
    pair_v,
    landing_v,
    bias_v,
    load_sem,
    piece_send,
    piece_recv,
    shard_send,
    shard_recv,
    bias_send,
    bias_recv,
    total_send,
    total_recv,
):
    here, layer = lax.axis_index("ctx"), lax.axis_index("dp")
    shard = layer * count + here
    partner = {"tp": 1 - lax.axis_index("tp")}
    thin = query_ref.shape[0]
    wide = heads * 3 * HEAD_DIM
    low, high = (count - 1).bit_length(), (depth - 1).bit_length()
    greet_all([partner] + others("ctx", count) + others("dp", depth))
    pieces = piece_copies(
        count,
        lambda i: rows_ref.at[pl.ds(pl.multiple_of(i * thin, thin), thin)],
        block_v,
        piece_send,
        piece_recv,
    )
    pieces.append(
        pltpu.make_async_copy(
            rows_ref.at[pl.ds(pl.multiple_of(here * thin, thin), thin)], block_v.at[here], load_sem.at[0]
        )
    )
    for copy in pieces:
        copy.start()
    for n in range(count * depth):
        at = slice(n * thin, (n + 1) * thin)
        shards_v[n, 0:4, :] = vectors_ref[0:4, at]
        shards_v[n, 4:8, :] = firsts_ref[0:4, at]

    def exchange(source, target, device, send, recv):
        copy = pltpu.make_async_remote_copy(
            src_ref=source,
            dst_ref=target,
            send_sem=send,
            recv_sem=recv,
            device_id=device,
            device_id_type=MESH,
        )
        copy.start()
        return copy

    bias_v[0] = biases_ref[0]
    bias_v[1] = biases_ref[1]
    stage = [
        exchange(shards_v, pair_v, partner, shard_send.at[low + high], shard_recv.at[low + high]),
        exchange(bias_v.at[1], bias_v.at[2], partner, bias_send.at[high], bias_recv.at[high]),
    ]
    for copy in stage:
        copy.wait()
    shards_v[...] += pair_v[...]
    bias_v[0] += bias_v[2]
    totals = []
    devices = axis_bits("ctx", count) + axis_bits("dp", depth)
    for bit in range(low + high - 1, -1, -1):
        reach = 1 << bit
        mine = shard // reach * reach
        theirs = (shard // reach ^ 1) * reach
        stage = [
            exchange(
                shards_v.at[pl.ds(theirs, reach)],
                landing_v.at[pl.ds(reach, reach)],
                devices[bit],
                shard_send.at[bit],
                shard_recv.at[bit],
            )
        ]
        if bit >= low:
            n = bit - low
            stage.append(
                exchange(bias_v.at[0], bias_v.at[3 + n], devices[bit], bias_send.at[n], bias_recv.at[n])
            )
        for copy in stage:
            copy.wait()
        shards_v[pl.ds(mine, reach)] += landing_v[reach : 2 * reach]
        if bit >= low:
            bias_v[0] += bias_v[3 + bit - low]
        if bit == low:
            totals_ref[here] = bias_v[0]
            totals = [
                exchange(
                    bias_v.at[0], totals_ref.at[here], device, total_send.at[n], total_recv.at[n]
                )
                for n, device in enumerate(others("ctx", count))
            ]
    features_ref[...] = shards_v[shard]
    for copy in pieces + totals:
        copy.wait()
    for c in range(count):
        for j in range(heads):
            to = slice((c * heads + j) * HEAD_DIM, (c * heads + j + 1) * HEAD_DIM)
            for n, ref in enumerate((query_ref, key_ref, value_ref)):
                column = (3 * j + n) * HEAD_DIM
                ref[:, to] = block_v[c, :, column : column + HEAD_DIM].astype(F32)
        rows = slice(c * heads * HEAD_DIM, (c + 1) * heads * HEAD_DIM)
        out_ref[rows, :] = block_v[c, :, wide : wide + heads * HEAD_DIM].astype(F32).T
        fall_ref[c] = block_v[c, :, wide + heads * HEAD_DIM :].astype(F32).T


def end(rows, vectors, firsts, biases, heads, count, depth):
    low, high = (count - 1).bit_length(), (depth - 1).bit_length()
    thin = rows.shape[0] // count
    columns = rows.shape[1]
    local = count * heads * HEAD_DIM
    inside = pl.BlockSpec(memory_space=pltpu.VMEM)
    dma = pltpu.SemaphoreType.DMA
    shards = (count * depth, 8, thin)
    return pl.pallas_call(
        functools.partial(end_kernel, count, depth, heads),
        out_shape=(
            jax.ShapeDtypeStruct((thin, local), F32),
            jax.ShapeDtypeStruct((thin, local), F32),
            jax.ShapeDtypeStruct((thin, local), F32),
            jax.ShapeDtypeStruct((local, thin), F32),
            jax.ShapeDtypeStruct((count, columns - heads * 4 * HEAD_DIM, thin), F32),
            jax.ShapeDtypeStruct((8, thin), F32),
            jax.ShapeDtypeStruct((count, 1, biases.shape[2]), F32),
        ),
        in_specs=[pl.BlockSpec(memory_space=pl.ANY), inside, inside, inside],
        out_specs=(inside,) * 7,
        scratch_shapes=[
            pltpu.VMEM((count, thin, columns), BF16),
            pltpu.VMEM(shards, F32),
            pltpu.VMEM(shards, F32),
            pltpu.VMEM(shards, F32),
            pltpu.VMEM((3 + high, 1, biases.shape[2]), F32),
            dma((1,)),
            dma((count - 1,)),
            dma((count - 1,)),
            dma((low + high + 1,)),
            dma((low + high + 1,)),
            dma((high + 1,)),
            dma((high + 1,)),
            dma((count - 1,)),
            dma((count - 1,)),
        ],
        compiler_params=pltpu.CompilerParams(
            collective_id=7, has_side_effects=True, vmem_limit_bytes=24 * 1024 * 1024
        ),
        cost_estimate=pl.CostEstimate(flops=0, bytes_accessed=40000000, transcendentals=0),
        name="end",
    )(rows, vectors, firsts, biases)


def attend_kernel(
    links,
    heads,
    rows_ref,
    weight_ref,
    shift_ref,
    cotangent_ref,
    tokens_ref,
    table_ref,
    qkv_ref,
    mixed_ref,
    log_ref,
    grads_full_ref,
    residual_ref,
    second_ref,
    whole_ref,
    own_v,
    rows_v,
    weight_v,
    qkv_v,
    mixed_v,
    scores_v,
    kept_v,
    send_v,
    recv_v,
    load_sem,
    store_sem,
    pair_send,
    pair_recv,
    share_send,
    share_recv,
    sum_send,
    sum_recv,
):
    count, half = links.count, links.half
    size = 2 * half
    here = lax.axis_index("ctx")
    core = lax.axis_index("tp")
    partner = {"tp": 1 - core}
    grads_ref = cotangent_ref.at[core]
    narrow = weight_ref.shape[1]
    wide = heads * 3 * HEAD_DIM // 2
    links.greet([partner])
    theirs = pltpu.make_async_remote_copy(
        src_ref=weight_ref,
        dst_ref=weight_v.at[1],
        send_sem=pair_send.at[0],
        recv_sem=pair_recv.at[0],
        device_id=partner,
        device_id_type=MESH,
    )
    theirs.start()
    shares = links.sharing(grads_ref, grads_full_ref, share_send, share_recv)
    sums = links.summing(send_v, recv_v, sum_send, sum_recv)
    links.pass_on(shares, 0)
    ours = pltpu.make_async_copy(weight_ref, weight_v.at[0], load_sem.at[0])
    ours.start()
    own = pltpu.make_async_copy(tokens_ref.at[core], own_v, load_sem.at[4])
    own.start()

    def load(n):
        return pltpu.make_async_copy(
            rows_ref.at[pl.ds(n * size, size)], rows_v.at[n % 2], load_sem.at[2 + n % 2]
        )

    coming = load(0)
    coming.start()
    ours.wait()
    theirs.wait_recv()
    wholes = []
    for core in (0, 1):
        copy = pltpu.make_async_copy(weight_v.at[core], whole_ref.at[core], store_sem.at[core])
        copy.start()
        wholes.append(copy)
    tile = 256 if wide % 256 == 0 else HEAD_DIM
    for n in range(count):
        coming.wait()
        if n + 1 < count:
            coming = load(n + 1)
            coming.start()
        for core in (0, 1):

            def step(m, _, n=n, core=core):
                at = pl.ds(pl.multiple_of(m * tile, tile), tile)
                to = pl.ds(pl.multiple_of(core * wide + m * tile, tile), tile)
                value = product(rows_v[n % 2], weight_v[core, :, at]) + shift_ref[0:1, to]
                qkv_v[n * size : (n + 1) * size, to] = value.astype(BF16)
                return 0

            lax.fori_loop(0, wide // tile, step, 0)
    keep_qkv = pltpu.make_async_copy(qkv_v, qkv_ref, store_sem.at[2])
    keep_qkv.start()
    own_grads = pltpu.make_async_copy(grads_ref, rows_v.at[0], load_sem.at[1])
    own_grads.start()
    keep = pltpu.make_async_copy(rows_v.at[0], grads_full_ref.at[pl.ds(0, size)], load_sem.at[1])

    def one_head(head, _):
        @pl.when(head == heads // 2)
        def _():
            for i in range(1, (count + 1) // 2):
                for part in (0, 1):
                    shares[(i, part)].wait_recv()
                links.pass_on(shares, i)

        attend_forward_head(here, head, size, count, qkv_v, mixed_v, log_ref, scores_v)
        return 0

    lax.fori_loop(0, heads, one_head, 0)
    keep_mixed = pltpu.make_async_copy(mixed_v, mixed_ref, store_sem.at[3])
    keep_mixed.start()
    own_grads.wait()
    keep.start()
    chip = heads * HEAD_DIM // 2
    for i in range(count - 1, -1, -1):

        def out_rows(core, i=i):
            at = slice(core * chip, (core + 1) * chip)
            first = [links.start_row(i, part) for part in (0, 1)]
            return jnp.concatenate([mixed_v[row : row + half, at] for row in first], axis=0)

        links.terms(
            i,
            lambda at: across(out_rows(0), weight_v[0, at, wide:narrow])
            + across(out_rows(1), weight_v[1, at, wide:narrow]),
            residual_ref.shape[1],
            kept_v,
            send_v,
        )
        if i >= count // 2:
            for part in (0, 1):
                sums[(i, part)].start()

    def norm(part, at, to, value):
        residual = own_v[to, :].astype(F32) + (value + table_ref[4:5, :])
        residual_ref[to, :] = residual
        normed = normalize(residual)[0]
        second_ref[to, :] = (normed * table_ref[2:3, :] + table_ref[3:4, :]).astype(BF16)

    own.wait()
    links.combine(sums, kept_v, send_v, recv_v, count // 2 - 1, 0, norm)
    for i in range(1, count):
        for part in (0, 1):
            if i >= (count + 1) // 2:
                shares[(i, part)].wait_recv()
    for copy in wholes + [keep_qkv, keep_mixed, keep]:
        copy.wait()
    theirs.wait_send()
    for pair in links.pairs:
        sums[pair].wait_send()
        shares[pair].wait_send()


def attend_forward_head(here, head, size, blocks, qkv_v, mixed_v, log_ref, scores_v):
    scaling = HEAD_DIM ** (-0.5)
    behind = lax.broadcasted_iota(jnp.int32, (size, size), 1) <= lax.broadcasted_iota(
        jnp.int32, (size, size), 0
    )
    column = pl.multiple_of(head * (3 * HEAD_DIM), HEAD_DIM)
    query_at = pl.ds(column, HEAD_DIM)
    key_at = pl.ds(pl.multiple_of(column + HEAD_DIM, HEAD_DIM), HEAD_DIM)
    value_at = pl.ds(pl.multiple_of(column + 2 * HEAD_DIM, HEAD_DIM), HEAD_DIM)
    head_at = pl.ds(pl.multiple_of(head * HEAD_DIM, HEAD_DIM), HEAD_DIM)
    for i in range(blocks):
        at = pl.ds(rows_of(here, i, size), size)
        queries = qkv_v[at, query_at]
        highest = jnp.full((size, 1), NEGATIVE, F32)
        for j in range(i + 1):
            keys = qkv_v[pl.ds(rows_of(here, j, size), size), key_at]
            scores = across(queries, keys) * scaling
            if j == i:
                scores = jnp.where(behind, scores, NEGATIVE)
            scores_v[:, j * size : (j + 1) * size] = scores
            highest = jnp.maximum(highest, jnp.max(scores, axis=1, keepdims=True))
        row_total = jnp.zeros((size, 1), F32)
        mixed = jnp.zeros((size, HEAD_DIM), F32)
        for j in range(i + 1):
            exponent = jnp.exp(scores_v[:, j * size : (j + 1) * size] - highest)
            row_total = row_total + jnp.sum(exponent, axis=1, keepdims=True)
            values = qkv_v[pl.ds(rows_of(here, j, size), size), value_at]
            mixed = mixed + product(exponent.astype(BF16), values)
        mixed_v[at, head_at] = (mixed / row_total).astype(BF16)
        log_total = jnp.broadcast_to(highest + jnp.log(row_total), (size, HEAD_DIM))
        log_ref[head, :, at] = log_total.T[0:8, :]


def attend(rows, weight, shift, cotangent, tokens, table, heads, count):
    length, width = rows.shape
    size = length // count
    narrow = weight.shape[1]
    columns = heads * 3 * HEAD_DIM
    links = Links(count, size // 2)
    half, copies = links.half, len(links.pairs)
    pairs = heads * length * (length + size) // 2
    anywhere = pl.BlockSpec(memory_space=pl.ANY)
    inside = pl.BlockSpec(memory_space=pltpu.VMEM)
    dma = pltpu.SemaphoreType.DMA
    return pl.pallas_call(
        functools.partial(attend_kernel, links, heads),
        out_shape=(
            jax.ShapeDtypeStruct((length, columns), BF16),
            jax.ShapeDtypeStruct((length, heads * HEAD_DIM), BF16),
            jax.ShapeDtypeStruct((heads, 8, length), F32),
            jax.ShapeDtypeStruct((length, width), BF16),
            jax.ShapeDtypeStruct((size, width), F32),
            jax.ShapeDtypeStruct((size, width), BF16),
            jax.ShapeDtypeStruct((2, width, narrow), BF16),
        ),
        in_specs=[anywhere, anywhere, inside, anywhere, anywhere, inside],
        out_specs=(anywhere, anywhere, inside, anywhere, inside, inside, anywhere),
        scratch_shapes=[
            pltpu.VMEM((size, width), BF16),
            pltpu.VMEM((2, size, width), BF16),
            pltpu.VMEM((2, width, narrow), BF16),
            pltpu.VMEM((length, columns), BF16),
            pltpu.VMEM((length, heads * HEAD_DIM), BF16),
            pltpu.VMEM((size, length), F32),
            pltpu.VMEM((count, half, width), F32),
            pltpu.VMEM((copies, half, width), BF16),
            pltpu.VMEM((copies, half, width), BF16),
            dma((5,)),
            dma((4,)),
            dma((1,)),
            dma((1,)),
            dma((copies,)),
            dma((copies,)),
            dma((copies,)),
            dma((copies,)),
        ],
        compiler_params=pltpu.CompilerParams(
            collective_id=2, has_side_effects=True, vmem_limit_bytes=60 * 1024 * 1024
        ),
        cost_estimate=pl.CostEstimate(
            flops=pairs * HEAD_DIM * 8 + 2 * length * width * heads * HEAD_DIM * 4,
            bytes_accessed=length * width * 8,
            transcendentals=pairs,
        ),
        name="attend",
    )(rows, weight, shift, cotangent, tokens, table)


def attend_back_kernel(
    links,
    heads,
    own_ref,
    weight_ref,
    qkv_ref,
    mixed_ref,
    log_ref,
    hid_ref,
    fall_ref,
    first_ref,
    residual_ref,
    late_ref,
    table_ref,
    full_ref,
    result_ref,
    low_ref,
    late_grad_ref,
    residual_v,
    weight_v,
    qkv_v,
    mixed_v,
    big_v,
    shared_v,
    came_v,
    grad_v,
    rows_v,
    hid_v,
    key_v,
    value_v,
    kept_v,
    send_v,
    recv_v,
    load_sem,
    grad_send,
    grad_recv,
    grad_store,
    share_send,
    share_recv,
    sum_send,
    sum_recv,
):
    half, count = links.half, links.count
    size = 2 * half
    here = lax.axis_index("ctx")
    chip = weight_v.shape[2]
    wide = heads * 3 * HEAD_DIM // 2
    narrow = residual_v.shape[1]
    middle = hid_v.shape[2] // 2
    partner = {"tp": 1 - lax.axis_index("tp")}
    links.greet([partner])
    shares = links.sharing(own_ref, full_ref, share_send, share_recv)
    sums = links.summing(send_v, recv_v, sum_send, sum_recv)
    links.pass_on(shares, 0)
    falls = [shared_v.at[pl.ds(n * narrow, narrow), pl.ds(0, middle)] for n in (0, 1)]
    theirs_v = shared_v.at[pl.ds(0, big_v.shape[1])]
    late_v = shared_v.at[pl.ds(0, big_v.shape[1]), pl.ds(0, late_ref.shape[1])]
    loads = [
        pltpu.make_async_copy(source, target, load_sem.at[n])
        for n, (source, target) in enumerate(
            (
                (fall_ref.at[pl.ds(0, narrow), pl.ds(0, middle)], falls[0]),
                (fall_ref.at[pl.ds(0, narrow), pl.ds(middle, middle)], falls[1]),
                (own_ref, rows_v),
                (weight_ref.at[:, :, pl.ds(weight_ref.shape[2] - chip, chip)], weight_v),
                (qkv_ref, qkv_v),
                (mixed_ref, mixed_v),
                (rows_v, full_ref.at[pl.ds(0, size)]),
                (first_ref, big_v),
                (residual_ref.at[:, pl.ds(0, narrow)], residual_v),
                (late_ref, late_v),
                (late_v, late_grad_ref.at[:, pl.ds(wide + chip, late_ref.shape[1])]),
            )
        )
    ]
    for n in (0, 1, 2, 3, 4, 5, 7, 8):
        loads[n].start()
    key_v[...] = jnp.zeros_like(key_v)
    value_v[...] = jnp.zeros_like(value_v)
    for copy in loads[:2]:
        copy.wait()
    out_terms(
        links,
        hid_ref,
        hid_v,
        lambda rows, at: across(rows[:, 0:middle], falls[0][at, :])
        + across(rows[:, middle : 2 * middle], falls[1][at, :]),
        narrow,
        kept_v,
        send_v,
        load_sem,
        11,
    )
    loads[9].start()
    for copy in loads[2:6]:
        copy.wait()
    loads[6].start()
    loads[9].wait()
    loads[10].start()
    together = min(2, heads)
    for i in range(count):
        if i:
            for part in (0, 1):
                shares[(i, part)].wait_recv()
            links.pass_on(shares, i)
            if i == 1:
                loads[6].wait()
            unit_loads = links.loads(full_ref, rows_v, i, load_sem, 11)
            for copy in unit_loads:
                copy.start()
            for copy in unit_loads:
                copy.wait()
        if i + 1 == count:
            for j in range(count - 1, count // 2 - 1, -1):
                for part in (0, 1):
                    sums[(j, part)].start()
        for core in (0, 1):
            term = product(rows_v[...], weight_v[core]).astype(BF16)
            for part in (0, 1):
                row = links.start_row(i, part)
                grad_v[row : row + half, core * chip : (core + 1) * chip] = term[
                    part * half : (part + 1) * half
                ]
        blocks = [links.block(i, part) for part in (0, 1)]
        firsts = [links.start_row(i, part) for part in (0, 1)]

        def one(n, _, blocks=blocks, firsts=firsts):
            part, first_head = n // (heads // together), n % (heads // together) * together
            row = pl.multiple_of(firsts[0] + part * (firsts[1] - firsts[0]), half)
            block = lax.bitwise_xor(here, blocks[0] + part * (blocks[1] - blocks[0]))
            attend_backward_unit(
                here,
                [first_head + m for m in range(together)],
                block,
                part * half,
                row,
                half,
                qkv_v,
                grad_v,
                mixed_v,
                log_ref,
                result_ref,
                key_v,
                value_v,
            )
            return 0

        lax.fori_loop(0, 2 * heads // together, one, 0)

    def store_head(head, _):
        at = pl.ds(pl.multiple_of(head * HEAD_DIM, HEAD_DIM), HEAD_DIM)
        column = head * (3 * HEAD_DIM)
        key_at = pl.ds(pl.multiple_of(column + HEAD_DIM, HEAD_DIM), HEAD_DIM)
        value_at = pl.ds(pl.multiple_of(column + 2 * HEAD_DIM, HEAD_DIM), HEAD_DIM)
        result_ref[:, key_at] = (key_v[:, at] * HEAD_DIM ** (-0.5)).astype(BF16)
        result_ref[:, value_at] = value_v[:, at].astype(BF16)
        return 0

    lax.fori_loop(0, heads, store_head, 0)
    loads[10].wait()
    loads[7].wait()
    end_first = weight_grads(
        partner,
        big_v,
        result_ref,
        theirs_v.at[:, pl.ds(0, wide)],
        came_v.at[:, pl.ds(0, wide)],
        (late_grad_ref.at[:, pl.ds(0, wide)],),
        grad_send.at[0],
        grad_recv.at[0],
        (grad_store.at[0],),
    )
    again = pltpu.make_async_copy(full_ref, big_v, load_sem.at[7])
    again.start()
    links.combine(sums, kept_v, send_v, recv_v, count // 2 - 1, 1)
    again.wait()
    end_second = weight_grads(
        partner,
        big_v,
        mixed_v,
        theirs_v.at[:, pl.ds(wide, chip)],
        came_v.at[:, pl.ds(wide, chip)],
        (late_grad_ref.at[:, pl.ds(wide, chip)],),
        grad_send.at[1],
        grad_recv.at[1],
        (grad_store.at[1],),
    )
    loads[8].wait()

    def low(part, at, to, value):
        low_ref[to, :] = (residual_v[to, :] + (value + table_ref[5:6, 0:narrow])).astype(BF16)

    links.combine(sums, kept_v, send_v, recv_v, 0, 0, low)
    end_first()
    end_second()
    for pair in links.pairs:
        sums[pair].wait_send()
        shares[pair].wait_send()


def attend_backward_unit(
    here, heads, block, offset, row, half, qkv_v, grad_v, mixed_v, log_ref, result_ref, key_v, value_v
):
    size = 2 * half
    scaling = HEAD_DIM ** (-0.5)
    at = pl.ds(row, half)

    def columns(head, n):
        return pl.ds(pl.multiple_of(head * (3 * HEAD_DIM) + n * HEAD_DIM, HEAD_DIM), HEAD_DIM)

    places = [pl.ds(pl.multiple_of(head * HEAD_DIM, HEAD_DIM), HEAD_DIM) for head in heads]
    queries = [qkv_v[at, columns(head, 0)] for head in heads]
    grads = [grad_v[at, place] for place in places]
    centres = [
        jnp.sum((grad.astype(F32) * mixed_v[at, place].astype(F32)).T, axis=0, keepdims=True)
        for grad, place in zip(grads, places)
    ]
    logs = [log_ref[head, 0:1, at] for head in heads]

    def step(j, query_grads, last):
        there = pl.ds(rows_of(here, j, size), size)
        results = []
        for n, head in enumerate(heads):
            keys = qkv_v[there, columns(head, 1)]
            values = qkv_v[there, columns(head, 2)]
            weights = jnp.exp(across(keys, queries[n]) * scaling - logs[n])
            if last:
                behind = lax.broadcasted_iota(jnp.int32, (size, half), 0) <= offset + (
                    lax.broadcasted_iota(jnp.int32, (size, half), 1)
                )
                weights = jnp.where(behind, weights, 0.0)
            slopes = (weights * (across(values, grads[n]) - centres[n])).astype(BF16)
            value_v[there, places[n]] += product(weights.astype(BF16), grads[n])
            key_v[there, places[n]] += product(slopes, queries[n])
            results.append(query_grads[n] + inner(slopes, keys))
        return tuple(results)

    query_grads = lax.fori_loop(
        0,
        block,
        lambda j, found: step(j, found, False),
        tuple(jnp.zeros((half, HEAD_DIM), F32) for _ in heads),
    )
    query_grads = step(block, query_grads, True)
    for n, head in enumerate(heads):
        result_ref[at, columns(head, 0)] = (query_grads[n] * scaling).astype(BF16)


def out_terms(links, hid_ref, hid_v, columns, narrow, kept_v, send_v, load_sem, base):
    count, slots = links.count, hid_v.shape[0]
    order = list(range(count - 1, -1, -1))

    def load(n):
        slot = n % slots
        copies = links.loads(hid_ref, hid_v.at[slot], order[n], load_sem, base + 2 * slot)
        for copy in copies:
            copy.start()
        return copies

    coming = [load(n) for n in range(slots)]
    for n, i in enumerate(order):
        for copy in coming[n]:
            copy.wait()
        links.terms(i, lambda at, n=n: columns(hid_v.at[n % slots], at), narrow, kept_v, send_v)
        if n + slots < count:
            coming.append(load(n + slots))


def attend_back(
    own, weight, qkv, mixed, log_total, hid, fall_weight, first, residual, late, table, count
):
    rows, width = own.shape
    length, columns = qkv.shape
    heads = columns // (3 * HEAD_DIM)
    hidden = hid.shape[1]
    links = Links(count, rows // 2)
    half, copies = links.half, len(links.pairs)
    narrow = width // 2
    pairs = heads * length * (length + rows) // 2
    anywhere = pl.BlockSpec(memory_space=pl.ANY)
    inside = pl.BlockSpec(memory_space=pltpu.VMEM)
    dma = pltpu.SemaphoreType.DMA
    return pl.pallas_call(
        functools.partial(attend_back_kernel, links, heads),
        out_shape=(
            jax.ShapeDtypeStruct((length, width), BF16),
            jax.ShapeDtypeStruct((length, columns), BF16),
            jax.ShapeDtypeStruct((rows, narrow), BF16),
            jax.ShapeDtypeStruct((width, 2 * heads * HEAD_DIM + late.shape[1]), BF16),
        ),
        in_specs=[anywhere] * 4 + [inside] + [anywhere] * 5 + [inside],
        out_specs=(anywhere, inside, inside, anywhere),
        scratch_shapes=[
            pltpu.VMEM((rows, narrow), F32),
            pltpu.VMEM((2, width, heads * HEAD_DIM // 2), BF16),
            pltpu.VMEM(qkv.shape, BF16),
            pltpu.VMEM(mixed.shape, BF16),
            pltpu.VMEM((length, width), BF16),
            pltpu.VMEM((width, max(2 * heads * HEAD_DIM, hidden // 2)), BF16),
            pltpu.VMEM((width, 2 * heads * HEAD_DIM), BF16),
            pltpu.VMEM(mixed.shape, BF16),
            pltpu.VMEM((rows, width), BF16),
            pltpu.VMEM((1, rows, hidden), BF16),
            pltpu.VMEM(mixed.shape, F32),
            pltpu.VMEM(mixed.shape, F32),
            pltpu.VMEM((count, half, narrow), F32),
            pltpu.VMEM((copies, half, narrow), BF16),
            pltpu.VMEM((copies, half, narrow), BF16),
            dma((13,)),
            dma((3, width // 512)),
            dma((3, width // 512)),
            dma((3, width // 512)),
            dma((copies,)),
            dma((copies,)),
            dma((copies,)),
            dma((copies,)),
        ],
        compiler_params=pltpu.CompilerParams(
            collective_id=4, has_side_effects=True, vmem_limit_bytes=63 * 1024 * 1024
        ),
        cost_estimate=pl.CostEstimate(
            flops=pairs * HEAD_DIM * 20 + 2 * length * width * (heads * HEAD_DIM + hidden // 2),
            bytes_accessed=length * width * 6 + length * columns * 4 + length * hidden * 2,
            transcendentals=pairs,
        ),
        name="attend_back",
    )(own, weight, qkv, mixed, log_total, hid, fall_weight, first, residual, late, table)


def first_back_kernel(
    links,
    grads_ref,
    weight_ref,
    hid_ref,
    fall_ref,
    low_ref,
    residual_ref,
    back_ref,
    tokens_ref,
    table_ref,
    hidden_ref,
    out_ref,
    input_ref,
    vector_ref,
    bias_ref,
    fall_grad_ref,
    rise_grad_ref,
    grads_v,
    weight_v,
    hid_v,
    fall_v,
    kept_v,
    send_v,
    recv_v,
    kept_w,
    send_w,
    recv_w,
    residual_v,
    tokens_v,
    high_v,
    block_v,
    load_sem,
    pair_send,
    pair_recv,
    piece_send,
    piece_recv,
    sum_send,
    sum_recv,
    late_send,
    late_recv,
):
    count, half = links.count, links.half
    size = 2 * half
    wide = weight_v.shape[2]
    thin = hidden_ref.shape[0] // count
    hidden = hidden_ref.shape[1] * 2 // 3
    narrow = fall_v.shape[0]
    core = lax.axis_index("tp")
    partner = {"tp": 1 - core}
    links.greet([partner], range(1, count))
    sums = links.summing(send_v, recv_v, sum_send, sum_recv)
    lates = links.summing(send_w, recv_w, late_send, late_recv)
    pieces = piece_copies(
        count,
        lambda i: hidden_ref.at[pl.ds(pl.multiple_of(i * thin, thin), thin)],
        block_v,
        piece_send,
        piece_recv,
    )
    here = lax.axis_index("ctx")
    pieces.append(
        pltpu.make_async_copy(
            hidden_ref.at[pl.ds(pl.multiple_of(here * thin, thin), thin)],
            block_v.at[here],
            load_sem.at[10],
        )
    )
    right = pl.ds(narrow, narrow)
    left = pl.ds(0, narrow)

    def both_cores(n, source, target_ref, rows, columns):
        target = target_ref.at[core, rows, columns]
        return [
            pltpu.make_async_copy(source, target, load_sem.at[11 + n]),
            pltpu.make_async_remote_copy(
                src_ref=source,
                dst_ref=target,
                send_sem=pair_send.at[n],
                recv_sem=pair_recv.at[n],
                device_id=partner,
                device_id_type=MESH,
            ),
        ]

    lows = both_cores(0, high_v, out_ref, pl.ds(0, size), left)
    low = pltpu.make_async_copy(low_ref, high_v, load_sem.at[11])
    low.start()
    outs = []
    loads = [
        pltpu.make_async_copy(source, target, load_sem.at[n])
        for n, (source, target) in enumerate(
            (
                (weight_ref.at[:, :, pl.ds(0, wide)], weight_v),
                (fall_ref.at[right], fall_v),
            )
        )
    ]
    more = [
        pltpu.make_async_copy(source, target, load_sem.at[15 + n])
        for n, (source, target) in enumerate(
            ((residual_ref.at[:, right], residual_v), (tokens_ref.at[core], tokens_v))
        )
    ]
    for copy in loads:
        copy.start()
    order = list(range(count - 1, -1, -1))
    unit_loads = links.loads(grads_ref, grads_v.at[0], order[0], load_sem, 2)
    for copy in unit_loads + pieces + more:
        copy.start()
    low.wait()
    for copy in lows:
        copy.start()
    bias_ref[...] = jnp.zeros_like(bias_ref)
    vector_ref[...] = jnp.zeros_like(vector_ref)
    loads[0].wait()
    for n, i in enumerate(order):
        for copy in unit_loads:
            copy.wait()
        if n + 1 < count:
            unit_loads = links.loads(
                grads_ref, grads_v.at[(n + 1) % 2], order[n + 1], load_sem, 2 + 2 * ((n + 1) % 2)
            )
            for copy in unit_loads:
                copy.start()
        links.terms(
            i,
            lambda at, n=n: across(grads_v[n % 2, :, :wide], weight_v[0, at, :])
            + across(grads_v[n % 2, :, wide:], weight_v[1, at, :]),
            weight_v.shape[1],
            kept_v,
            send_v,
        )
        if i >= count // 2:
            for part in (0, 1):
                sums[(i, part)].start()
        chunk = min(64, half)

        def bias(step, _, n=n):
            rows = pl.ds(pl.multiple_of(step * chunk, chunk), chunk)
            value = grads_v[n % 2, rows, :].astype(F32)
            bias_ref[0:1, :] += jnp.sum(value, axis=0, keepdims=True)
            return 0

        lax.fori_loop(0, size // chunk, bias, 0)
    loads[1].wait()
    out_terms(
        links,
        hid_ref,
        hid_v,
        lambda rows, at: across(rows[...], fall_v[at, :]),
        narrow,
        kept_w,
        send_w,
        load_sem,
        6,
    )
    for copy in pieces:
        copy.wait()
    for c in range(count):
        rise_grad_ref[:, c * hidden : (c + 1) * hidden] = block_v[c, :, 0:hidden].astype(F32)
        fall_grad_ref[c] = block_v[c, :, hidden:].astype(F32).T
    links.combine(sums, kept_v, send_v, recv_v, count // 2 - 1, 1)
    backs = [
        pltpu.make_async_copy(
            back_ref.at[pl.ds(part * half, half)], kept_v.at[2 + part], load_sem.at[2 + part]
        )
        for part in (0, 1)
    ]
    for copy in backs:
        copy.start()
    for i in range(count - 1, count // 2 - 1, -1):
        for part in (0, 1):
            lates[(i, part)].start()
    for copy in more + backs:
        copy.wait()

    def last(part, at, to, first):
        normed, spread = normalize(tokens_v[to, :].astype(F32))
        grad = kept_v[2 + part, at, :] + norm_back(first * table_ref[0:1, :], normed, spread)
        tokens_v[to, :] = grad.astype(BF16)
        for n, value in enumerate((first * normed, first)):
            vector_ref[n : n + 1, :] += jnp.sum(value, axis=0, keepdims=True)

    def send_part(part):
        rows = pl.ds(part * half, half)
        copies = both_cores(
            1 + part, tokens_v.at[rows], input_ref, rows, pl.ds(0, 2 * narrow)
        )
        for copy in copies:
            copy.start()
        outs.extend(copies)

    links.combine(sums, kept_v, send_v, recv_v, 0, 0, last, send_part)

    def high(part, at, to, value):
        high_v[to, :] = (
            residual_v[to, :] + (value + table_ref[5:6, narrow : 2 * narrow])
        ).astype(BF16)

    for copy in lows:
        copy.wait()
    links.combine(lates, kept_w, send_w, recv_w, count // 2 - 1, 0, high)
    copies = both_cores(3, high_v, out_ref, pl.ds(0, size), right)
    for copy in copies:
        copy.start()
    for copy in outs + copies:
        copy.wait()
    for pair in links.pairs:
        sums[pair].wait_send()
        lates[pair].wait_send()


def first_back(
    grads, weight, hid, fall_weight, low, residual, back, tokens, table, hidden_rows, count
):
    length, columns = grads.shape
    width, hidden = fall_weight.shape
    rows = length // count
    links = Links(count, rows // 2)
    half, copies = links.half, len(links.pairs)
    narrow = width // 2
    thin, piece = hidden_rows.shape[0] // count, hidden_rows.shape[1] * 2 // 3
    anywhere = pl.BlockSpec(memory_space=pl.ANY)
    inside = pl.BlockSpec(memory_space=pltpu.VMEM)
    dma = pltpu.SemaphoreType.DMA
    return pl.pallas_call(
        functools.partial(first_back_kernel, links),
        out_shape=(
            jax.ShapeDtypeStruct((2, rows, width), BF16),
            jax.ShapeDtypeStruct((2, rows, width), BF16),
            jax.ShapeDtypeStruct((8, width), F32),
            jax.ShapeDtypeStruct((1, columns), F32),
            jax.ShapeDtypeStruct((count, piece // 2, thin), F32),
            jax.ShapeDtypeStruct((thin, count * piece), F32),
        ),
        in_specs=[anywhere] * 8 + [inside, anywhere],
        out_specs=(anywhere, anywhere, inside, inside, inside, inside),
        scratch_shapes=[
            pltpu.VMEM((2, rows, columns), BF16),
            pltpu.VMEM((2, width, columns // 2), BF16),
            pltpu.VMEM((2, rows, hidden), BF16),
            pltpu.VMEM((narrow, hidden), BF16),
            pltpu.VMEM((count, half, width), F32),
            pltpu.VMEM((copies, half, width), BF16),
            pltpu.VMEM((copies, half, width), BF16),
            pltpu.VMEM((count, half, narrow), F32),
            pltpu.VMEM((copies, half, narrow), BF16),
            pltpu.VMEM((copies, half, narrow), BF16),
            pltpu.VMEM((rows, narrow), F32),
            pltpu.VMEM((rows, width), BF16),
            pltpu.VMEM((rows, narrow), BF16),
            pltpu.VMEM((count, thin, piece * 3 // 2), BF16),
            dma((17,)),
            dma((4,)),
            dma((4,)),
            dma((count - 1,)),
            dma((count - 1,)),
            dma((copies,)),
            dma((copies,)),
            dma((copies,)),
            dma((copies,)),
        ],
        compiler_params=pltpu.CompilerParams(
            collective_id=5, has_side_effects=True, vmem_limit_bytes=63 * 1024 * 1024
        ),
        cost_estimate=pl.CostEstimate(
            flops=2 * length * width * (columns + hidden // 2),
            bytes_accessed=length * columns * 2 + length * hidden * 2 + width * (columns + hidden) * 2,
            transcendentals=0,
        ),
        name="first_back",
    )(grads, weight, hid, fall_weight, low, residual, back, tokens, table, hidden_rows)


def body(
    tokens,
    cotangent,
    attention_gain,
    attention_bias,
    feedforward_gain,
    feedforward_bias,
    query_weight,
    query_bias,
    key_weight,
    value_weight,
    value_bias,
    output_weight,
    output_bias,
    up_weight,
    up_bias,
    down_weight,
    down_bias,
):
    _, local_rows, model_width = tokens.shape
    ctx, dp = lax.axis_size("ctx"), lax.axis_size("dp")
    here, core = lax.axis_index("ctx"), lax.axis_index("tp")
    thin = query_weight.shape[0]
    heads = query_weight.shape[1] // (HEAD_DIM * ctx)
    hidden = up_weight.shape[1] // ctx
    packed = jnp.stack(
        [w.reshape(thin, ctx, heads, HEAD_DIM) for w in (query_weight, key_weight, value_weight)],
        axis=3,
    ).reshape(thin, ctx, heads * 3 * HEAD_DIM)
    head_pieces = jnp.concatenate(
        [
            packed.transpose(1, 0, 2),
            output_weight.reshape(ctx, heads * HEAD_DIM, thin).transpose(0, 2, 1),
        ],
        axis=2,
    )
    hidden_pieces = jnp.concatenate(
        [
            down_weight.reshape(ctx, hidden, thin).transpose(0, 2, 1),
            up_weight.reshape(thin, ctx, hidden).transpose(1, 0, 2),
        ],
        axis=2,
    )

    small = jnp.stack(
        [attention_gain, attention_bias, feedforward_gain, feedforward_bias, output_bias, down_bias]
    ).astype(F32)
    small = jnp.concatenate([small, jnp.zeros((2, thin), F32)])
    def own_columns(vector):
        return lax.dynamic_index_in_dim(vector.reshape(ctx, -1), here, 0, keepdims=False)

    query_shift = own_columns(query_bias).reshape(heads, HEAD_DIM)
    value_shift = own_columns(value_bias).reshape(heads, HEAD_DIM)
    qkv_shift = jnp.stack([query_shift, jnp.zeros_like(query_shift), value_shift], axis=1)
    shifts = jnp.concatenate([qkv_shift.reshape(-1), own_columns(up_bias)])
    other_shifts = swap(shifts, "tp", 1)
    wide = heads * 3 * HEAD_DIM
    qkv_shift = jnp.concatenate([shifts[:wide], other_shifts[:wide]]).astype(F32)
    rise_shift = jnp.concatenate([shifts[wide:], other_shifts[wide:]]).astype(F32)

    ones, head_weights, hidden_block, table = front(
        tokens, head_pieces, hidden_pieces, small, ctx, dp
    )
    head_weights = head_weights.reshape(model_width, -1)
    hidden_weights = lax.all_gather(
        hidden_block.reshape(ctx * thin, -1), "dp", axis=0, tiled=True
    )
    qkv, mixed, log_total, grads_in, residual, input_two, head_whole = attend(
        ones, head_weights, qkv_shift[None], cotangent, tokens, table, 2 * heads, ctx
    )
    _, hid, _, hidden_both, late, residual_grad, branch_grad, vectors, rise_bias, fall_weight = (
        feed_forward(input_two, grads_in, hidden_weights, rise_shift[None], residual, table, ctx)
    )
    hidden_rows = over_dp(hidden_both)

    _, qkv_grads, low_columns, head_both = attend_back(
        branch_grad,
        head_whole,
        qkv,
        mixed,
        log_total,
        hid,
        fall_weight,
        ones,
        residual,
        late,
        table,
        ctx,
    )
    head_both, hidden_rows = lax.optimization_barrier((head_both, hidden_rows))
    head_rows = over_dp(head_both)
    outputs, input_grads, firsts, qkv_bias, fall_first, rise_grad = first_back(
        qkv_grads,
        head_whole,
        hid,
        fall_weight,
        low_columns,
        residual,
        residual_grad,
        tokens,
        table,
        hidden_rows,
        ctx,
    )
    biases = jnp.concatenate(
        [rise_bias.reshape(2, 1, hidden), qkv_bias.reshape(2, 1, wide)], axis=2
    )
    query_grad, key_grad, value_grad, out_grad, fall_second, features, totals = end(
        head_rows, vectors, firsts, biases, heads, ctx, dp
    )
    fall_grad = jnp.concatenate([fall_first, fall_second], axis=1).reshape(-1, thin)
    totals = totals[:, 0]
    qkv_bias = totals[:, hidden:].reshape(ctx * heads, 3, HEAD_DIM)
    return (
        outputs,
        input_grads,
        features[4],
        features[5],
        features[0],
        features[1],
        query_grad,
        qkv_bias[:, 0].reshape(-1),
        key_grad,
        value_grad,
        qkv_bias[:, 2].reshape(-1),
        out_grad,
        features[2],
        rise_grad,
        totals[:, :hidden].reshape(-1),
        fall_grad,
        features[3],
    )


def solution(mesh):
    placed = (
        P("dp", "ctx", None),
        P("dp", "ctx", None),
        P(("dp", "ctx")),
        P(("dp", "ctx")),
        P(("dp", "ctx")),
        P(("dp", "ctx")),
        P(("dp", "ctx"), "tp"),
        P("tp"),
        P(("dp", "ctx"), "tp"),
        P(("dp", "ctx"), "tp"),
        P("tp"),
        P("tp", ("dp", "ctx")),
        P(("dp", "ctx")),
        P(("dp", "ctx"), "tp"),
        P("tp"),
        P("tp", ("dp", "ctx")),
        P(("dp", "ctx")),
    )
    return jax.shard_map(
        body,
        mesh=mesh,
        in_specs=placed,
        out_specs=(
            P("dp", "ctx", None),
            P("dp", "ctx", None),
            P(("dp", "ctx")),
            P(("dp", "ctx")),
            P(("dp", "ctx")),
            P(("dp", "ctx")),
            P(("dp", "ctx"), "tp"),
            P("tp"),
            P(("dp", "ctx"), "tp"),
            P(("dp", "ctx"), "tp"),
            P("tp"),
            P("tp", ("dp", "ctx")),
            P(("dp", "ctx")),
            P(("dp", "ctx"), "tp"),
            P("tp"),
            P("tp", ("dp", "ctx")),
            P(("dp", "ctx")),
        ),
        check_vma=False,
    )
```

```python
import functools

import jax
import jax.numpy as jnp
from jax import lax
from jax.experimental import pallas as pl
from jax.experimental.pallas import tpu as pltpu
from jax.sharding import PartitionSpec as P

HEAD_DIM = 128
EPSILON = 1e-05
NEGATIVE = -1e30
F32 = jnp.float32
BF16 = jnp.bfloat16
MESH = pl.DeviceIdType.MESH


def product(former, latter):
    return jnp.dot(former, latter, preferred_element_type=F32)


def inner(former, latter):
    return lax.dot_general(former, latter, (((0,), (0,)), ((), ())), preferred_element_type=F32)


def across(former, latter):
    return lax.dot_general(former, latter, (((1,), (1,)), ((), ())), preferred_element_type=F32)


def normalize(values):
    average = jnp.mean(values, axis=-1, keepdims=True)
    centred = values - average
    spread = lax.rsqrt(jnp.mean(centred * centred, axis=-1, keepdims=True) + EPSILON)
    return (centred * spread, spread)


def norm_back(gradient, normed, spread):
    first_mean = jnp.mean(gradient, axis=-1, keepdims=True)
    second_mean = jnp.mean(gradient * normed, axis=-1, keepdims=True)
    return spread * (gradient - first_mean - normed * second_mean)


def swap(value, axis, mask):
    size = lax.axis_size(axis)
    return lax.ppermute(value, axis, [(i, i ^ mask) for i in range(size)])


def over_dp(both):
    return lax.psum_scatter(both, "dp", scatter_dimension=0, tiled=True)


def rows_of(here, block, size):
    return pl.multiple_of(lax.bitwise_xor(here, block) * size, size)


class Links:
    def __init__(self, count, half):
        self.count, self.half = count, half
        self.bits = (count - 1).bit_length()
        self.pairs = [(i, part) for i in range(1, count) for part in (0, 1)]
        self.slot = {pair: n for n, pair in enumerate(self.pairs)}

    def block(self, i, part):
        if part == 0:
            return i
        return sum(((i >> b) & 1) << (self.bits - 1 - b) for b in range(self.bits))

    def top(self, i):
        return 1 << (i.bit_length() - 1)

    def near(self, i):
        return i ^ self.top(i)

    def given(self, i):
        return [j for j in range(self.count - 1, 0, -1) if self.near(j) == i]

    def far(self, i, part):
        mask = self.block(self.top(i), part)
        return {"ctx": lax.bitwise_xor(lax.axis_index("ctx"), mask)}

    def start_row(self, i, part):
        return (2 * self.block(i, part) + part) * self.half

    def rows(self, ref, i, part):
        return ref.at[pl.ds(self.start_row(i, part), self.half)]

    def greet(self, others=(), masks=None):
        barrier = pltpu.get_barrier_semaphore()
        masks = [1 << bit for bit in range(self.bits)] if masks is None else masks
        partners = [{"ctx": lax.bitwise_xor(lax.axis_index("ctx"), mask)} for mask in masks]
        partners += list(others)
        for partner in partners:
            pl.semaphore_signal(barrier, 1, device_id=partner, device_id_type=MESH)
        pl.semaphore_wait(barrier, len(partners))

    def sharing(self, own_ref, full_ref, send_sem, recv_sem):
        copies = {}
        for i, part in self.pairs:
            near = self.near(i)
            source = (
                own_ref.at[pl.ds(part * self.half, self.half)]
                if near == 0
                else self.rows(full_ref, near, part)
            )
            n = self.slot[(i, part)]
            copies[(i, part)] = pltpu.make_async_remote_copy(
                src_ref=source,
                dst_ref=self.rows(full_ref, i, part),
                send_sem=send_sem.at[n],
                recv_sem=recv_sem.at[n],
                device_id=self.far(i, part),
                device_id_type=MESH,
            )
        return copies

    def summing(self, send_ref, recv_ref, send_sem, recv_sem):
        copies = {}
        for i, part in self.pairs:
            n = self.slot[(i, part)]
            copies[(i, part)] = pltpu.make_async_remote_copy(
                src_ref=send_ref.at[n],
                dst_ref=recv_ref.at[n],
                send_sem=send_sem.at[n],
                recv_sem=recv_sem.at[n],
                device_id=self.far(i, part),
                device_id_type=MESH,
            )
        return copies

    def pass_on(self, copies, arrived, own=False):
        for i, part in self.pairs:
            if self.near(i) == arrived:
                copies[(i, part)].start()

    def loads(self, ref, buffer, i, sem, base):
        return [
            pltpu.make_async_copy(
                self.rows(ref, i, part),
                buffer.at[pl.ds(part * self.half, self.half)],
                sem.at[base + part],
            )
            for part in (0, 1)
        ]

    def terms(self, i, columns, width, kept_v, send_v):
        tile = min(512, width)

        def step(n, _):
            at = pl.ds(pl.multiple_of(n * tile, tile), tile)
            term = columns(at)
            for part in (0, 1):
                piece = term[part * self.half : (part + 1) * self.half]
                if i < self.count // 2:
                    kept_v[2 * i + part, :, at] = piece
                else:
                    send_v[self.slot[(i, part)], :, at] = piece.astype(BF16)
            return 0

        lax.fori_loop(0, width // tile, step, 0)

    def combine(self, copies, kept_ref, send_ref, recv_ref, first, last, final=None, then=None):
        for i in range(first, last - 1, -1):
            for part in (0, 1):
                for j in self.given(i):
                    copies[(j, part)].wait_recv()
                chunk = min(32, self.half)

                def add(step, _, i=i, part=part):
                    at = pl.ds(pl.multiple_of(step * chunk, chunk), chunk)
                    value = kept_ref[2 * i + part, at, :]
                    for j in self.given(i):
                        value = value + recv_ref[self.slot[(j, part)], at, :].astype(F32)
                    if i == 0:
                        to = pl.ds(pl.multiple_of(part * self.half + step * chunk, chunk), chunk)
                        final(part, at, to, value)
                    else:
                        send_ref[self.slot[(i, part)], at, :] = value.astype(BF16)
                    return 0

                lax.fori_loop(0, self.half // chunk, add, 0)
                if i:
                    copies[(i, part)].start()
                elif then:
                    then(part)


def weight_grads(partner, rows_v, columns_v, theirs_v, came_v, results, send_sem, recv_sem, store_sem):
    tile = 512
    width = rows_v.shape[1]
    own = columns_v.shape[1] // 2

    def place(m):
        return pl.ds(pl.multiple_of(m * tile, tile), tile)

    def swap_tile(m):
        return pltpu.make_async_remote_copy(
            src_ref=theirs_v.at[place(m)],
            dst_ref=came_v.at[place(m)],
            send_sem=send_sem.at[m],
            recv_sem=recv_sem.at[m],
            device_id=partner,
            device_id_type=MESH,
        )

    def store_tile(m):
        copies, column = [], 0
        for n, result in enumerate(results):
            count = result.shape[1]
            copies.append(
                pltpu.make_async_copy(
                    came_v.at[place(m), pl.ds(column, count)], result.at[place(m)], store_sem[n].at[m]
                )
            )
            column += count
        return copies

    def first(m, _):
        term = inner(rows_v[:, place(m)], columns_v[:, own : 2 * own])
        theirs_v[place(m), :] = term.astype(BF16)
        swap_tile(m).start()
        return 0

    def second(m, _):
        swap_tile(m).wait_recv()
        term = inner(rows_v[:, place(m)], columns_v[:, 0:own])
        came_v[place(m), :] = (term + came_v[place(m), :].astype(F32)).astype(BF16)
        for copy in store_tile(m):
            copy.start()
        return 0

    def end(m, _):
        for copy in store_tile(m):
            copy.wait()
        swap_tile(m).wait_send()
        return 0

    lax.fori_loop(0, width // tile, first, 0)
    lax.fori_loop(0, width // tile, second, 0)
    return lambda: lax.fori_loop(0, width // tile, end, 0)


def feed_forward_kernel(
    links,
    own_ref,
    grads_ref,
    both_ref,
    shift_ref,
    residual_ref,
    table_ref,
    full_ref,
    hid_ref,
    slope_ref,
    both_grad_ref,
    late_grad_ref,
    back_ref,
    branch_ref,
    vector_ref,
    bias_ref,
    fall_ref,
    rise_big,
    fall_big,
    rows_v,
    grads_v,
    hid_v,
    slope_v,
    kept_v,
    send_v,
    recv_v,
    theirs_v,
    came_v,
    load_sem,
    store_sem,
    pair_send,
    pair_recv,
    grad_send,
    grad_recv,
    grad_store,
    share_send,
    share_recv,
    sum_send,
    sum_recv,
):
    half, count = links.half, links.count
    width, hidden = own_ref.shape[1], hid_v.shape[1]
    length = 2 * half * count
    rise_v = rise_big.at[pl.ds(0, width), pl.ds(0, hidden)]
    fall_v = fall_big.at[pl.ds(0, width), pl.ds(0, hidden)]
    own_half = pl.ds(0, hidden // 2)
    other_half = pl.ds(hidden // 2, hidden // 2)
    partner = {"tp": 1 - lax.axis_index("tp")}
    links.greet([partner])
    swaps = [
        pltpu.make_async_remote_copy(
            src_ref=both_ref.at[:, pl.ds(n * (hidden // 2), hidden // 2)],
            dst_ref=target.at[:, other_half],
            send_sem=pair_send.at[n],
            recv_sem=pair_recv.at[n],
            device_id=partner,
            device_id_type=MESH,
        )
        for n, target in enumerate((fall_v, rise_v))
    ]
    for copy in swaps:
        copy.start()
    shares = links.sharing(own_ref, full_ref, share_send, share_recv)
    sums = links.summing(send_v, recv_v, sum_send, sum_recv)
    links.pass_on(shares, 0)
    keep = pltpu.make_async_copy(rows_v, full_ref.at[pl.ds(0, 2 * half)], load_sem.at[0])
    first = pltpu.make_async_copy(own_ref, rows_v, load_sem.at[1])
    first.start()
    rise = pltpu.make_async_copy(both_ref.at[:, other_half], rise_v.at[:, own_half], load_sem.at[2])
    rise.start()
    fall = pltpu.make_async_copy(both_ref.at[:, own_half], fall_v.at[:, own_half], load_sem.at[3])
    fall.start()
    bias_ref[...] = jnp.zeros_like(bias_ref)

    grad_loads = links.loads(grads_ref, grads_v, 0, load_sem, 4)
    for copy in grad_loads:
        copy.start()
    stores = []
    tile = min(512, hidden)
    for i in range(count):
        if i == 0:
            first.wait()
            keep.start()
            rise.wait()
            fall.wait()
            for copy in swaps:
                copy.wait_recv()
            keep_fall = pltpu.make_async_copy(fall_v, fall_ref, store_sem.at[4])
            keep_fall.start()
        else:
            for part in (0, 1):
                shares[(i, part)].wait_recv()
            links.pass_on(shares, i)
            if i == 1:
                keep.wait()
            row_loads = links.loads(full_ref, rows_v, i, load_sem, 8)
            for copy in row_loads:
                copy.start()
            for copy in row_loads:
                copy.wait()
        for copy in grad_loads + stores:
            copy.wait()

        def rise_step(step, _, i=i):
            at = pl.ds(pl.multiple_of(step * tile, tile), tile)
            pre = product(rows_v[...], rise_v[:, at]) + shift_ref[0:1, at]
            back = product(grads_v[...], fall_v[:, at])
            cumulative = 0.5 * (1.0 + lax.erf(pre * 0.7071067811865476))
            density = jnp.exp(-0.5 * pre * pre) * 0.3989422804014327
            hid_v[:, at] = (pre * cumulative).astype(BF16)
            slope = (back * (cumulative + pre * density)).astype(BF16)
            slope_v[:, at] = slope
            bias_ref[0:1, at] += jnp.sum(slope.astype(F32), axis=0, keepdims=True)
            return 0

        lax.fori_loop(0, hidden // tile, rise_step, 0)
        if i + 1 < count:
            grad_loads = links.loads(grads_ref, grads_v, i + 1, load_sem, 4)
            for copy in grad_loads:
                copy.start()
        stores = []
        for n, (buffer, ref) in enumerate(((hid_v, hid_ref), (slope_v, slope_ref))):
            for part in (0, 1):
                copy = pltpu.make_async_copy(
                    buffer.at[pl.ds(part * half, half)],
                    links.rows(ref, i, part),
                    store_sem.at[2 * n + part],
                )
                copy.start()
                stores.append(copy)

        links.terms(i, lambda at: across(slope_v[...], rise_v[at, :]), width, kept_v, send_v)
        if i >= count // 2:
            for part in (0, 1):
                sums[(i, part)].start()
    for copy in stores:
        copy.wait()
    keep_fall.wait()
    rows_big = rise_big.at[pl.ds(0, length), pl.ds(0, width)]
    columns_big = fall_big.at[pl.ds(0, length), pl.ds(0, hidden)]
    ends = []
    quarter = hidden // 4
    results = (
        (both_grad_ref.at[:, own_half],),
        (both_grad_ref.at[:, pl.ds(hidden // 2, quarter)], late_grad_ref),
    )
    stores = ((grad_store.at[0],), (grad_store.at[1], grad_store.at[2]))
    for n, (left, right) in enumerate(((full_ref, slope_ref), (grads_ref, hid_ref))):
        lefts = pltpu.make_async_copy(left, rows_big, load_sem.at[0])
        rights = pltpu.make_async_copy(right, columns_big, load_sem.at[1])
        lefts.start()
        rights.start()
        for end in ends:
            end()
        lefts.wait()
        rights.wait()
        ends = [
            weight_grads(
                partner,
                rows_big,
                columns_big,
                theirs_v,
                came_v.at[n],
                results[n],
                grad_send.at[n],
                grad_recv.at[n],
                stores[n],
            )
        ]
        if n == 0:
            links.combine(sums, kept_v, send_v, recv_v, count // 2 - 1, 1)
            finals = [
                pltpu.make_async_copy(
                    residual_ref.at[pl.ds(part * half, half)], kept_v.at[2 + part], load_sem.at[2 + part]
                )
                for part in (0, 1)
            ]
            finals.append(
                pltpu.make_async_copy(grads_ref.at[pl.ds(0, 2 * half)], rows_v, load_sem.at[4])
            )
            for copy in finals:
                copy.start()
    for copy in finals:
        copy.wait()
    vector_ref[...] = jnp.zeros_like(vector_ref)
    results = []

    def last(part, at, to, second):
        normed, spread = normalize(kept_v[2 + part, at, :])
        incoming = rows_v[to, :].astype(F32)
        back = incoming + norm_back(second * table_ref[2:3, :], normed, spread)
        branch = back.astype(BF16)
        kept_v[part, at, :] = back
        rows_v[to, :] = branch
        for n, value in enumerate((second * normed, second, branch.astype(F32), incoming)):
            vector_ref[n : n + 1, :] += jnp.sum(value, axis=0, keepdims=True)

    def store_part(part):
        rows = pl.ds(part * half, half)
        for n, (source, target) in enumerate(
            ((kept_v.at[part], back_ref.at[rows]), (rows_v.at[rows], branch_ref.at[rows]))
        ):
            copy = pltpu.make_async_copy(source, target, load_sem.at[2 * part + n])
            copy.start()
            results.append(copy)

    links.combine(sums, kept_v, send_v, recv_v, 0, 0, last, store_part)
    for end in ends:
        end()
    for copy in results:
        copy.wait()
    for copy in swaps:
        copy.wait_send()
    for pair in links.pairs:
        shares[pair].wait_send()
        sums[pair].wait_send()


def feed_forward(own, grads, both_weights, shift, residual, table, count):
    rows, width = own.shape
    hidden = both_weights.shape[1]
    length = rows * count
    links = Links(count, rows // 2)
    half, copies = links.half, len(links.pairs)
    anywhere = pl.BlockSpec(memory_space=pl.ANY)
    inside = pl.BlockSpec(memory_space=pltpu.VMEM)
    dma = pltpu.SemaphoreType.DMA
    return pl.pallas_call(
        functools.partial(feed_forward_kernel, links),
        out_shape=(
            jax.ShapeDtypeStruct((length, width), BF16),
            jax.ShapeDtypeStruct((length, hidden), BF16),
            jax.ShapeDtypeStruct((length, hidden), BF16),
            jax.ShapeDtypeStruct((width, hidden * 3 // 4), BF16),
            jax.ShapeDtypeStruct((width, hidden // 4), BF16),
            jax.ShapeDtypeStruct((rows, width), F32),
            jax.ShapeDtypeStruct((rows, width), BF16),
            jax.ShapeDtypeStruct((8, width), F32),
            jax.ShapeDtypeStruct((1, hidden), F32),
            jax.ShapeDtypeStruct((width, hidden), BF16),
        ),
        in_specs=[anywhere, anywhere, anywhere, inside, anywhere, inside],
        out_specs=(anywhere,) * 7 + (inside, inside, anywhere),
        scratch_shapes=[
            pltpu.VMEM((max(width, length), max(width, hidden)), BF16),
            pltpu.VMEM((max(width, length), hidden), BF16),
            pltpu.VMEM((rows, width), BF16),
            pltpu.VMEM((rows, width), BF16),
            pltpu.VMEM((rows, hidden), BF16),
            pltpu.VMEM((rows, hidden), BF16),
            pltpu.VMEM((count, half, width), F32),
            pltpu.VMEM((copies, half, width), BF16),
            pltpu.VMEM((copies, half, width), BF16),
            pltpu.VMEM((width, hidden // 2), BF16),
            pltpu.VMEM((2, width, hidden // 2), BF16),
            dma((10,)),
            dma((5,)),
            dma((2,)),
            dma((2,)),
            dma((3, width // 512)),
            dma((3, width // 512)),
            dma((3, width // 512)),
            dma((copies,)),
            dma((copies,)),
            dma((copies,)),
            dma((copies,)),
        ],
        compiler_params=pltpu.CompilerParams(
            collective_id=3, has_side_effects=True, vmem_limit_bytes=63 * 1024 * 1024
        ),
        cost_estimate=pl.CostEstimate(
            flops=10 * length * width * hidden,
            bytes_accessed=length * width * 8 + width * hidden * 4 + length * hidden * 4,
            transcendentals=length * hidden * 2,
        ),
        name="feed_forward",
    )(own, grads, both_weights, shift, residual, table)


def greet_all(partners):
    barrier = pltpu.get_barrier_semaphore()
    for partner in partners:
        pl.semaphore_signal(barrier, 1, device_id=partner, device_id_type=MESH)
    pl.semaphore_wait(barrier, len(partners))


def others(axis, count):
    return [{axis: lax.bitwise_xor(lax.axis_index(axis), mask)} for mask in range(1, count)]


def axis_bits(axis, size):
    return [
        {axis: lax.bitwise_xor(lax.axis_index(axis), 1 << bit)}
        for bit in range((size - 1).bit_length())
    ]


def piece_copies(count, source, target_ref, send_sem, recv_sem):
    here = lax.axis_index("ctx")
    return [
        pltpu.make_async_remote_copy(
            src_ref=source(lax.bitwise_xor(here, mask)),
            dst_ref=target_ref.at[here],
            send_sem=send_sem.at[mask - 1],
            recv_sem=recv_sem.at[mask - 1],
            device_id={"ctx": lax.bitwise_xor(here, mask)},
            device_id_type=MESH,
        )
        for mask in range(1, count)
    ]


class Line:
    def __init__(self, whole_ref, depth, send_sem, recv_sem):
        self.whole, self.depth = whole_ref, depth
        self.send_sem, self.recv_sem = send_sem, recv_sem
        self.me = lax.axis_index("dp")

    def copy(self, way, step, block):
        block = jnp.clip(block, 0, self.depth - 1)
        target = jnp.clip(self.me + way, 0, self.depth - 1)
        n = 0 if way > 0 else 1
        return pltpu.make_async_remote_copy(
            src_ref=self.whole.at[block],
            dst_ref=self.whole.at[block],
            send_sem=self.send_sem.at[n, step - 1],
            recv_sem=self.recv_sem.at[n, step - 1],
            device_id={"dp": target},
            device_id_type=MESH,
        )

    def sends(self, step, act):
        me, depth = self.me, self.depth

        @pl.when((me + 1 < depth) & (me - step + 1 >= 0))
        def _():
            act(self.copy(1, step, me - step + 1))

        @pl.when((me >= 1) & (me + step - 1 < depth))
        def _():
            act(self.copy(-1, step, me + step - 1))

    def start(self, step):
        self.sends(step, lambda copy: copy.start())

    def arrive(self, step):
        @pl.when(self.me - step >= 0)
        def _():
            self.copy(1, step, self.me - step).wait_recv()

        @pl.when(self.me + step < self.depth)
        def _():
            self.copy(-1, step, self.me + step).wait_recv()

    def finish(self):
        for step in range(1, self.depth):
            self.sends(step, lambda copy: copy.wait_send())


def front_kernel(
    links,
    depth,
    tokens_ref,
    head_pieces_ref,
    pieces_ref,
    small_ref,
    normed_ref,
    head_ref,
    block_ref,
    table_ref,
    rows_v,
    normed_v,
    head_v,
    piece_v,
    shards_v,
    load_sem,
    store_sem,
    share_send,
    share_recv,
    head_send,
    head_recv,
    piece_send,
    piece_recv,
    line_send,
    line_recv,
    shard_send,
    shard_recv,
):
    count, half = links.count, links.half
    size = 2 * half
    here, layer = lax.axis_index("ctx"), lax.axis_index("dp")
    shard = here * depth + layer
    thin = small_ref.shape[1]
    own_ref = tokens_ref.at[lax.axis_index("tp")]
    greet_all(others("ctx", count) + others("dp", depth))
    heads = piece_copies(
        count, lambda i: head_pieces_ref.at[i], head_ref.at[layer], head_send, head_recv
    )
    pieces = piece_copies(
        count, lambda i: pieces_ref.at[i], block_ref, piece_send, piece_recv
    )
    for copy in heads:
        copy.start()
    own_pieces = [
        pltpu.make_async_copy(head_pieces_ref.at[here], head_v, load_sem.at[2]),
        pltpu.make_async_copy(pieces_ref.at[here], piece_v, load_sem.at[0]),
    ]
    for copy in own_pieces:
        copy.start()
    first = pltpu.make_async_copy(own_ref, rows_v.at[pl.ds(0, size)], load_sem.at[1])
    first.start()
    shards_v[shard] = small_ref[...]
    for bit, device in enumerate(axis_bits("dp", depth) + axis_bits("ctx", count)):
        reach = 1 << bit
        mine = pl.ds(shard // reach * reach, reach)
        theirs = pl.ds((shard // reach ^ 1) * reach, reach)
        copies = [
            pltpu.make_async_remote_copy(
                src_ref=shards_v.at[mine],
                dst_ref=shards_v.at[place],
                send_sem=shard_send.at[bit],
                recv_sem=shard_recv.at[bit],
                device_id=device,
                device_id_type=MESH,
            )
            for place in (mine, theirs)
        ]
        copies[0].start()
        copies[0].wait_send()
        copies[1].wait_recv()
    shares = links.sharing(own_ref, rows_v, share_send, share_recv)
    links.pass_on(shares, 0)
    line = Line(head_ref, depth, line_send, line_recv)
    own_stores = [
        pltpu.make_async_copy(head_v, head_ref.at[layer, here], load_sem.at[2]),
        pltpu.make_async_copy(piece_v, block_ref.at[here], load_sem.at[0]),
    ]
    for load, store in zip(own_pieces, own_stores):
        load.wait()
        store.start()
    for copy in heads:
        copy.wait()
    own_stores[0].wait()
    line.start(1)
    for copy in pieces:
        copy.start()
    for c in range(count):
        for d in range(depth):
            n = d * count + c
            table_ref[:, n * thin : (n + 1) * thin] = shards_v[c * depth + d]
    chunk = min(32, half)
    stores = []
    for i in range(max(count, depth)):
        if 0 < i < depth:
            line.arrive(i)
            if i + 1 < depth:
                line.start(i + 1)
        if i >= count:
            continue
        if i == 0:
            first.wait()
        else:
            for part in (0, 1):
                shares[(i, part)].wait_recv()
            links.pass_on(shares, i)
        for part in (0, 1):
            base = links.start_row(i, part)

            def norm(step, _, base=base):
                at = pl.ds(pl.multiple_of(base + step * chunk, chunk), chunk)
                normed = normalize(rows_v[at, :].astype(F32))[0]
                normed_v[at, :] = (normed * table_ref[0:1, :] + table_ref[1:2, :]).astype(BF16)
                return 0

            lax.fori_loop(0, half // chunk, norm, 0)
            store = pltpu.make_async_copy(
                links.rows(normed_v, i, part), links.rows(normed_ref, i, part), store_sem.at[2 * i + part]
            )
            store.start()
            stores.append(store)
    for copy in stores + pieces + own_stores[1:]:
        copy.wait()
    line.finish()
    for pair in links.pairs:
        shares[pair].wait_send()


def front(tokens, head_pieces, pieces, small, count, depth):
    _, rows, width = tokens.shape
    length = rows * count
    links = Links(count, rows // 2)
    copies = len(links.pairs)
    bits = (count - 1).bit_length() + (depth - 1).bit_length()
    anywhere = pl.BlockSpec(memory_space=pl.ANY)
    inside = pl.BlockSpec(memory_space=pltpu.VMEM)
    dma = pltpu.SemaphoreType.DMA
    return pl.pallas_call(
        functools.partial(front_kernel, links, depth),
        out_shape=(
            jax.ShapeDtypeStruct((length, width), BF16),
            jax.ShapeDtypeStruct((depth, *head_pieces.shape), BF16),
            jax.ShapeDtypeStruct(pieces.shape, BF16),
            jax.ShapeDtypeStruct((8, width), F32),
        ),
        in_specs=[anywhere, anywhere, anywhere, inside],
        out_specs=(anywhere, anywhere, anywhere, inside),
        scratch_shapes=[
            pltpu.VMEM((length, width), BF16),
            pltpu.VMEM((length, width), BF16),
            pltpu.VMEM(head_pieces.shape[1:], BF16),
            pltpu.VMEM(pieces.shape[1:], BF16),
            pltpu.VMEM((count * depth, *small.shape), F32),
            dma((3,)),
            dma((2 * count,)),
            dma((copies,)),
            dma((copies,)),
            dma((count - 1,)),
            dma((count - 1,)),
            dma((count - 1,)),
            dma((count - 1,)),
            dma((2, depth - 1)),
            dma((2, depth - 1)),
            dma((bits,)),
            dma((bits,)),
        ],
        compiler_params=pltpu.CompilerParams(
            collective_id=1, has_side_effects=True, vmem_limit_bytes=40 * 1024 * 1024
        ),
        cost_estimate=pl.CostEstimate(
            flops=20 * length * width, bytes_accessed=120000000, transcendentals=0
        ),
        name="front",
    )(tokens, head_pieces, pieces, small)


def end_kernel(
    count,
    depth,
    heads,
    rows_ref,
    vectors_ref,
    firsts_ref,
    biases_ref,
    query_ref,
    key_ref,
    value_ref,
    out_ref,
    fall_ref,
    features_ref,
    totals_ref,
    block_v,
    shards_v,
    pair_v,
    landing_v,
    bias_v,
    load_sem,
    piece_send,
    piece_recv,
    shard_send,
    shard_recv,
    bias_send,
    bias_recv,
    total_send,
    total_recv,
):
    here, layer = lax.axis_index("ctx"), lax.axis_index("dp")
    shard = layer * count + here
    partner = {"tp": 1 - lax.axis_index("tp")}
    thin = query_ref.shape[0]
    wide = heads * 3 * HEAD_DIM
    low, high = (count - 1).bit_length(), (depth - 1).bit_length()
    greet_all([partner] + others("ctx", count) + others("dp", depth))
    pieces = piece_copies(
        count,
        lambda i: rows_ref.at[pl.ds(pl.multiple_of(i * thin, thin), thin)],
        block_v,
        piece_send,
        piece_recv,
    )
    pieces.append(
        pltpu.make_async_copy(
            rows_ref.at[pl.ds(pl.multiple_of(here * thin, thin), thin)], block_v.at[here], load_sem.at[0]
        )
    )
    for copy in pieces:
        copy.start()
    for n in range(count * depth):
        at = slice(n * thin, (n + 1) * thin)
        shards_v[n, 0:4, :] = vectors_ref[0:4, at]
        shards_v[n, 4:8, :] = firsts_ref[0:4, at]

    def exchange(source, target, device, send, recv):
        copy = pltpu.make_async_remote_copy(
            src_ref=source,
            dst_ref=target,
            send_sem=send,
            recv_sem=recv,
            device_id=device,
            device_id_type=MESH,
        )
        copy.start()
        return copy

    bias_v[0] = biases_ref[0]
    bias_v[1] = biases_ref[1]
    stage = [
        exchange(shards_v, pair_v, partner, shard_send.at[low + high], shard_recv.at[low + high]),
        exchange(bias_v.at[1], bias_v.at[2], partner, bias_send.at[high], bias_recv.at[high]),
    ]
    for copy in stage:
        copy.wait()
    shards_v[...] += pair_v[...]
    bias_v[0] += bias_v[2]
    totals = []
    devices = axis_bits("ctx", count) + axis_bits("dp", depth)
    for bit in range(low + high - 1, -1, -1):
        reach = 1 << bit
        mine = shard // reach * reach
        theirs = (shard // reach ^ 1) * reach
        stage = [
            exchange(
                shards_v.at[pl.ds(theirs, reach)],
                landing_v.at[pl.ds(reach, reach)],
                devices[bit],
                shard_send.at[bit],
                shard_recv.at[bit],
            )
        ]
        if bit >= low:
            n = bit - low
            stage.append(
                exchange(bias_v.at[0], bias_v.at[3 + n], devices[bit], bias_send.at[n], bias_recv.at[n])
            )
        for copy in stage:
            copy.wait()
        shards_v[pl.ds(mine, reach)] += landing_v[reach : 2 * reach]
        if bit >= low:
            bias_v[0] += bias_v[3 + bit - low]
        if bit == low:
            totals_ref[here] = bias_v[0]
            totals = [
                exchange(
                    bias_v.at[0], totals_ref.at[here], device, total_send.at[n], total_recv.at[n]
                )
                for n, device in enumerate(others("ctx", count))
            ]
    features_ref[...] = shards_v[shard]
    for copy in pieces + totals:
        copy.wait()
    for c in range(count):
        for j in range(heads):
            to = slice((c * heads + j) * HEAD_DIM, (c * heads + j + 1) * HEAD_DIM)
            for n, ref in enumerate((query_ref, key_ref, value_ref)):
                column = (3 * j + n) * HEAD_DIM
                ref[:, to] = block_v[c, :, column : column + HEAD_DIM].astype(F32)
        rows = slice(c * heads * HEAD_DIM, (c + 1) * heads * HEAD_DIM)
        out_ref[rows, :] = block_v[c, :, wide : wide + heads * HEAD_DIM].astype(F32).T
        fall_ref[c] = block_v[c, :, wide + heads * HEAD_DIM :].astype(F32).T


def end(rows, vectors, firsts, biases, heads, count, depth):
    low, high = (count - 1).bit_length(), (depth - 1).bit_length()
    thin = rows.shape[0] // count
    columns = rows.shape[1]
    local = count * heads * HEAD_DIM
    inside = pl.BlockSpec(memory_space=pltpu.VMEM)
    dma = pltpu.SemaphoreType.DMA
    shards = (count * depth, 8, thin)
    return pl.pallas_call(
        functools.partial(end_kernel, count, depth, heads),
        out_shape=(
            jax.ShapeDtypeStruct((thin, local), F32),
            jax.ShapeDtypeStruct((thin, local), F32),
            jax.ShapeDtypeStruct((thin, local), F32),
            jax.ShapeDtypeStruct((local, thin), F32),
            jax.ShapeDtypeStruct((count, columns - heads * 4 * HEAD_DIM, thin), F32),
            jax.ShapeDtypeStruct((8, thin), F32),
            jax.ShapeDtypeStruct((count, 1, biases.shape[2]), F32),
        ),
        in_specs=[pl.BlockSpec(memory_space=pl.ANY), inside, inside, inside],
        out_specs=(inside,) * 7,
        scratch_shapes=[
            pltpu.VMEM((count, thin, columns), BF16),
            pltpu.VMEM(shards, F32),
            pltpu.VMEM(shards, F32),
            pltpu.VMEM(shards, F32),
            pltpu.VMEM((3 + high, 1, biases.shape[2]), F32),
            dma((1,)),
            dma((count - 1,)),
            dma((count - 1,)),
            dma((low + high + 1,)),
            dma((low + high + 1,)),
            dma((high + 1,)),
            dma((high + 1,)),
            dma((count - 1,)),
            dma((count - 1,)),
        ],
        compiler_params=pltpu.CompilerParams(
            collective_id=7, has_side_effects=True, vmem_limit_bytes=24 * 1024 * 1024
        ),
        cost_estimate=pl.CostEstimate(flops=0, bytes_accessed=40000000, transcendentals=0),
        name="end",
    )(rows, vectors, firsts, biases)


def attend_kernel(
    links,
    heads,
    rows_ref,
    weight_ref,
    shift_ref,
    cotangent_ref,
    tokens_ref,
    table_ref,
    qkv_ref,
    mixed_ref,
    log_ref,
    grads_full_ref,
    residual_ref,
    second_ref,
    whole_ref,
    own_v,
    rows_v,
    weight_v,
    qkv_v,
    mixed_v,
    scores_v,
    kept_v,
    send_v,
    recv_v,
    load_sem,
    store_sem,
    pair_send,
    pair_recv,
    share_send,
    share_recv,
    sum_send,
    sum_recv,
):
    count, half = links.count, links.half
    size = 2 * half
    here = lax.axis_index("ctx")
    core = lax.axis_index("tp")
    partner = {"tp": 1 - core}
    grads_ref = cotangent_ref.at[core]
    narrow = weight_ref.shape[1]
    wide = heads * 3 * HEAD_DIM // 2
    links.greet([partner])
    theirs = pltpu.make_async_remote_copy(
        src_ref=weight_ref,
        dst_ref=weight_v.at[1],
        send_sem=pair_send.at[0],
        recv_sem=pair_recv.at[0],
        device_id=partner,
        device_id_type=MESH,
    )
    theirs.start()
    shares = links.sharing(grads_ref, grads_full_ref, share_send, share_recv)
    sums = links.summing(send_v, recv_v, sum_send, sum_recv)
    links.pass_on(shares, 0)
    ours = pltpu.make_async_copy(weight_ref, weight_v.at[0], load_sem.at[0])
    ours.start()
    own = pltpu.make_async_copy(tokens_ref.at[core], own_v, load_sem.at[4])
    own.start()

    def load(n):
        return pltpu.make_async_copy(
            rows_ref.at[pl.ds(n * size, size)], rows_v.at[n % 2], load_sem.at[2 + n % 2]
        )

    coming = load(0)
    coming.start()
    ours.wait()
    theirs.wait_recv()
    wholes = []
    for core in (0, 1):
        copy = pltpu.make_async_copy(weight_v.at[core], whole_ref.at[core], store_sem.at[core])
        copy.start()
        wholes.append(copy)
    tile = 256 if wide % 256 == 0 else HEAD_DIM
    for n in range(count):
        coming.wait()
        if n + 1 < count:
            coming = load(n + 1)
            coming.start()
        for core in (0, 1):

            def step(m, _, n=n, core=core):
                at = pl.ds(pl.multiple_of(m * tile, tile), tile)
                to = pl.ds(pl.multiple_of(core * wide + m * tile, tile), tile)
                value = product(rows_v[n % 2], weight_v[core, :, at]) + shift_ref[0:1, to]
                qkv_v[n * size : (n + 1) * size, to] = value.astype(BF16)
                return 0

            lax.fori_loop(0, wide // tile, step, 0)
    keep_qkv = pltpu.make_async_copy(qkv_v, qkv_ref, store_sem.at[2])
    keep_qkv.start()
    own_grads = pltpu.make_async_copy(grads_ref, rows_v.at[0], load_sem.at[1])
    own_grads.start()
    keep = pltpu.make_async_copy(rows_v.at[0], grads_full_ref.at[pl.ds(0, size)], load_sem.at[1])

    def one_head(head, _):
        @pl.when(head == heads // 2)
        def _():
            for i in range(1, (count + 1) // 2):
                for part in (0, 1):
                    shares[(i, part)].wait_recv()
                links.pass_on(shares, i)

        attend_forward_head(here, head, size, count, qkv_v, mixed_v, log_ref, scores_v)
        return 0

    lax.fori_loop(0, heads, one_head, 0)
    keep_mixed = pltpu.make_async_copy(mixed_v, mixed_ref, store_sem.at[3])
    keep_mixed.start()
    own_grads.wait()
    keep.start()
    chip = heads * HEAD_DIM // 2
    for i in range(count - 1, -1, -1):

        def out_rows(core, i=i):
            at = slice(core * chip, (core + 1) * chip)
            first = [links.start_row(i, part) for part in (0, 1)]
            return jnp.concatenate([mixed_v[row : row + half, at] for row in first], axis=0)

        links.terms(
            i,
            lambda at: across(out_rows(0), weight_v[0, at, wide:narrow])
            + across(out_rows(1), weight_v[1, at, wide:narrow]),
            residual_ref.shape[1],
            kept_v,
            send_v,
        )
        if i >= count // 2:
            for part in (0, 1):
                sums[(i, part)].start()

    def norm(part, at, to, value):
        residual = own_v[to, :].astype(F32) + (value + table_ref[4:5, :])
        residual_ref[to, :] = residual
        normed = normalize(residual)[0]
        second_ref[to, :] = (normed * table_ref[2:3, :] + table_ref[3:4, :]).astype(BF16)

    own.wait()
    links.combine(sums, kept_v, send_v, recv_v, count // 2 - 1, 0, norm)
    for i in range(1, count):
        for part in (0, 1):
            if i >= (count + 1) // 2:
                shares[(i, part)].wait_recv()
    for copy in wholes + [keep_qkv, keep_mixed, keep]:
        copy.wait()
    theirs.wait_send()
    for pair in links.pairs:
        sums[pair].wait_send()
        shares[pair].wait_send()


def attend_forward_head(here, head, size, blocks, qkv_v, mixed_v, log_ref, scores_v):
    scaling = HEAD_DIM ** (-0.5)
    behind = lax.broadcasted_iota(jnp.int32, (size, size), 1) <= lax.broadcasted_iota(
        jnp.int32, (size, size), 0
    )
    column = pl.multiple_of(head * (3 * HEAD_DIM), HEAD_DIM)
    query_at = pl.ds(column, HEAD_DIM)
    key_at = pl.ds(pl.multiple_of(column + HEAD_DIM, HEAD_DIM), HEAD_DIM)
    value_at = pl.ds(pl.multiple_of(column + 2 * HEAD_DIM, HEAD_DIM), HEAD_DIM)
    head_at = pl.ds(pl.multiple_of(head * HEAD_DIM, HEAD_DIM), HEAD_DIM)
    for i in range(blocks):
        at = pl.ds(rows_of(here, i, size), size)
        queries = qkv_v[at, query_at]
        highest = jnp.full((size, 1), NEGATIVE, F32)
        for j in range(i + 1):
            keys = qkv_v[pl.ds(rows_of(here, j, size), size), key_at]
            scores = across(queries, keys) * scaling
            if j == i:
                scores = jnp.where(behind, scores, NEGATIVE)
            scores_v[:, j * size : (j + 1) * size] = scores
            highest = jnp.maximum(highest, jnp.max(scores, axis=1, keepdims=True))
        row_total = jnp.zeros((size, 1), F32)
        mixed = jnp.zeros((size, HEAD_DIM), F32)
        for j in range(i + 1):
            exponent = jnp.exp(scores_v[:, j * size : (j + 1) * size] - highest)
            row_total = row_total + jnp.sum(exponent, axis=1, keepdims=True)
            values = qkv_v[pl.ds(rows_of(here, j, size), size), value_at]
            mixed = mixed + product(exponent.astype(BF16), values)
        mixed_v[at, head_at] = (mixed / row_total).astype(BF16)
        log_total = jnp.broadcast_to(highest + jnp.log(row_total), (size, HEAD_DIM))
        log_ref[head, :, at] = log_total.T[0:8, :]


def attend(rows, weight, shift, cotangent, tokens, table, heads, count):
    length, width = rows.shape
    size = length // count
    narrow = weight.shape[1]
    columns = heads * 3 * HEAD_DIM
    links = Links(count, size // 2)
    half, copies = links.half, len(links.pairs)
    pairs = heads * length * (length + size) // 2
    anywhere = pl.BlockSpec(memory_space=pl.ANY)
    inside = pl.BlockSpec(memory_space=pltpu.VMEM)
    dma = pltpu.SemaphoreType.DMA
    return pl.pallas_call(
        functools.partial(attend_kernel, links, heads),
        out_shape=(
            jax.ShapeDtypeStruct((length, columns), BF16),
            jax.ShapeDtypeStruct((length, heads * HEAD_DIM), BF16),
            jax.ShapeDtypeStruct((heads, 8, length), F32),
            jax.ShapeDtypeStruct((length, width), BF16),
            jax.ShapeDtypeStruct((size, width), F32),
            jax.ShapeDtypeStruct((size, width), BF16),
            jax.ShapeDtypeStruct((2, width, narrow), BF16),
        ),
        in_specs=[anywhere, anywhere, inside, anywhere, anywhere, inside],
        out_specs=(anywhere, anywhere, inside, anywhere, inside, inside, anywhere),
        scratch_shapes=[
            pltpu.VMEM((size, width), BF16),
            pltpu.VMEM((2, size, width), BF16),
            pltpu.VMEM((2, width, narrow), BF16),
            pltpu.VMEM((length, columns), BF16),
            pltpu.VMEM((length, heads * HEAD_DIM), BF16),
            pltpu.VMEM((size, length), F32),
            pltpu.VMEM((count, half, width), F32),
            pltpu.VMEM((copies, half, width), BF16),
            pltpu.VMEM((copies, half, width), BF16),
            dma((5,)),
            dma((4,)),
            dma((1,)),
            dma((1,)),
            dma((copies,)),
            dma((copies,)),
            dma((copies,)),
            dma((copies,)),
        ],
        compiler_params=pltpu.CompilerParams(
            collective_id=2, has_side_effects=True, vmem_limit_bytes=60 * 1024 * 1024
        ),
        cost_estimate=pl.CostEstimate(
            flops=pairs * HEAD_DIM * 8 + 2 * length * width * heads * HEAD_DIM * 4,
            bytes_accessed=length * width * 8,
            transcendentals=pairs,
        ),
        name="attend",
    )(rows, weight, shift, cotangent, tokens, table)


def attend_back_kernel(
    links,
    heads,
    own_ref,
    weight_ref,
    qkv_ref,
    mixed_ref,
    log_ref,
    hid_ref,
    fall_ref,
    first_ref,
    residual_ref,
    late_ref,
    table_ref,
    full_ref,
    result_ref,
    low_ref,
    late_grad_ref,
    residual_v,
    weight_v,
    qkv_v,
    mixed_v,
    big_v,
    shared_v,
    came_v,
    grad_v,
    rows_v,
    hid_v,
    key_v,
    value_v,
    kept_v,
    send_v,
    recv_v,
    load_sem,
    grad_send,
    grad_recv,
    grad_store,
    share_send,
    share_recv,
    sum_send,
    sum_recv,
):
    half, count = links.half, links.count
    size = 2 * half
    here = lax.axis_index("ctx")
    chip = weight_v.shape[2]
    wide = heads * 3 * HEAD_DIM // 2
    narrow = residual_v.shape[1]
    middle = hid_v.shape[2] // 2
    partner = {"tp": 1 - lax.axis_index("tp")}
    links.greet([partner])
    shares = links.sharing(own_ref, full_ref, share_send, share_recv)
    sums = links.summing(send_v, recv_v, sum_send, sum_recv)
    links.pass_on(shares, 0)
    falls = [shared_v.at[pl.ds(n * narrow, narrow), pl.ds(0, middle)] for n in (0, 1)]
    theirs_v = shared_v.at[pl.ds(0, big_v.shape[1])]
    late_v = shared_v.at[pl.ds(0, big_v.shape[1]), pl.ds(0, late_ref.shape[1])]
    loads = [
        pltpu.make_async_copy(source, target, load_sem.at[n])
        for n, (source, target) in enumerate(
            (
                (fall_ref.at[pl.ds(0, narrow), pl.ds(0, middle)], falls[0]),
                (fall_ref.at[pl.ds(0, narrow), pl.ds(middle, middle)], falls[1]),
                (own_ref, rows_v),
                (weight_ref.at[:, :, pl.ds(weight_ref.shape[2] - chip, chip)], weight_v),
                (qkv_ref, qkv_v),
                (mixed_ref, mixed_v),
                (rows_v, full_ref.at[pl.ds(0, size)]),
                (first_ref, big_v),
                (residual_ref.at[:, pl.ds(0, narrow)], residual_v),
                (late_ref, late_v),
                (late_v, late_grad_ref.at[:, pl.ds(wide + chip, late_ref.shape[1])]),
            )
        )
    ]
    for n in (0, 1, 2, 3, 4, 5, 7, 8):
        loads[n].start()
    key_v[...] = jnp.zeros_like(key_v)
    value_v[...] = jnp.zeros_like(value_v)
    for copy in loads[:2]:
        copy.wait()
    out_terms(
        links,
        hid_ref,
        hid_v,
        lambda rows, at: across(rows[:, 0:middle], falls[0][at, :])
        + across(rows[:, middle : 2 * middle], falls[1][at, :]),
        narrow,
        kept_v,
        send_v,
        load_sem,
        11,
    )
    loads[9].start()
    for copy in loads[2:6]:
        copy.wait()
    loads[6].start()
    loads[9].wait()
    loads[10].start()
    together = min(2, heads)
    for i in range(count):
        if i:
            for part in (0, 1):
                shares[(i, part)].wait_recv()
            links.pass_on(shares, i)
            if i == 1:
                loads[6].wait()
            unit_loads = links.loads(full_ref, rows_v, i, load_sem, 11)
            for copy in unit_loads:
                copy.start()
            for copy in unit_loads:
                copy.wait()
        if i + 1 == count:
            for j in range(count - 1, count // 2 - 1, -1):
                for part in (0, 1):
                    sums[(j, part)].start()
        for core in (0, 1):
            term = product(rows_v[...], weight_v[core]).astype(BF16)
            for part in (0, 1):
                row = links.start_row(i, part)
                grad_v[row : row + half, core * chip : (core + 1) * chip] = term[
                    part * half : (part + 1) * half
                ]
        blocks = [links.block(i, part) for part in (0, 1)]
        firsts = [links.start_row(i, part) for part in (0, 1)]

        def one(n, _, blocks=blocks, firsts=firsts):
            part, first_head = n // (heads // together), n % (heads // together) * together
            row = pl.multiple_of(firsts[0] + part * (firsts[1] - firsts[0]), half)
            block = lax.bitwise_xor(here, blocks[0] + part * (blocks[1] - blocks[0]))
            attend_backward_unit(
                here,
                [first_head + m for m in range(together)],
                block,
                part * half,
                row,
                half,
                qkv_v,
                grad_v,
                mixed_v,
                log_ref,
                result_ref,
                key_v,
                value_v,
            )
            return 0

        lax.fori_loop(0, 2 * heads // together, one, 0)

    def store_head(head, _):
        at = pl.ds(pl.multiple_of(head * HEAD_DIM, HEAD_DIM), HEAD_DIM)
        column = head * (3 * HEAD_DIM)
        key_at = pl.ds(pl.multiple_of(column + HEAD_DIM, HEAD_DIM), HEAD_DIM)
        value_at = pl.ds(pl.multiple_of(column + 2 * HEAD_DIM, HEAD_DIM), HEAD_DIM)
        result_ref[:, key_at] = (key_v[:, at] * HEAD_DIM ** (-0.5)).astype(BF16)
        result_ref[:, value_at] = value_v[:, at].astype(BF16)
        return 0

    links.combine(sums, kept_v, send_v, recv_v, count // 2 - 1, 1)
    lax.fori_loop(0, heads, store_head, 0)
    loads[10].wait()
    loads[7].wait()
    end_first = weight_grads(
        partner,
        big_v,
        result_ref,
        theirs_v.at[:, pl.ds(0, wide)],
        came_v.at[:, pl.ds(0, wide)],
        (late_grad_ref.at[:, pl.ds(0, wide)],),
        grad_send.at[0],
        grad_recv.at[0],
        (grad_store.at[0],),
    )
    again = pltpu.make_async_copy(full_ref, big_v, load_sem.at[7])
    again.start()
    again.wait()
    end_second = weight_grads(
        partner,
        big_v,
        mixed_v,
        theirs_v.at[:, pl.ds(wide, chip)],
        came_v.at[:, pl.ds(wide, chip)],
        (late_grad_ref.at[:, pl.ds(wide, chip)],),
        grad_send.at[1],
        grad_recv.at[1],
        (grad_store.at[1],),
    )
    loads[8].wait()

    def low(part, at, to, value):
        low_ref[to, :] = (residual_v[to, :] + (value + table_ref[5:6, 0:narrow])).astype(BF16)

    links.combine(sums, kept_v, send_v, recv_v, 0, 0, low)
    end_first()
    end_second()
    for pair in links.pairs:
        sums[pair].wait_send()
        shares[pair].wait_send()


def attend_backward_unit(
    here, heads, block, offset, row, half, qkv_v, grad_v, mixed_v, log_ref, result_ref, key_v, value_v
):
    size = 2 * half
    scaling = HEAD_DIM ** (-0.5)
    at = pl.ds(row, half)

    def columns(head, n):
        return pl.ds(pl.multiple_of(head * (3 * HEAD_DIM) + n * HEAD_DIM, HEAD_DIM), HEAD_DIM)

    places = [pl.ds(pl.multiple_of(head * HEAD_DIM, HEAD_DIM), HEAD_DIM) for head in heads]
    queries = [qkv_v[at, columns(head, 0)] for head in heads]
    grads = [grad_v[at, place] for place in places]
    centres = [
        jnp.sum((grad.astype(F32) * mixed_v[at, place].astype(F32)).T, axis=0, keepdims=True)
        for grad, place in zip(grads, places)
    ]
    logs = [log_ref[head, 0:1, at] for head in heads]

    def step(j, query_grads, last):
        there = pl.ds(rows_of(here, j, size), size)
        results = []
        for n, head in enumerate(heads):
            keys = qkv_v[there, columns(head, 1)]
            values = qkv_v[there, columns(head, 2)]
            weights = jnp.exp(across(keys, queries[n]) * scaling - logs[n])
            if last:
                behind = lax.broadcasted_iota(jnp.int32, (size, half), 0) <= offset + (
                    lax.broadcasted_iota(jnp.int32, (size, half), 1)
                )
                weights = jnp.where(behind, weights, 0.0)
            slopes = (weights * (across(values, grads[n]) - centres[n])).astype(BF16)
            value_v[there, places[n]] += product(weights.astype(BF16), grads[n])
            key_v[there, places[n]] += product(slopes, queries[n])
            results.append(query_grads[n] + inner(slopes, keys))
        return tuple(results)

    query_grads = lax.fori_loop(
        0,
        block,
        lambda j, found: step(j, found, False),
        tuple(jnp.zeros((half, HEAD_DIM), F32) for _ in heads),
    )
    query_grads = step(block, query_grads, True)
    for n, head in enumerate(heads):
        result_ref[at, columns(head, 0)] = (query_grads[n] * scaling).astype(BF16)


def out_terms(links, hid_ref, hid_v, columns, narrow, kept_v, send_v, load_sem, base):
    count, slots = links.count, hid_v.shape[0]
    order = list(range(count - 1, -1, -1))

    def load(n):
        slot = n % slots
        copies = links.loads(hid_ref, hid_v.at[slot], order[n], load_sem, base + 2 * slot)
        for copy in copies:
            copy.start()
        return copies

    coming = [load(n) for n in range(slots)]
    for n, i in enumerate(order):
        for copy in coming[n]:
            copy.wait()
        links.terms(i, lambda at, n=n: columns(hid_v.at[n % slots], at), narrow, kept_v, send_v)
        if n + slots < count:
            coming.append(load(n + slots))


def attend_back(
    own, weight, qkv, mixed, log_total, hid, fall_weight, first, residual, late, table, count
):
    rows, width = own.shape
    length, columns = qkv.shape
    heads = columns // (3 * HEAD_DIM)
    hidden = hid.shape[1]
    links = Links(count, rows // 2)
    half, copies = links.half, len(links.pairs)
    narrow = width // 2
    pairs = heads * length * (length + rows) // 2
    anywhere = pl.BlockSpec(memory_space=pl.ANY)
    inside = pl.BlockSpec(memory_space=pltpu.VMEM)
    dma = pltpu.SemaphoreType.DMA
    return pl.pallas_call(
        functools.partial(attend_back_kernel, links, heads),
        out_shape=(
            jax.ShapeDtypeStruct((length, width), BF16),
            jax.ShapeDtypeStruct((length, columns), BF16),
            jax.ShapeDtypeStruct((rows, narrow), BF16),
            jax.ShapeDtypeStruct((width, 2 * heads * HEAD_DIM + late.shape[1]), BF16),
        ),
        in_specs=[anywhere] * 4 + [inside] + [anywhere] * 5 + [inside],
        out_specs=(anywhere, inside, inside, anywhere),
        scratch_shapes=[
            pltpu.VMEM((rows, narrow), F32),
            pltpu.VMEM((2, width, heads * HEAD_DIM // 2), BF16),
            pltpu.VMEM(qkv.shape, BF16),
            pltpu.VMEM(mixed.shape, BF16),
            pltpu.VMEM((length, width), BF16),
            pltpu.VMEM((width, max(2 * heads * HEAD_DIM, hidden // 2)), BF16),
            pltpu.VMEM((width, 2 * heads * HEAD_DIM), BF16),
            pltpu.VMEM(mixed.shape, BF16),
            pltpu.VMEM((rows, width), BF16),
            pltpu.VMEM((1, rows, hidden), BF16),
            pltpu.VMEM(mixed.shape, F32),
            pltpu.VMEM(mixed.shape, F32),
            pltpu.VMEM((count, half, narrow), F32),
            pltpu.VMEM((copies, half, narrow), BF16),
            pltpu.VMEM((copies, half, narrow), BF16),
            dma((13,)),
            dma((3, width // 512)),
            dma((3, width // 512)),
            dma((3, width // 512)),
            dma((copies,)),
            dma((copies,)),
            dma((copies,)),
            dma((copies,)),
        ],
        compiler_params=pltpu.CompilerParams(
            collective_id=4, has_side_effects=True, vmem_limit_bytes=63 * 1024 * 1024
        ),
        cost_estimate=pl.CostEstimate(
            flops=pairs * HEAD_DIM * 20 + 2 * length * width * (heads * HEAD_DIM + hidden // 2),
            bytes_accessed=length * width * 6 + length * columns * 4 + length * hidden * 2,
            transcendentals=pairs,
        ),
        name="attend_back",
    )(own, weight, qkv, mixed, log_total, hid, fall_weight, first, residual, late, table)


def first_back_kernel(
    links,
    grads_ref,
    weight_ref,
    hid_ref,
    fall_ref,
    low_ref,
    residual_ref,
    back_ref,
    tokens_ref,
    table_ref,
    hidden_ref,
    out_ref,
    input_ref,
    vector_ref,
    bias_ref,
    fall_grad_ref,
    rise_grad_ref,
    grads_v,
    weight_v,
    hid_v,
    fall_v,
    kept_v,
    send_v,
    recv_v,
    kept_w,
    send_w,
    recv_w,
    residual_v,
    tokens_v,
    high_v,
    block_v,
    load_sem,
    pair_send,
    pair_recv,
    piece_send,
    piece_recv,
    sum_send,
    sum_recv,
    late_send,
    late_recv,
):
    count, half = links.count, links.half
    size = 2 * half
    wide = weight_v.shape[2]
    thin = hidden_ref.shape[0] // count
    hidden = hidden_ref.shape[1] * 2 // 3
    narrow = fall_v.shape[0]
    core = lax.axis_index("tp")
    partner = {"tp": 1 - core}
    links.greet([partner], range(1, count))
    sums = links.summing(send_v, recv_v, sum_send, sum_recv)
    lates = links.summing(send_w, recv_w, late_send, late_recv)
    pieces = piece_copies(
        count,
        lambda i: hidden_ref.at[pl.ds(pl.multiple_of(i * thin, thin), thin)],
        block_v,
        piece_send,
        piece_recv,
    )
    here = lax.axis_index("ctx")
    pieces.append(
        pltpu.make_async_copy(
            hidden_ref.at[pl.ds(pl.multiple_of(here * thin, thin), thin)],
            block_v.at[here],
            load_sem.at[10],
        )
    )
    right = pl.ds(narrow, narrow)
    left = pl.ds(0, narrow)

    def both_cores(n, source, target_ref, rows, columns):
        target = target_ref.at[core, rows, columns]
        return [
            pltpu.make_async_copy(source, target, load_sem.at[11 + n]),
            pltpu.make_async_remote_copy(
                src_ref=source,
                dst_ref=target,
                send_sem=pair_send.at[n],
                recv_sem=pair_recv.at[n],
                device_id=partner,
                device_id_type=MESH,
            ),
        ]

    lows = both_cores(0, high_v, out_ref, pl.ds(0, size), left)
    low = pltpu.make_async_copy(low_ref, high_v, load_sem.at[11])
    low.start()
    outs = []
    loads = [
        pltpu.make_async_copy(source, target, load_sem.at[n])
        for n, (source, target) in enumerate(
            (
                (weight_ref.at[:, :, pl.ds(0, wide)], weight_v),
                (fall_ref.at[right], fall_v),
            )
        )
    ]
    more = [
        pltpu.make_async_copy(source, target, load_sem.at[15 + n])
        for n, (source, target) in enumerate(
            ((residual_ref.at[:, right], residual_v), (tokens_ref.at[core], tokens_v))
        )
    ]
    for copy in loads:
        copy.start()
    order = list(range(count - 1, -1, -1))
    unit_loads = links.loads(grads_ref, grads_v.at[0], order[0], load_sem, 2)
    for copy in unit_loads + pieces + more:
        copy.start()
    low.wait()
    for copy in lows:
        copy.start()
    bias_ref[...] = jnp.zeros_like(bias_ref)
    vector_ref[...] = jnp.zeros_like(vector_ref)
    loads[0].wait()
    for n, i in enumerate(order):
        for copy in unit_loads:
            copy.wait()
        if n + 1 < count:
            unit_loads = links.loads(
                grads_ref, grads_v.at[(n + 1) % 2], order[n + 1], load_sem, 2 + 2 * ((n + 1) % 2)
            )
            for copy in unit_loads:
                copy.start()
        links.terms(
            i,
            lambda at, n=n: across(grads_v[n % 2, :, :wide], weight_v[0, at, :])
            + across(grads_v[n % 2, :, wide:], weight_v[1, at, :]),
            weight_v.shape[1],
            kept_v,
            send_v,
        )
        if i >= count // 2:
            for part in (0, 1):
                sums[(i, part)].start()
        chunk = min(64, half)

        def bias(step, _, n=n):
            rows = pl.ds(pl.multiple_of(step * chunk, chunk), chunk)
            value = grads_v[n % 2, rows, :].astype(F32)
            bias_ref[0:1, :] += jnp.sum(value, axis=0, keepdims=True)
            return 0

        lax.fori_loop(0, size // chunk, bias, 0)
    loads[1].wait()
    out_terms(
        links,
        hid_ref,
        hid_v,
        lambda rows, at: across(rows[...], fall_v[at, :]),
        narrow,
        kept_w,
        send_w,
        load_sem,
        6,
    )
    for copy in pieces:
        copy.wait()
    for c in range(count):
        rise_grad_ref[:, c * hidden : (c + 1) * hidden] = block_v[c, :, 0:hidden].astype(F32)
        fall_grad_ref[c] = block_v[c, :, hidden:].astype(F32).T
    links.combine(sums, kept_v, send_v, recv_v, count // 2 - 1, 1)
    backs = [
        pltpu.make_async_copy(
            back_ref.at[pl.ds(part * half, half)], kept_v.at[2 + part], load_sem.at[2 + part]
        )
        for part in (0, 1)
    ]
    for copy in backs:
        copy.start()
    for i in range(count - 1, count // 2 - 1, -1):
        for part in (0, 1):
            lates[(i, part)].start()
    for copy in more + backs:
        copy.wait()

    def last(part, at, to, first):
        normed, spread = normalize(tokens_v[to, :].astype(F32))
        grad = kept_v[2 + part, at, :] + norm_back(first * table_ref[0:1, :], normed, spread)
        tokens_v[to, :] = grad.astype(BF16)
        for n, value in enumerate((first * normed, first)):
            vector_ref[n : n + 1, :] += jnp.sum(value, axis=0, keepdims=True)

    def send_part(part):
        rows = pl.ds(part * half, half)
        copies = both_cores(
            1 + part, tokens_v.at[rows], input_ref, rows, pl.ds(0, 2 * narrow)
        )
        for copy in copies:
            copy.start()
        outs.extend(copies)

    links.combine(sums, kept_v, send_v, recv_v, 0, 0, last, send_part)

    def high(part, at, to, value):
        high_v[to, :] = (
            residual_v[to, :] + (value + table_ref[5:6, narrow : 2 * narrow])
        ).astype(BF16)

    for copy in lows:
        copy.wait()
    links.combine(lates, kept_w, send_w, recv_w, count // 2 - 1, 0, high)
    copies = both_cores(3, high_v, out_ref, pl.ds(0, size), right)
    for copy in copies:
        copy.start()
    for copy in outs + copies:
        copy.wait()
    for pair in links.pairs:
        sums[pair].wait_send()
        lates[pair].wait_send()


def first_back(
    grads, weight, hid, fall_weight, low, residual, back, tokens, table, hidden_rows, count
):
    length, columns = grads.shape
    width, hidden = fall_weight.shape
    rows = length // count
    links = Links(count, rows // 2)
    half, copies = links.half, len(links.pairs)
    narrow = width // 2
    thin, piece = hidden_rows.shape[0] // count, hidden_rows.shape[1] * 2 // 3
    anywhere = pl.BlockSpec(memory_space=pl.ANY)
    inside = pl.BlockSpec(memory_space=pltpu.VMEM)
    dma = pltpu.SemaphoreType.DMA
    return pl.pallas_call(
        functools.partial(first_back_kernel, links),
        out_shape=(
            jax.ShapeDtypeStruct((2, rows, width), BF16),
            jax.ShapeDtypeStruct((2, rows, width), BF16),
            jax.ShapeDtypeStruct((8, width), F32),
            jax.ShapeDtypeStruct((1, columns), F32),
            jax.ShapeDtypeStruct((count, piece // 2, thin), F32),
            jax.ShapeDtypeStruct((thin, count * piece), F32),
        ),
        in_specs=[anywhere] * 8 + [inside, anywhere],
        out_specs=(anywhere, anywhere, inside, inside, inside, inside),
        scratch_shapes=[
            pltpu.VMEM((2, rows, columns), BF16),
            pltpu.VMEM((2, width, columns // 2), BF16),
            pltpu.VMEM((2, rows, hidden), BF16),
            pltpu.VMEM((narrow, hidden), BF16),
            pltpu.VMEM((count, half, width), F32),
            pltpu.VMEM((copies, half, width), BF16),
            pltpu.VMEM((copies, half, width), BF16),
            pltpu.VMEM((count, half, narrow), F32),
            pltpu.VMEM((copies, half, narrow), BF16),
            pltpu.VMEM((copies, half, narrow), BF16),
            pltpu.VMEM((rows, narrow), F32),
            pltpu.VMEM((rows, width), BF16),
            pltpu.VMEM((rows, narrow), BF16),
            pltpu.VMEM((count, thin, piece * 3 // 2), BF16),
            dma((17,)),
            dma((4,)),
            dma((4,)),
            dma((count - 1,)),
            dma((count - 1,)),
            dma((copies,)),
            dma((copies,)),
            dma((copies,)),
            dma((copies,)),
        ],
        compiler_params=pltpu.CompilerParams(
            collective_id=5, has_side_effects=True, vmem_limit_bytes=63 * 1024 * 1024
        ),
        cost_estimate=pl.CostEstimate(
            flops=2 * length * width * (columns + hidden // 2),
            bytes_accessed=length * columns * 2 + length * hidden * 2 + width * (columns + hidden) * 2,
            transcendentals=0,
        ),
        name="first_back",
    )(grads, weight, hid, fall_weight, low, residual, back, tokens, table, hidden_rows)


def body(
    tokens,
    cotangent,
    attention_gain,
    attention_bias,
    feedforward_gain,
    feedforward_bias,
    query_weight,
    query_bias,
    key_weight,
    value_weight,
    value_bias,
    output_weight,
    output_bias,
    up_weight,
    up_bias,
    down_weight,
    down_bias,
):
    _, local_rows, model_width = tokens.shape
    ctx, dp = lax.axis_size("ctx"), lax.axis_size("dp")
    here, core = lax.axis_index("ctx"), lax.axis_index("tp")
    thin = query_weight.shape[0]
    heads = query_weight.shape[1] // (HEAD_DIM * ctx)
    hidden = up_weight.shape[1] // ctx
    packed = jnp.stack(
        [w.reshape(thin, ctx, heads, HEAD_DIM) for w in (query_weight, key_weight, value_weight)],
        axis=3,
    ).reshape(thin, ctx, heads * 3 * HEAD_DIM)
    head_pieces = jnp.concatenate(
        [
            packed.transpose(1, 0, 2),
            output_weight.reshape(ctx, heads * HEAD_DIM, thin).transpose(0, 2, 1),
        ],
        axis=2,
    )
    hidden_pieces = jnp.concatenate(
        [
            down_weight.reshape(ctx, hidden, thin).transpose(0, 2, 1),
            up_weight.reshape(thin, ctx, hidden).transpose(1, 0, 2),
        ],
        axis=2,
    )

    small = jnp.stack(
        [attention_gain, attention_bias, feedforward_gain, feedforward_bias, output_bias, down_bias]
    ).astype(F32)
    small = jnp.concatenate([small, jnp.zeros((2, thin), F32)])
    def own_columns(vector):
        return lax.dynamic_index_in_dim(vector.reshape(ctx, -1), here, 0, keepdims=False)

    query_shift = own_columns(query_bias).reshape(heads, HEAD_DIM)
    value_shift = own_columns(value_bias).reshape(heads, HEAD_DIM)
    qkv_shift = jnp.stack([query_shift, jnp.zeros_like(query_shift), value_shift], axis=1)
    shifts = jnp.concatenate([qkv_shift.reshape(-1), own_columns(up_bias)])
    other_shifts = swap(shifts, "tp", 1)
    wide = heads * 3 * HEAD_DIM
    qkv_shift = jnp.concatenate([shifts[:wide], other_shifts[:wide]]).astype(F32)
    rise_shift = jnp.concatenate([shifts[wide:], other_shifts[wide:]]).astype(F32)

    ones, head_weights, hidden_block, table = front(
        tokens, head_pieces, hidden_pieces, small, ctx, dp
    )
    head_weights = head_weights.reshape(model_width, -1)
    hidden_weights = lax.all_gather(
        hidden_block.reshape(ctx * thin, -1), "dp", axis=0, tiled=True
    )
    qkv, mixed, log_total, grads_in, residual, input_two, head_whole = attend(
        ones, head_weights, qkv_shift[None], cotangent, tokens, table, 2 * heads, ctx
    )
    _, hid, _, hidden_both, late, residual_grad, branch_grad, vectors, rise_bias, fall_weight = (
        feed_forward(input_two, grads_in, hidden_weights, rise_shift[None], residual, table, ctx)
    )
    hidden_rows = over_dp(hidden_both)

    _, qkv_grads, low_columns, head_both = attend_back(
        branch_grad,
        head_whole,
        qkv,
        mixed,
        log_total,
        hid,
        fall_weight,
        ones,
        residual,
        late,
        table,
        ctx,
    )
    head_both, hidden_rows = lax.optimization_barrier((head_both, hidden_rows))
    head_rows = over_dp(head_both)
    outputs, input_grads, firsts, qkv_bias, fall_first, rise_grad = first_back(
        qkv_grads,
        head_whole,
        hid,
        fall_weight,
        low_columns,
        residual,
        residual_grad,
        tokens,
        table,
        hidden_rows,
        ctx,
    )
    biases = jnp.concatenate(
        [rise_bias.reshape(2, 1, hidden), qkv_bias.reshape(2, 1, wide)], axis=2
    )
    query_grad, key_grad, value_grad, out_grad, fall_second, features, totals = end(
        head_rows, vectors, firsts, biases, heads, ctx, dp
    )
    fall_grad = jnp.concatenate([fall_first, fall_second], axis=1).reshape(-1, thin)
    totals = totals[:, 0]
    qkv_bias = totals[:, hidden:].reshape(ctx * heads, 3, HEAD_DIM)
    return (
        outputs,
        input_grads,
        features[4],
        features[5],
        features[0],
        features[1],
        query_grad,
        qkv_bias[:, 0].reshape(-1),
        key_grad,
        value_grad,
        qkv_bias[:, 2].reshape(-1),
        out_grad,
        features[2],
        rise_grad,
        totals[:, :hidden].reshape(-1),
        fall_grad,
        features[3],
    )


def solution(mesh):
    placed = (
        P("dp", "ctx", None),
        P("dp", "ctx", None),
        P(("dp", "ctx")),
        P(("dp", "ctx")),
        P(("dp", "ctx")),
        P(("dp", "ctx")),
        P(("dp", "ctx"), "tp"),
        P("tp"),
        P(("dp", "ctx"), "tp"),
        P(("dp", "ctx"), "tp"),
        P("tp"),
        P("tp", ("dp", "ctx")),
        P(("dp", "ctx")),
        P(("dp", "ctx"), "tp"),
        P("tp"),
        P("tp", ("dp", "ctx")),
        P(("dp", "ctx")),
    )
    return jax.shard_map(
        body,
        mesh=mesh,
        in_specs=placed,
        out_specs=(
            P("dp", "ctx", None),
            P("dp", "ctx", None),
            P(("dp", "ctx")),
            P(("dp", "ctx")),
            P(("dp", "ctx")),
            P(("dp", "ctx")),
            P(("dp", "ctx"), "tp"),
            P("tp"),
            P(("dp", "ctx"), "tp"),
            P(("dp", "ctx"), "tp"),
            P("tp"),
            P("tp", ("dp", "ctx")),
            P(("dp", "ctx")),
            P(("dp", "ctx"), "tp"),
            P("tp"),
            P("tp", ("dp", "ctx")),
            P(("dp", "ctx")),
        ),
        check_vma=False,
    )
```
